32 devices in a mesh: dp: 8 (over y, x, core), tensor: 4 (over z).
Axes of the slice: x: 2, y: 2, z: 4, core: 2. Of those that a mesh axis runs over, the one named last changes fastest.
Arguments:
- tokens: bfloat16 [20736, 1280], P(('dp', 'tensor')), may hold values from -14 to 14
- counts: int32 [8, 4], P('dp'), may hold values from 1 to 648, 2056 in all within a row
- gains: float32 [2, 1280], P(None, ('dp', 'tensor')), may hold values from 0.1 to 1.9
- biases: float32 [6, 1280], P(None, ('dp', 'tensor')), may hold values from -3 to 3
- fc1_bias: float32 [5120], P(('dp', 'tensor')), may hold values from -3 to 3
- w_qkv: bfloat16 [1280, 3, 1280], P('dp', None, 'tensor'), may hold values from -0.1677051 to 0.1677051
- w_o: bfloat16 [1280, 1280], P('tensor', 'dp'), may hold values from -1.25 to 1.25
- w_1: bfloat16 [1280, 5120], P('dp', 'tensor'), may hold values from -0.15625 to 0.15625
- w_2: bfloat16 [5120, 1280], P('tensor', 'dp'), may hold values from -0.078125 to 0.078125
- cotangent: bfloat16 [20736, 1280], P(('dp', 'tensor')), may hold values from -6 to 6
Outputs:
- mixed: bfloat16 [20736, 1280], P(('dp', 'tensor'))
- d_tokens: bfloat16 [20736, 1280], P(('dp', 'tensor'))
- d_w_qkv: float32 [1280, 3, 1280], P('dp', None, 'tensor')
- d_w_o: float32 [1280, 1280], P('tensor', 'dp')
- d_w_1: float32 [1280, 5120], P('dp', 'tensor')
- d_w_2: float32 [5120, 1280], P('tensor', 'dp')
- d_gains: float32 [2, 1280], P(None, ('dp', 'tensor'))
- d_biases: float32 [6, 1280], P(None, ('dp', 'tensor'))
- d_fc1_bias: float32 [5120], P(('dp', 'tensor'))
The draws below stay inside these ranges and needn't reach their ends.
Inputs may be any that keep to these rules, and one draw needn't show every extreme that they name: Each row of counts sums to 2056, and each row has a block with exactly 648 valid rows.
All inputs are finite; a program needn't handle non-finite values.
Results may differ from the reference program's by a relative error of at most 0.015.
The reference program's roundings to bfloat16 on the way (of `attn_in`, `probs`, `attended`, `mlp_in`, `act` and `grad_att`) count: a program that leaves them out, or rounds other values in their place, can miss the bound.
Values may be sent and summed in bfloat16 or wider, within the bound.
A program may use at most 192 MiB of HBM per device.

```python
import math
import jax
import jax.numpy as jnp
import numpy as np
from jax import lax

D = 1280
HEADS = 16
HD = 80
FF = 5120
TOK_IMG = 257
IMG_DEV = 8
ROWS_BLK = 648
ROWS = 20736
N_DP = 8
N_TENSOR = 4


def draw_tokens(key, part):
    base_key = jax.random.fold_in(key, 11)
    rows = jnp.clip(jax.random.normal(base_key, (ROWS, D), jnp.float32), -6.0, 6.0)
    return rows.astype(jnp.bfloat16)


def draw_w_qkv(key, part):
    width = HEADS * HD
    base_key = jax.random.fold_in(key, 22)
    base = jnp.clip(jax.random.normal(base_key, (D, 3, width), jnp.float32), -6.0, 6.0) * D ** (-0.5)
    return base.astype(jnp.bfloat16)


def block_scale(key, dims, shards, least, largest):
    def one(dim, blocks):
        draws = jax.random.uniform(jax.random.fold_in(jax.random.fold_in(key, 6), dim), (blocks,), jnp.float32, least / len(shards), largest / len(shards))
        return jnp.repeat(jnp.exp(draws), dims[dim] // blocks).reshape((-1,) + (1,) * (len(dims) - dim - 1))

    factor_of = one(*shards[0])
    for cut in shards[1:]:
        factor_of = factor_of * one(*cut)
    return factor_of


def profile(count, total, bound, skew):
    loads = [(1 << 20) // math.isqrt(grade ** skew) + 1 for grade in range(2, count + 1)]
    surplus, given = total - bound - (count - 1), [1] * (count - 1)
    while surplus > 0:
        candidates = [i for i in range(count - 1) if given[i] < bound]
        pool, remaining = sum([loads[i] for i in candidates]), surplus
        for i in candidates:
            more = min(bound - given[i], max(1, remaining * loads[i] // pool), surplus)
            given[i] = given[i] + more
            surplus = surplus - more
    return np.array([bound] + given)


def ragged(stream_key, number_of, total, most, lean):
    if number_of == 2:
        one = jax.random.randint(stream_key, (), max(1, total - most), min(most, total - 1) + 1)
        return jnp.stack([one, total - one])
    lengths = jnp.asarray(profile(number_of, total, most, lean), jnp.int32)
    pairs = (number_of - 1) // 2
    source_of, sink = lengths[1:1 + 2 * pairs:2], lengths[2:2 + 2 * pairs:2]
    slack = jnp.minimum(source_of - 1, most - sink)
    shifted = jax.random.randint(jax.random.fold_in(stream_key, 1), (pairs,), 0, 1 << 20) % (slack + 1)
    lengths = lengths.at[1:1 + 2 * pairs:2].set(source_of - shifted).at[2:2 + 2 * pairs:2].set(sink + shifted)
    return lengths[jax.random.permutation(jax.random.fold_in(stream_key, 2), number_of)]


def bell_draw(key, extent, deviation, most, pieces=(), kind=jnp.bfloat16):
    values = jax.random.normal(key, extent, jnp.float32) * deviation
    if len(pieces) > 0:
        values = block_scale(key, extent, pieces, -0.22, 0.18) * values
    return jnp.clip(values, min=-most, max=most).astype(kind)


def setup_inputs(seed: int = 0) -> dict:
    arg_keys = jax.random.split(jax.random.key(seed), 11)
    return {
        "tokens": draw_tokens(jax.random.fold_in(arg_keys[10], 71), 0),
        "counts": jax.vmap(lambda own: ragged(own, N_TENSOR, IMG_DEV * TOK_IMG, ROWS_BLK, 1))(jax.random.split(arg_keys[1], N_DP)).reshape((N_DP, N_TENSOR)).astype(jnp.int32),
        "gains": jnp.clip(1.0 + 0.18 * jax.random.normal(arg_keys[2], (2, D), jnp.float32), 0.1, 1.9),
        "biases": bell_draw(arg_keys[3], (6, D), 0.5, 3.0, ((1, 32),), jnp.float32),
        "fc1_bias": bell_draw(arg_keys[4], (FF,), 0.5, 3.0, ((0, 32),), jnp.float32),
        "w_qkv": draw_w_qkv(jax.random.fold_in(arg_keys[10], 71), 0),
        "w_o": bell_draw(arg_keys[6], (HEADS * HD, D), (HEADS * HD * 4 // TOK_IMG) ** -0.5, 1.25, ((0, 4), (1, 8))),
        "w_1": bell_draw(arg_keys[7], (D, FF), D ** -0.5, 0.15625, ((0, 8), (1, 4))),
        "w_2": bell_draw(arg_keys[8], (FF, D), FF ** -0.5, 0.078125, ((0, 4), (1, 8))),
        "cotangent": bell_draw(arg_keys[9], (ROWS, D), 1.0, 6.0, ((0, 32),)),
    }


EPS = 1e-06

def norm_rows(values, gain, shift):
    mean = lax.optimization_barrier(jnp.mean(values, axis=-1, keepdims=True))
    centred = values - mean
    spread = lax.optimization_barrier(jnp.mean(centred * centred, axis=-1, keepdims=True))
    inverse = lax.rsqrt(spread + EPS)
    normed = centred * inverse
    return (normed * gain + shift, normed, inverse)

def norm_back(upstream, normed, inverse, gain):
    scaled = upstream * gain
    return inverse * (scaled - lax.optimization_barrier(jnp.mean(scaled, axis=-1, keepdims=True)) - normed * lax.optimization_barrier(jnp.mean(scaled * normed, axis=-1, keepdims=True)))

def gelu_slope(pre):
    return 0.5 * (1.0 + lax.erf(pre * (1.0 / math.sqrt(2.0)))) + pre * jnp.exp(-0.5 * pre * pre) * (1.0 / math.sqrt(2.0 * math.pi))

def block_layout(counts_row, block_rows, total):
    parts = counts_row.shape[0]
    ends = jnp.cumsum(counts_row).astype(jnp.int32)
    starts = (ends - counts_row).astype(jnp.int32)
    places = jnp.arange(total, dtype=jnp.int32)
    owners = lax.optimization_barrier(jnp.sum((places[:, None] >= ends[None, :]).astype(jnp.int32), axis=1)).astype(jnp.int32)
    picked = owners[:, None] == jnp.arange(parts, dtype=jnp.int32)[None, :]
    first = lax.optimization_barrier(jnp.sum(jnp.where(picked, starts[None, :], 0), axis=1)).astype(jnp.int32)
    return owners * block_rows + places - first

def padded_rows(counts_row, block_rows, total, row_start, row_count):
    parts = counts_row.shape[0]
    ends = jnp.cumsum(counts_row).astype(jnp.int32)
    starts = (ends - counts_row).astype(jnp.int32)
    rows = row_start + jnp.arange(row_count, dtype=jnp.int32)
    owners = rows // block_rows
    within = rows - owners * block_rows
    picked = owners[:, None] == jnp.arange(parts, dtype=jnp.int32)[None, :]
    limit = lax.optimization_barrier(jnp.sum(jnp.where(picked, counts_row[None, :], 0), axis=1)).astype(jnp.int32)
    first = lax.optimization_barrier(jnp.sum(jnp.where(picked, starts[None, :], 0), axis=1)).astype(jnp.int32)
    valid = within < limit
    places = jnp.clip(first + within, 0, total - 1).astype(jnp.int32)
    return (places, valid)

def attend_image(inputs):
    query, keys, values = inputs
    scale = HD ** (-0.5)
    scores = jnp.einsum('thd,shd->hts', query.astype(jnp.float32), keys.astype(jnp.float32)) * scale
    top = lax.optimization_barrier(jnp.max(scores, axis=-1, keepdims=True))
    expo = jnp.exp(scores - top)
    summed = lax.optimization_barrier(jnp.sum(expo, axis=-1, keepdims=True))
    probs = (expo / summed).astype(jnp.bfloat16)
    output = jnp.einsum('hts,shd->thd', probs.astype(jnp.float32), values.astype(jnp.float32)).astype(jnp.bfloat16)
    return (output, (top + jnp.log(summed))[..., 0])

def attend_back(inputs):
    query, keys, values, output, grad_out, lse = inputs
    scale = HD ** (-0.5)
    scores = jnp.einsum('thd,shd->hts', query.astype(jnp.float32), keys.astype(jnp.float32)) * scale
    probs = jnp.exp(scores - lse[..., None])
    probs_b = probs.astype(jnp.bfloat16)
    grad_v = jnp.einsum('hts,thd->shd', probs_b.astype(jnp.float32), grad_out.astype(jnp.float32))
    grad_p = jnp.einsum('thd,shd->hts', grad_out.astype(jnp.float32), values.astype(jnp.float32))
    delta = jnp.einsum('thd,thd->ht', grad_out.astype(jnp.float32), output.astype(jnp.float32))
    grad_s = (probs * (grad_p - delta[..., None]) * scale).astype(jnp.bfloat16)
    grad_q = jnp.einsum('hts,shd->thd', grad_s.astype(jnp.float32), keys.astype(jnp.float32))
    grad_k = jnp.einsum('hts,thd->shd', grad_s.astype(jnp.float32), query.astype(jnp.float32))
    return (grad_q, grad_k, grad_v)

def reference(tokens, counts, gains, biases, fc1_bias, w_qkv, w_o, w_1, w_2, cotangent):
    width = HEADS * HD
    group_rows = N_TENSOR * ROWS_BLK
    total = IMG_DEV * TOK_IMG
    qkv_flat = w_qkv.reshape(D, 3 * width)
    shaped = (IMG_DEV, TOK_IMG, HEADS, HD)

    def group(carry, index):
        start = index * group_rows
        rows_in = lax.dynamic_slice_in_dim(tokens, start, group_rows, 0)
        cot_in = lax.dynamic_slice_in_dim(cotangent, start, group_rows, 0)
        counts_row = lax.dynamic_index_in_dim(counts, index, 0, keepdims=False)
        source = block_layout(counts_row, ROWS_BLK, total)
        x = jnp.take(rows_in, source, axis=0).astype(jnp.float32)
        cot = jnp.take(cot_in, source, axis=0)
        attn_norm, normed1, inverse1 = norm_rows(x, gains[0], biases[0])
        attn_in = attn_norm.astype(jnp.bfloat16)
        qkv = jnp.dot(attn_in, qkv_flat, preferred_element_type=jnp.float32).reshape(total, 3, width)
        query = (qkv[:, 0] + biases[2]).astype(jnp.bfloat16).reshape(shaped)
        keys = qkv[:, 1].astype(jnp.bfloat16).reshape(shaped)
        values = (qkv[:, 2] + biases[3]).astype(jnp.bfloat16).reshape(shaped)
        attended, lse = lax.map(attend_image, (query, keys, values))
        attended_flat = attended.reshape(total, width)
        hidden = x + jnp.dot(attended_flat, w_o, preferred_element_type=jnp.float32) + biases[4]
        mlp_norm, normed2, inverse2 = norm_rows(hidden, gains[1], biases[1])
        mlp_in = mlp_norm.astype(jnp.bfloat16)
        pre = jnp.dot(mlp_in, w_1, preferred_element_type=jnp.float32) + fc1_bias
        act = jax.nn.gelu(pre, approximate=False).astype(jnp.bfloat16)
        mixed = (hidden + jnp.dot(act, w_2, preferred_element_type=jnp.float32) + biases[5]).astype(jnp.bfloat16)
        cot_f = cot.astype(jnp.float32)
        grad_w2 = jnp.dot(act.T, cot, preferred_element_type=jnp.float32)
        grad_pre = jnp.dot(cot, w_2.T, preferred_element_type=jnp.float32) * gelu_slope(pre)
        grad_pre_b = grad_pre.astype(jnp.bfloat16)
        grad_w1 = jnp.dot(mlp_in.T, grad_pre_b, preferred_element_type=jnp.float32)
        grad_mlp_in = jnp.dot(grad_pre_b, w_1.T, preferred_element_type=jnp.float32)
        grad_hidden = cot_f + norm_back(grad_mlp_in, normed2, inverse2, gains[1])
        grad_hidden_b = grad_hidden.astype(jnp.bfloat16)
        grad_wo = jnp.dot(attended_flat.T, grad_hidden_b, preferred_element_type=jnp.float32)
        grad_att = jnp.dot(grad_hidden_b, w_o.T, preferred_element_type=jnp.float32).astype(jnp.bfloat16)
        grad_q, grad_k, grad_v = lax.map(attend_back, (query, keys, values, attended, grad_att.reshape(shaped), lse))
        grad_q = grad_q.reshape(total, width)
        grad_k = grad_k.reshape(total, width)
        grad_v = grad_v.reshape(total, width)
        grad_qkv = jnp.stack([grad_q, grad_k, grad_v], axis=1).astype(jnp.bfloat16).reshape(total, 3 * width)
        grad_wqkv = jnp.dot(attn_in.T, grad_qkv, preferred_element_type=jnp.float32).reshape(D, 3, width)
        grad_attn_in = jnp.dot(grad_qkv, qkv_flat.T, preferred_element_type=jnp.float32)
        grad_x = grad_hidden + norm_back(grad_attn_in, normed1, inverse1, gains[0])
        gain_terms = jnp.stack([lax.optimization_barrier(jnp.sum(grad_attn_in * normed1, axis=0)), lax.optimization_barrier(jnp.sum(grad_mlp_in * normed2, axis=0))])
        bias_terms = jnp.stack([lax.optimization_barrier(jnp.sum(grad_attn_in, axis=0)), lax.optimization_barrier(jnp.sum(grad_mlp_in, axis=0)), lax.optimization_barrier(jnp.sum(grad_q, axis=0)), lax.optimization_barrier(jnp.sum(grad_v, axis=0)), lax.optimization_barrier(jnp.sum(grad_hidden, axis=0)), lax.optimization_barrier(jnp.sum(cot_f, axis=0))])
        fc1_terms = lax.optimization_barrier(jnp.sum(grad_pre, axis=0))
        places, valid = padded_rows(counts_row, ROWS_BLK, total, 0, group_rows)
        mixed_rows = jnp.where(valid[:, None], jnp.take(mixed, places, axis=0), jnp.zeros((), jnp.bfloat16))
        grad_rows = jnp.where(valid[:, None], jnp.take(grad_x.astype(jnp.bfloat16), places, axis=0), jnp.zeros((), jnp.bfloat16))
        terms = (grad_wqkv, grad_wo, grad_w1, grad_w2, gain_terms, bias_terms, fc1_terms)
        carry = tuple((older + newer for older, newer in zip(carry, terms)))
        return (carry, (mixed_rows, grad_rows))
    start_sums = (jnp.zeros((D, 3, width), jnp.float32), jnp.zeros((width, D), jnp.float32), jnp.zeros((D, FF), jnp.float32), jnp.zeros((FF, D), jnp.float32), jnp.zeros((2, D), jnp.float32), jnp.zeros((6, D), jnp.float32), jnp.zeros((FF,), jnp.float32))
    sums, outputs = lax.scan(group, start_sums, jnp.arange(N_DP, dtype=jnp.int32))
    mixed_all = outputs[0].reshape(N_DP * group_rows, D)
    grad_all = outputs[1].reshape(N_DP * group_rows, D)
    return (mixed_all, grad_all, sums[0], sums[1], sums[2], sums[3], sums[4], sums[5], sums[6])
```

```python
import functools
import math

import jax
import jax.numpy as jnp
from jax import lax
from jax.experimental import pallas as pl
from jax.experimental.pallas import tpu as pltpu
from jax.sharding import PartitionSpec as P

D = 1280
HD = 80
HEADS = 16
FF = 5120
TOK_IMG = 257
IMG_DEV = 8
TOTAL = IMG_DEV * TOK_IMG
EPS = 1e-06
PT = 272
F32 = jnp.float32
BF16 = jnp.bfloat16
NEG = -1e30
VMEM_LIMIT = 56 * 1024 * 1024


class Cfg:
    def __init__(self, n_dp, n_t, block_rows):
        self.n_dp, self.n_t, self.block = n_dp, n_t, block_rows
        self.n_p = n_dp // 2
        self.imgs = IMG_DEV // n_t
        self.ni = 2 * self.imgs
        self.rows = self.imgs * TOK_IMG
        self.m = self.ni * PT
        self.pd = D // n_dp
        self.hh = HEADS // n_t // 2
        self.hc = self.hh * HD
        self.f2 = FF // n_t // 2
        assert 4 * self.hc == self.f2
        self.caps = self._caps()

    def _caps(self):
        n, b, r = self.n_t, self.block, self.rows
        low = [max(t, TOTAL - (n - t) * b) for t in range(n + 1)]
        high = [min(t * b, TOTAL - (n - t)) for t in range(n + 1)]
        caps = {}
        for t in range(n):
            for dest in range(n):
                size = min(high[t + 1], r * (dest + 1)) - max(low[t], r * dest)
                size = min(size, b, r)
                if size > 0 and dest != t:
                    caps[dest - t] = max(caps.get(dest - t, 0), size)
        return {s: min(-(-c // 16) * 16, b, r) for s, c in sorted(caps.items())}


def dot(a, b):
    return lax.dot_general(a, b, (((1,), (0,)), ((), ())), preferred_element_type=F32)


def dot_nt(a, b):
    return lax.dot_general(a, b, (((1,), (1,)), ((), ())), preferred_element_type=F32)


def dot_tn(a, b):
    return lax.dot_general(a, b, (((0,), (0,)), ((), ())), preferred_element_type=F32)


def norm(values):
    mean = jnp.mean(values, axis=-1, keepdims=True)
    centred = values - mean
    spread = jnp.mean(centred * centred, axis=-1, keepdims=True)
    inverse = lax.rsqrt(spread + EPS)
    return centred * inverse, inverse


def norm_back(upstream, normed, inverse, gain):
    scaled = upstream * gain
    return inverse * (
        scaled
        - jnp.mean(scaled, axis=-1, keepdims=True)
        - normed * jnp.mean(scaled * normed, axis=-1, keepdims=True)
    )


def swap_dp(value, bit, cfg):
    return lax.ppermute(value, "dp", [(i, i ^ bit) for i in range(cfg.n_dp)])


def turn_tensor(value, shift, cfg):
    return lax.ppermute(value, "tensor", [(i, (i + shift) % cfg.n_t) for i in range(cfg.n_t)])


def step_tensor(value, shift, cfg):
    pairs = [(i, i + shift) for i in range(cfg.n_t) if 0 <= i + shift < cfg.n_t]
    return lax.ppermute(value, "tensor", pairs)


def gather_pair(a, b, cfg):
    both = jnp.stack([a, b])
    if cfg.n_p == 4:
        from_x = swap_dp(both, 2, cfg)
        from_y = swap_dp(both, 4, cfg)
        diag_a = swap_dp(from_x[0], 4, cfg)
        diag_b = swap_dp(from_y[1], 2, cfg)
        arrays = [both, from_x, from_y, diag_a[None], diag_b[None]]
        where_a = [(0, 0), (1, 0), (2, 0), (3, 0)]
        where_b = [(0, 1), (1, 1), (2, 1), (4, 0)]
        return arrays, where_a, where_b
    arrays = [both] + [swap_dp(both, 2 * m, cfg) for m in range(1, cfg.n_p)]
    return arrays, [(m, 0) for m in range(cfg.n_p)], [(m, 1) for m in range(cfg.n_p)]


def slot_order(cfg):
    if cfg.n_p == 4:
        return [1, 3, 0, 2], [2, 3, 0, 1]
    order = list(range(1, cfg.n_p)) + [0]
    return order, order


def scatter_pair(send_a, keep_a, send_b, keep_b, cfg):
    if cfg.n_p == 4:
        got_a = swap_dp(send_a, 2, cfg)
        got_b = swap_dp(send_b, 4, cfg)
        next_a = (keep_a[1].astype(F32) + got_a[1].astype(F32)).astype(BF16)
        next_b = (keep_b[1].astype(F32) + got_b[1].astype(F32)).astype(BF16)
        last_a = swap_dp(next_a, 4, cfg)
        last_b = swap_dp(next_b, 2, cfg)
        sum_a = keep_a[0].astype(F32) + got_a[0].astype(F32) + last_a.astype(F32)
        sum_b = keep_b[0].astype(F32) + got_b[0].astype(F32) + last_b.astype(F32)
        return sum_a, sum_b
    sum_a, sum_b = keep_a[0].astype(F32), keep_b[0].astype(F32)
    for m in range(1, cfg.n_p):
        got = swap_dp(jnp.stack([send_a[m - 1], send_b[m - 1]]), 2 * m, cfg)
        sum_a = sum_a + got[0].astype(F32)
        sum_b = sum_b + got[1].astype(F32)
    return sum_a, sum_b


def gather_small(value, cfg, me, z):
    value = value[None]
    bit = 1
    while bit < cfg.n_t:
        other = lax.ppermute(value, "tensor", [(i, i ^ bit) for i in range(cfg.n_t)])
        first = (z & bit) == 0
        value = jnp.concatenate([jnp.where(first, value, other), jnp.where(first, other, value)])
        bit *= 2
    value = value[None]
    bit = 1
    while bit < cfg.n_dp:
        other = swap_dp(value, bit, cfg)
        first = (me & bit) == 0
        value = jnp.concatenate([jnp.where(first, value, other), jnp.where(first, other, value)])
        bit *= 2
    return value


def scatter_small(value, cfg, me, z):
    bit = cfg.n_dp // 2
    while bit >= 1:
        half = value.shape[0] // 2
        first = (me & bit) == 0
        keep = jnp.where(first, value[:half], value[half:])
        send = jnp.where(first, value[half:], value[:half])
        value = keep + swap_dp(send, bit, cfg)
        bit //= 2
    value = value[0]
    bit = cfg.n_t // 2
    while bit >= 1:
        half = value.shape[0] // 2
        first = (z & bit) == 0
        keep = jnp.where(first, value[:half], value[half:])
        send = jnp.where(first, value[half:], value[:half])
        value = keep + lax.ppermute(send, "tensor", [(i, i ^ bit) for i in range(cfg.n_t)])
        bit //= 2
    return value[0]


def pick(positions, limit):
    return (positions[:, None] == jnp.arange(limit, dtype=jnp.int32)[None, :]).astype(BF16)


def window_start(starts, t, dest, size, cfg):
    return jnp.clip(cfg.rows * dest - starts[t], 0, cfg.block - size)


def to_images(block, starts, ends, z, cfg):
    slot = jnp.arange(cfg.imgs * PT, dtype=jnp.int32)
    within = slot % PT
    place = cfg.rows * z + (slot // PT) * TOK_IMG + within
    valid = within < TOK_IMG
    owner = jnp.sum((place[:, None] >= ends[None, :]).astype(jnp.int32), axis=1)
    padded = jnp.where(valid & (owner == z), place - starts[z], -1)
    total = dot(pick(padded, cfg.block), block)
    for shift, size in cfg.caps.items():
        dest = jnp.clip(z + shift, 0, cfg.n_t - 1)
        sent = lax.dynamic_slice_in_dim(block, window_start(starts, z, dest, size, cfg), size)
        got = step_tensor(sent, shift, cfg)
        source = jnp.clip(z - shift, 0, cfg.n_t - 1)
        offset = place - starts[source] - window_start(starts, source, z, size, cfg)
        offset = jnp.where(valid & (owner == z - shift), offset, -1)
        total = total + dot(pick(offset, size), got)
    return total.astype(BF16)


def to_blocks(images, starts, ends, z, cfg):
    row = jnp.arange(cfg.block, dtype=jnp.int32)
    place = starts[z] + row
    valid = place < ends[z]
    owner = place // cfg.rows
    local = place - cfg.rows * z
    slots = (local // TOK_IMG) * PT + local % TOK_IMG
    total = dot(pick(jnp.where(valid & (owner == z), slots, -1), cfg.imgs * PT), images)
    for shift, size in cfg.caps.items():
        block_to = jnp.clip(z - shift, 0, cfg.n_t - 1)
        begin = jnp.clip(starts[block_to] - cfg.rows * z, 0, cfg.rows - size)
        want = begin + jnp.arange(size, dtype=jnp.int32)
        want = (want // TOK_IMG) * PT + want % TOK_IMG
        sent = dot(pick(want, cfg.imgs * PT), images).astype(BF16)
        got = step_tensor(sent, -shift, cfg)
        source = jnp.clip(z + shift, 0, cfg.n_t - 1)
        begin_there = jnp.clip(starts[z] - cfg.rows * source, 0, cfg.rows - size)
        offset = place - cfg.rows * source - begin_there
        offset = jnp.where(valid & (owner == z + shift), offset, -1)
        total = total + dot(pick(offset, size), got)
    return total.astype(BF16)


def weight_copies(scalars, refs, wheres, scratch, sem, cfg):
    plane, core = scalars[0], scalars[1]
    copies = []
    for m, (array, index) in enumerate(wheres):
        for r in range(2):
            owner = 2 * (plane ^ m) + (core ^ r)
            rows = pl.ds(pl.multiple_of(owner * cfg.pd, 16), cfg.pd)
            copies.append(
                pltpu.make_async_copy(refs[array].at[index, r], scratch.at[rows, :], sem)
            )
    return copies


def any_spec():
    return pl.BlockSpec(memory_space=pl.ANY)


def params(**more):
    return pltpu.CompilerParams(vmem_limit_bytes=VMEM_LIMIT, **more)


def image_spec(width):
    return pl.BlockSpec((1, PT, width), lambda i, s: (i, 0, 0))


def row_spec(count=1, width=D):
    return pl.BlockSpec((count, width), lambda i, s: (0, 0))


def attention_forward(scalars, x, gain, shift, query_bias, value_bias, weights, cfg):
    flat, plan = [], []
    for arrays, wheres in weights:
        ids = []
        for a in arrays:
            found = [i for i, f in enumerate(flat) if f is a]
            if not found:
                flat.append(a)
                found = [len(flat) - 1]
            ids.append(found[0])
        plan.append([(ids[a], i) for a, i in wheres])
    n_t, hc, hh = cfg.n_t, cfg.hc, cfg.hh

    def kernel(s, x_ref, gain_ref, shift_ref, qb_ref, vb_ref, *rest):
        w_refs = rest[: len(flat)]
        in_ref, qkv_ref, att_ref, lse_ref, out_ref, w, sem = rest[len(flat) :]

        @pl.when(pl.program_id(0) == 0)
        def _():
            copies = []
            for k in range(n_t):
                copies += weight_copies(s, w_refs, plan[k], w.at[k], sem, cfg)
            for copy in copies:
                copy.start()
            for copy in copies:
                copy.wait()

        normed, _ = norm(x_ref[0].astype(F32))
        attn_in = (normed * gain_ref[...] + shift_ref[...]).astype(BF16)
        in_ref[0] = attn_in
        keyed = lax.broadcasted_iota(jnp.int32, (PT, PT), 1) < TOK_IMG
        out = jnp.zeros((PT, D), F32)
        for k in range(n_t):
            block = 2 * lax.rem(s[2] - k + n_t, n_t) + s[1]
            qkv = dot(attn_in, w[k, :, : 3 * hc])
            query = (qkv[:, :hc] + qb_ref[pl.ds(block, 1), :]).astype(BF16)
            keys = qkv[:, hc : 2 * hc].astype(BF16)
            values = (qkv[:, 2 * hc :] + vb_ref[pl.ds(block, 1), :]).astype(BF16)
            qkv_ref[k, 0, :, :hc] = query
            qkv_ref[k, 0, :, hc : 2 * hc] = keys
            qkv_ref[k, 0, :, 2 * hc :] = values
            for h in range(hh):
                cols = slice(h * HD, (h + 1) * HD)
                scores = dot_nt(query[:, cols], keys[:, cols]) * (HD**-0.5)
                scores = jnp.where(keyed, scores, NEG)
                top = jnp.max(scores, axis=-1, keepdims=True)
                expo = jnp.exp(scores - top)
                summed = jnp.sum(expo, axis=-1, keepdims=True)
                probs = (expo / summed).astype(BF16)
                att_ref[k, 0, :, cols] = dot(probs, values[:, cols]).astype(BF16)
                j = k * hh + h
                lse_ref[0, :, j : j + 1] = top + jnp.log(summed)
            out = out + dot_nt(att_ref[k, 0], w[k, :, 3 * hc :])
        out_ref[0] = out

    return pl.pallas_call(
        kernel,
        grid_spec=pltpu.PrefetchScalarGridSpec(
            num_scalar_prefetch=1,
            grid=(cfg.ni,),
            in_specs=[
                image_spec(D),
                row_spec(),
                row_spec(),
                row_spec(2 * n_t, hc),
                row_spec(2 * n_t, hc),
            ]
            + [any_spec()] * len(flat),
            out_specs=[
                image_spec(D),
                pl.BlockSpec((n_t, 1, PT, 3 * hc), lambda i, s: (0, i, 0, 0)),
                pl.BlockSpec((n_t, 1, PT, hc), lambda i, s: (0, i, 0, 0)),
                image_spec(n_t * hh),
                image_spec(D),
            ],
            scratch_shapes=[
                pltpu.VMEM((n_t, D, cfg.f2), BF16),
                pltpu.SemaphoreType.DMA,
            ],
        ),
        out_shape=[
            jax.ShapeDtypeStruct((cfg.ni, PT, D), BF16),
            jax.ShapeDtypeStruct((n_t, cfg.ni, PT, 3 * hc), BF16),
            jax.ShapeDtypeStruct((n_t, cfg.ni, PT, hc), BF16),
            jax.ShapeDtypeStruct((cfg.ni, PT, n_t * hh), F32),
            jax.ShapeDtypeStruct((cfg.ni, PT, D), F32),
        ],
        compiler_params=params(),
        cost_estimate=pl.CostEstimate(
            flops=2 * cfg.m * D * cfg.f2 * n_t,
            bytes_accessed=2 * n_t * D * cfg.f2 + 12 * cfg.m * D,
            transcendentals=cfg.m * PT * n_t * hh,
        ),
        name="attention_forward",
    )(scalars, x, gain, shift, query_bias, value_bias, *flat)


def attention_backward(scalars, grad_hidden, qkv, attended, lse, weights, cfg):
    flat, plan = [], []
    for arrays, wheres in weights:
        ids = []
        for a in arrays:
            found = [i for i, f in enumerate(flat) if f is a]
            if not found:
                flat.append(a)
                found = [len(flat) - 1]
            ids.append(found[0])
        plan.append([(ids[a], i) for a, i in wheres])
    n_t, hc, hh = cfg.n_t, cfg.hc, cfg.hh
    scale = HD**-0.5

    def kernel(s, gh_ref, qkv_ref, att_ref, lse_ref, *rest):
        w_refs = rest[: len(flat)]
        gqkv_ref, out_ref, dq_ref, dv_ref, w, sem = rest[len(flat) :]

        @pl.when(pl.program_id(0) == 0)
        def _():
            copies = []
            for k in range(n_t):
                copies += weight_copies(s, w_refs, plan[k], w.at[k], sem, cfg)
            for copy in copies:
                copy.start()
            for copy in copies:
                copy.wait()
            dq_ref[...] = jnp.zeros_like(dq_ref)
            dv_ref[...] = jnp.zeros_like(dv_ref)

        keyed = lax.broadcasted_iota(jnp.int32, (PT, PT), 1) < TOK_IMG
        grad_hidden_b = gh_ref[0]
        out = jnp.zeros((PT, D), F32)
        for k in range(n_t):
            grad_att = dot(grad_hidden_b, w[k, :, 3 * hc :]).astype(BF16)
            for h in range(hh):
                cols = slice(h * HD, (h + 1) * HD)
                key_cols = slice(hc + h * HD, hc + (h + 1) * HD)
                value_cols = slice(2 * hc + h * HD, 2 * hc + (h + 1) * HD)
                query = qkv_ref[k, 0, :, cols]
                keys = qkv_ref[k, 0, :, key_cols]
                values = qkv_ref[k, 0, :, value_cols]
                grad = grad_att[:, cols]
                j = k * hh + h
                scores = dot_nt(query, keys) * scale - lse_ref[0, :, j : j + 1]
                probs = jnp.exp(jnp.where(keyed, scores, NEG))
                delta = jnp.sum(
                    grad.astype(F32) * att_ref[k, 0, :, cols].astype(F32), axis=-1, keepdims=True
                )
                grad_v = dot_tn(probs.astype(BF16), grad)
                grad_s = (probs * (dot_nt(grad, values) - delta) * scale).astype(BF16)
                grad_q = dot(grad_s, keys)
                grad_k = dot_tn(grad_s, query)
                dq_ref[k : k + 1, cols] += jnp.sum(grad_q, axis=0, keepdims=True)
                dv_ref[k : k + 1, cols] += jnp.sum(grad_v, axis=0, keepdims=True)
                gqkv_ref[k, 0, :, cols] = grad_q.astype(BF16)
                gqkv_ref[k, 0, :, key_cols] = grad_k.astype(BF16)
                gqkv_ref[k, 0, :, value_cols] = grad_v.astype(BF16)
            out = out + dot_nt(gqkv_ref[k, 0], w[k, :, : 3 * hc])
        out_ref[0] = out

    return pl.pallas_call(
        kernel,
        grid_spec=pltpu.PrefetchScalarGridSpec(
            num_scalar_prefetch=1,
            grid=(cfg.ni,),
            in_specs=[
                image_spec(D),
                pl.BlockSpec((n_t, 1, PT, 3 * hc), lambda i, s: (0, i, 0, 0)),
                pl.BlockSpec((n_t, 1, PT, hc), lambda i, s: (0, i, 0, 0)),
                image_spec(n_t * hh),
            ]
            + [any_spec()] * len(flat),
            out_specs=[
                pl.BlockSpec((n_t, 1, PT, 3 * hc), lambda i, s: (0, i, 0, 0)),
                image_spec(D),
                row_spec(n_t, hc),
                row_spec(n_t, hc),
            ],
            scratch_shapes=[
                pltpu.VMEM((n_t, D, cfg.f2), BF16),
                pltpu.SemaphoreType.DMA,
            ],
        ),
        out_shape=[
            jax.ShapeDtypeStruct((n_t, cfg.ni, PT, 3 * hc), BF16),
            jax.ShapeDtypeStruct((cfg.ni, PT, D), F32),
            jax.ShapeDtypeStruct((n_t, hc), F32),
            jax.ShapeDtypeStruct((n_t, hc), F32),
        ],
        compiler_params=params(),
        cost_estimate=pl.CostEstimate(
            flops=2 * cfg.m * D * cfg.f2 * n_t + 10 * cfg.m * PT * HD * n_t * hh,
            bytes_accessed=2 * n_t * D * cfg.f2 + 12 * cfg.m * D,
            transcendentals=cfg.m * PT * n_t * hh,
        ),
        name="attention_backward",
    )(scalars, grad_hidden, qkv, attended, lse, *flat)


def attention_weights(scalars, attn_in_t, grad_t, gqkv, attended, k, cfg):
    hc, pd = cfg.hc, cfg.pd
    order_a, order_b = slot_order(cfg)
    send = 2 if cfg.n_p == 4 else cfg.n_p - 1
    keep = cfg.n_p - send

    def kernel(s, in_ref, gt_ref, gqkv_ref, att_ref, sa_ref, ka_ref, sb_ref, kb_ref):
        step = pl.program_id(0)

        def one(order, chunk, send_ref, keep_ref):
            slot = functools.reduce(
                lambda acc, i: jnp.where(step == i, order[i], acc), range(cfg.n_p), 0
            )
            rows = pl.ds(pl.multiple_of((slot ^ s[0]) * 2 * pd, 16), 2 * pd)
            left = dot(in_ref[rows, :], gqkv_ref[chunk]).astype(BF16)
            right = dot(gt_ref[rows, :], att_ref[chunk]).astype(BF16)

            def put(ref):
                for r in range(2):
                    ref[0, s[1] ^ r, :, : 3 * hc] = left[r * pd : (r + 1) * pd]
                    ref[0, s[1] ^ r, :, 3 * hc :] = right[r * pd : (r + 1) * pd]

            @pl.when(step < send)
            def _():
                put(send_ref)

            @pl.when(step >= send)
            def _():
                put(keep_ref)

        one(order_a, 0, sa_ref, ka_ref)
        one(order_b, 1, sb_ref, kb_ref)

    send_spec = pl.BlockSpec(
        (1, 2, pd, cfg.f2), lambda i, s: (jnp.minimum(i, send - 1), 0, 0, 0)
    )
    keep_spec = pl.BlockSpec((1, 2, pd, cfg.f2), lambda i, s: (jnp.maximum(i - send, 0), 0, 0, 0))
    send_shape = jax.ShapeDtypeStruct((send, 2, pd, cfg.f2), BF16)
    keep_shape = jax.ShapeDtypeStruct((keep, 2, pd, cfg.f2), BF16)
    return pl.pallas_call(
        kernel,
        grid_spec=pltpu.PrefetchScalarGridSpec(
            num_scalar_prefetch=1,
            grid=(cfg.n_p,),
            in_specs=[
                row_spec(D, cfg.m),
                row_spec(D, cfg.m),
                pl.BlockSpec((2, cfg.m, 3 * hc), lambda i, s: (k // 2, 0, 0)),
                pl.BlockSpec((2, cfg.m, hc), lambda i, s: (k // 2, 0, 0)),
            ],
            out_specs=[send_spec, keep_spec, send_spec, keep_spec],
        ),
        out_shape=[send_shape, keep_shape, send_shape, keep_shape],
        compiler_params=params(),
        cost_estimate=pl.CostEstimate(
            flops=4 * cfg.m * D * cfg.f2,
            bytes_accessed=4 * cfg.m * D + 4 * D * cfg.f2,
            transcendentals=0,
        ),
        name="attention_weights",
    )(
        scalars,
        attn_in_t,
        grad_t,
        gqkv.reshape(cfg.n_t, cfg.m, 3 * hc),
        attended.reshape(cfg.n_t, cfg.m, hc),
    )


def mlp_chunk(scalars, mlp_in, cot, mlp_in_t, cot_t, fc1, weights, k, cfg):
    arrays, where_1, where_2 = weights
    n = len(arrays)
    pd, f2, ni = cfg.pd, cfg.f2, cfg.ni
    order_a, order_b = slot_order(cfg)
    send = 2 if cfg.n_p == 4 else cfg.n_p - 1
    keep = cfg.n_p - send

    def kernel(s, in_ref, cot_ref, in_t_ref, cot_t_ref, fc1_ref, *rest):
        w_refs = rest[:n]
        act_ref, gpre_ref, sum_ref, sa_ref, ka_ref, sb_ref, kb_ref, w1, w2, act_all, gpre_all, sem = (
            rest[n:]
        )
        step = pl.program_id(0)

        @pl.when(step == 0)
        def _():
            copies = weight_copies(s, w_refs, where_1, w1, sem, cfg)
            copies += weight_copies(s, w_refs, where_2, w2, sem, cfg)
            for copy in copies:
                copy.start()
            for copy in copies:
                copy.wait()
            sum_ref[...] = jnp.zeros_like(sum_ref)

        @pl.when(step < ni)
        def _():
            block = 2 * lax.rem(s[2] - k + cfg.n_t, cfg.n_t) + s[1]
            pre = dot(in_ref[0], w1[...]) + fc1_ref[pl.ds(block, 1), :]
            phi = 0.5 * (1.0 + lax.erf(pre * (1.0 / math.sqrt(2.0))))
            act = (pre * phi).astype(BF16)
            slope = phi + pre * jnp.exp(-0.5 * pre * pre) * (1.0 / math.sqrt(2.0 * math.pi))
            gpre = dot(cot_ref[0], w2[...]) * slope
            sum_ref[...] += jnp.sum(gpre, axis=0, keepdims=True)
            gpre = gpre.astype(BF16)
            act_ref[0] = act
            gpre_ref[0] = gpre
            rows = pl.ds(pl.multiple_of(step * PT, 16), PT)
            act_all[rows, :] = act
            gpre_all[rows, :] = gpre

        def one(lhs_ref, rhs, send_ref, keep_ref):
            value = dot(lhs_ref[...], rhs[...]).astype(BF16)

            def put(ref):
                for r in range(2):
                    ref[0, s[1] ^ r] = value[r * pd : (r + 1) * pd]

            @pl.when(step < ni + send)
            def _():
                put(send_ref)

            @pl.when(step >= ni + send)
            def _():
                put(keep_ref)

        @pl.when(step >= ni)
        def _():
            one(in_t_ref, gpre_all, sa_ref, ka_ref)
            one(cot_t_ref, act_all, sb_ref, kb_ref)

    def tile_spec(order):
        def place(i, s):
            slot = functools.reduce(
                lambda acc, j: jnp.where(i == ni + j, order[j], acc), range(1, cfg.n_p), order[0]
            )
            return slot ^ s[0], 0

        return pl.BlockSpec((2 * pd, cfg.m), place)

    rows_in = pl.BlockSpec((1, PT, D), lambda i, s: (jnp.minimum(i, ni - 1), 0, 0))
    rows_out = pl.BlockSpec((1, PT, f2), lambda i, s: (jnp.minimum(i, ni - 1), 0, 0))
    send_spec = pl.BlockSpec(
        (1, 2, pd, f2), lambda i, s: (jnp.clip(i - ni, 0, send - 1), 0, 0, 0)
    )
    keep_spec = pl.BlockSpec((1, 2, pd, f2), lambda i, s: (jnp.maximum(i - ni - send, 0), 0, 0, 0))
    send_shape = jax.ShapeDtypeStruct((send, 2, pd, f2), BF16)
    keep_shape = jax.ShapeDtypeStruct((keep, 2, pd, f2), BF16)
    return pl.pallas_call(
        kernel,
        grid_spec=pltpu.PrefetchScalarGridSpec(
            num_scalar_prefetch=1,
            grid=(ni + cfg.n_p,),
            in_specs=[
                rows_in,
                rows_in,
                tile_spec(order_a),
                tile_spec(order_b),
                row_spec(2 * cfg.n_t, f2),
            ]
            + [any_spec()] * n,
            out_specs=[
                rows_out,
                rows_out,
                row_spec(1, f2),
                send_spec,
                keep_spec,
                send_spec,
                keep_spec,
            ],
            scratch_shapes=[
                pltpu.VMEM((D, f2), BF16),
                pltpu.VMEM((D, f2), BF16),
                pltpu.VMEM((cfg.m, f2), BF16),
                pltpu.VMEM((cfg.m, f2), BF16),
                pltpu.SemaphoreType.DMA,
            ],
        ),
        out_shape=[
            jax.ShapeDtypeStruct((ni, PT, f2), BF16),
            jax.ShapeDtypeStruct((ni, PT, f2), BF16),
            jax.ShapeDtypeStruct((1, f2), F32),
            send_shape,
            keep_shape,
            send_shape,
            keep_shape,
        ],
        compiler_params=params(),
        cost_estimate=pl.CostEstimate(
            flops=8 * cfg.m * D * f2,
            bytes_accessed=8 * cfg.m * D + 8 * D * f2 + 4 * cfg.m * f2,
            transcendentals=2 * cfg.m * f2,
        ),
        name="mlp_chunk",
    )(scalars, mlp_in, cot, mlp_in_t, cot_t, fc1, *arrays)


def project_back(scalars, lefts, weights, part, cfg):
    flat, plan = [], []
    for arrays, wheres in weights:
        plan.append([(len(flat) + a, i) for a, i in wheres])
        flat += arrays
    n_t, f2, imgs = cfg.n_t, cfg.f2, cfg.imgs

    def kernel(s, *refs):
        left_refs = refs[:n_t]
        w_refs = refs[n_t : n_t + len(flat)]
        out_ref, w, sems = refs[n_t + len(flat) :]
        copies = [weight_copies(s, w_refs, plan[k], w.at[k], sems.at[k], cfg) for k in range(n_t)]

        @pl.when(pl.program_id(0) == 0)
        def _():
            for k in range(n_t):
                for copy in copies[k]:
                    copy.start()
            for k in range(n_t):
                for copy in copies[k]:
                    copy.wait()

        out = dot_nt(left_refs[0][0], w[0])
        for k in range(1, n_t):
            out = out + dot_nt(left_refs[k][0], w[k])
        out_ref[0] = out

    return pl.pallas_call(
        kernel,
        grid_spec=pltpu.PrefetchScalarGridSpec(
            num_scalar_prefetch=1,
            grid=(imgs,),
            in_specs=[pl.BlockSpec((1, PT, f2), lambda i, s: (part * imgs + i, 0, 0))] * n_t
            + [any_spec()] * len(flat),
            out_specs=image_spec(D),
            scratch_shapes=[
                pltpu.VMEM((n_t, D, f2), BF16),
                pltpu.SemaphoreType.DMA((n_t,)),
            ],
        ),
        out_shape=jax.ShapeDtypeStruct((imgs, PT, D), F32),
        compiler_params=params(),
        cost_estimate=pl.CostEstimate(
            flops=2 * imgs * PT * D * f2 * n_t,
            bytes_accessed=2 * n_t * D * f2 + 4 * imgs * PT * D,
            transcendentals=0,
        ),
        name="project_back",
    )(scalars, *lefts, *flat)


def plain_spec(width):
    return pl.BlockSpec((1, PT, width), lambda i: (i, 0, 0))


def plain_row(count=1):
    return pl.BlockSpec((count, D), lambda i: (0, 0))


def second_norm(x, part, other, shift_o, gain, shift, cfg):
    def kernel(x_ref, part_ref, other_ref, so_ref, gain_ref, shift_ref, hidden_ref, in_ref):
        hidden = x_ref[0].astype(F32) + (part_ref[0] + other_ref[0]) + so_ref[...]
        hidden_ref[0] = hidden
        normed, _ = norm(hidden)
        in_ref[0] = (normed * gain_ref[...] + shift_ref[...]).astype(BF16)

    return pl.pallas_call(
        kernel,
        grid=(cfg.imgs,),
        in_specs=[plain_spec(D)] * 3 + [plain_row()] * 3,
        out_specs=[plain_spec(D)] * 2,
        out_shape=[
            jax.ShapeDtypeStruct((cfg.imgs, PT, D), F32),
            jax.ShapeDtypeStruct((cfg.imgs, PT, D), BF16),
        ],
        compiler_params=params(),
        cost_estimate=pl.CostEstimate(
            flops=0, bytes_accessed=16 * cfg.imgs * PT * D, transcendentals=0
        ),
        name="second_norm",
    )(x, part, other, shift_o, gain, shift)


def second_norm_back(part, other, hidden, cot, gain, cfg):
    def kernel(part_ref, other_ref, hidden_ref, cot_ref, gain_ref, grad_ref, gradb_ref, sum_ref):
        @pl.when(pl.program_id(0) == 0)
        def _():
            sum_ref[...] = jnp.zeros_like(sum_ref)

        up = part_ref[0] + other_ref[0]
        normed, inverse = norm(hidden_ref[0])
        cot_f = cot_ref[0].astype(F32)
        grad = cot_f + norm_back(up, normed, inverse, gain_ref[...])
        grad_ref[0] = grad
        gradb_ref[0] = grad.astype(BF16)
        sum_ref[0:1, :] += jnp.sum(up * normed, axis=0, keepdims=True)
        sum_ref[1:2, :] += jnp.sum(up, axis=0, keepdims=True)
        sum_ref[2:3, :] += jnp.sum(grad, axis=0, keepdims=True)
        sum_ref[3:4, :] += jnp.sum(cot_f, axis=0, keepdims=True)

    return pl.pallas_call(
        kernel,
        grid=(cfg.imgs,),
        in_specs=[plain_spec(D)] * 4 + [plain_row()],
        out_specs=[plain_spec(D), plain_spec(D), plain_row(4)],
        out_shape=[
            jax.ShapeDtypeStruct((cfg.imgs, PT, D), F32),
            jax.ShapeDtypeStruct((cfg.imgs, PT, D), BF16),
            jax.ShapeDtypeStruct((4, D), F32),
        ],
        compiler_params=params(),
        cost_estimate=pl.CostEstimate(
            flops=0, bytes_accessed=20 * cfg.imgs * PT * D, transcendentals=0
        ),
        name="second_norm_back",
    )(part, other, hidden, cot, gain)


def first_norm_back(part, other, x, grad_hidden, gain, cfg):
    def kernel(part_ref, other_ref, x_ref, grad_ref, gain_ref, out_ref, sum_ref):
        @pl.when(pl.program_id(0) == 0)
        def _():
            sum_ref[...] = jnp.zeros_like(sum_ref)

        up = part_ref[0] + other_ref[0]
        normed, inverse = norm(x_ref[0].astype(F32))
        grad = grad_ref[0] + norm_back(up, normed, inverse, gain_ref[...])
        out_ref[0] = grad.astype(BF16)
        sum_ref[0:1, :] += jnp.sum(up * normed, axis=0, keepdims=True)
        sum_ref[1:2, :] += jnp.sum(up, axis=0, keepdims=True)

    return pl.pallas_call(
        kernel,
        grid=(cfg.imgs,),
        in_specs=[plain_spec(D)] * 4 + [plain_row()],
        out_specs=[plain_spec(D), plain_row(2)],
        out_shape=[
            jax.ShapeDtypeStruct((cfg.imgs, PT, D), BF16),
            jax.ShapeDtypeStruct((2, D), F32),
        ],
        compiler_params=params(),
        cost_estimate=pl.CostEstimate(
            flops=0, bytes_accessed=16 * cfg.imgs * PT * D, transcendentals=0
        ),
        name="first_norm_back",
    )(part, other, x, grad_hidden, gain)


def body(cfg, tokens, counts, gains, biases, fc1_bias, w_qkv, w_o, w_1, w_2, cotangent):
    n_t, n_dp, pd, f2, hc, imgs, ni = cfg.n_t, cfg.n_dp, cfg.pd, cfg.f2, cfg.hc, cfg.imgs, cfg.ni
    me = lax.axis_index("dp")
    z = lax.axis_index("tensor")
    core = me & 1
    scalars = jnp.stack([me >> 1, core, z]).astype(jnp.int32)
    ends = jnp.cumsum(counts[0]).astype(jnp.int32)
    starts = ends - counts[0]

    halves = jnp.stack(
        [
            jnp.concatenate(
                [
                    w_qkv.reshape(pd, 3, 2, hc).transpose(2, 0, 1, 3).reshape(2, pd, 3 * hc),
                    w_o.T.reshape(pd, 2, hc).transpose(1, 0, 2),
                ],
                axis=2,
            ),
            w_1.reshape(pd, 2, f2).transpose(1, 0, 2),
            w_2.T.reshape(pd, 2, f2).transpose(1, 0, 2),
        ],
        axis=1,
    )
    first_core = core == 0
    mine = jnp.where(first_core, halves[0], halves[1])
    theirs = swap_dp(jnp.where(first_core, halves[1], halves[0]), 1, cfg)
    unit_0 = jnp.stack([mine[0], theirs[0]])
    unit_1 = jnp.stack([mine[1], theirs[1]])
    unit_2 = jnp.stack([mine[2], theirs[2]])

    def turned(value, k):
        return value if k == 0 else turn_tensor(value, k, cfg)

    attn_blocks = [turned(unit_0, k) for k in range(n_t)]
    attn_weights = []
    for k in range(0, n_t, 2):
        arrays, where_a, where_b = gather_pair(attn_blocks[k], attn_blocks[k + 1], cfg)
        attn_weights += [(arrays, where_a), (arrays, where_b)]

    def paired(value):
        return jnp.concatenate([value, swap_dp(value, 1, cfg)])

    small = jnp.concatenate([gains, biases, fc1_bias.reshape(4, -1)])
    small = gather_small(small, cfg, me, z).reshape(n_dp * n_t, 12, -1)
    rows = small[:, :8].transpose(1, 0, 2).reshape(8, D)
    gain_all, shift_all = rows[:2], rows[2:]
    fc1_all = small[:, 8:].reshape(2 * n_t, f2)

    x_own = to_images(tokens, starts, ends, z, cfg).reshape(imgs, PT, D)
    x = paired(x_own)
    cot_own = to_images(cotangent, starts, ends, z, cfg).reshape(imgs, PT, D)
    cot = paired(cot_own)
    cot_t = cot.reshape(cfg.m, D).T

    attn_in, qkv, attended, lse, attn_out = attention_forward(
        scalars,
        x,
        gain_all[0:1],
        shift_all[0:1],
        shift_all[2].reshape(2 * n_t, hc),
        shift_all[3].reshape(2 * n_t, hc),
        attn_weights,
        cfg,
    )
    hidden, mlp_in_own = second_norm(
        x_own,
        attn_out[:imgs],
        swap_dp(attn_out[imgs:], 1, cfg),
        shift_all[4:5],
        gain_all[1:2],
        shift_all[1:2],
        cfg,
    )
    mlp_in = paired(mlp_in_own)
    mlp_in_t = mlp_in.reshape(cfg.m, D).T

    mlp_weights, acts, gpres, fc1_sums, mlp_grads = [], [], [], [], []
    for k in range(n_t):
        both = turned(jnp.stack([unit_1, unit_2]), k)
        weights = gather_pair(both[0], both[1], cfg)
        mlp_weights.append(weights)
        act, gpre, fc1_sum, send_1, keep_1, send_2, keep_2 = mlp_chunk(
            scalars, mlp_in, cot, mlp_in_t, cot_t, fc1_all, weights, k, cfg
        )
        acts.append(act)
        gpres.append(gpre)
        fc1_sums.append(fc1_sum)
        mlp_grads.append(scatter_pair(send_1, keep_1, send_2, keep_2, cfg))

    back = [(arrays, where_1) for arrays, where_1, _ in mlp_weights]
    out = [(arrays, where_2) for arrays, _, where_2 in mlp_weights]

    def summed(lefts, weights):
        pair_part = project_back(scalars, lefts, weights, 1, cfg)
        other = swap_dp(pair_part, 1, cfg)
        return project_back(scalars, lefts, weights, 0, cfg), other

    part, other = summed(gpres, back)
    grad_hidden, grad_hidden_b, sums_2 = second_norm_back(
        part, other, hidden, cot_own, gain_all[1:2], cfg
    )
    grad_hidden_b = paired(grad_hidden_b)
    gqkv, grad_in, dq, dv = attention_backward(
        scalars, grad_hidden_b, qkv, attended, lse, attn_weights, cfg
    )
    d_images, sums_1 = first_norm_back(
        grad_in[:imgs], swap_dp(grad_in[imgs:], 1, cfg), x_own, grad_hidden, gain_all[0:1], cfg
    )
    attn_in_t = attn_in.reshape(cfg.m, D).T
    grad_t = grad_hidden_b.reshape(cfg.m, D).T
    attn_grads = []
    for k in range(0, n_t, 2):
        pieces = attention_weights(scalars, attn_in_t, grad_t, gqkv, attended, k, cfg)
        attn_grads += list(scatter_pair(*pieces, cfg))

    part, other = summed(acts, out)
    mixed_own = (hidden + (part + other) + shift_all[5]).astype(BF16)
    mixed = to_blocks(mixed_own.reshape(imgs * PT, D), starts, ends, z, cfg)
    d_tokens = to_blocks(d_images.reshape(imgs * PT, D), starts, ends, z, cfg)

    total = jnp.stack([attn_grads[0], mlp_grads[0][0], mlp_grads[0][1]])
    for k in range(1, n_t):
        mlp_part = turn_tensor(jnp.stack(mlp_grads[k]).astype(BF16), -k, cfg)
        attn_part = turn_tensor(attn_grads[k].astype(BF16), -k, cfg)
        total = total + jnp.concatenate([attn_part[None], mlp_part]).astype(F32)
    mine = total[:, 0]
    theirs = swap_dp(total[:, 1], 1, cfg)
    half_0 = jnp.where(first_core, mine, theirs)
    half_1 = jnp.where(first_core, theirs, mine)
    d_qkv = jnp.stack(
        [half_0[0, :, : 3 * hc].reshape(pd, 3, hc), half_1[0, :, : 3 * hc].reshape(pd, 3, hc)],
        axis=2,
    ).reshape(pd, 3, 2 * hc)
    d_o = jnp.concatenate([half_0[0, :, 3 * hc :], half_1[0, :, 3 * hc :]], axis=1).T
    d_1 = jnp.concatenate([half_0[1], half_1[1]], axis=1)
    d_2 = jnp.concatenate([half_0[2], half_1[2]], axis=1).T

    order = (z - jnp.arange(n_t)) % n_t
    on_core = (jnp.arange(2) == core)[None, :, None]

    def placed(chunks):
        return jnp.where(on_core, jnp.take(chunks, order, axis=0)[:, None, :], 0.0)

    vectors = jnp.stack(
        [
            sums_1[0],
            sums_2[0],
            sums_1[1],
            sums_2[1],
            placed(dq).reshape(D),
            placed(dv).reshape(D),
            sums_2[2],
            sums_2[3],
        ]
    )
    vectors = vectors.reshape(8, n_dp, n_t, -1).transpose(1, 2, 0, 3)
    fc1_terms = placed(jnp.concatenate(fc1_sums)).reshape(n_dp, n_t, 4, -1)
    small = scatter_small(jnp.concatenate([vectors, fc1_terms], axis=2), cfg, me, z)
    return (
        mixed,
        d_tokens,
        d_qkv,
        d_o,
        d_1,
        d_2,
        small[:2],
        small[2:8],
        small[8:].reshape(-1),
    )


def solution(mesh):
    n_dp, n_t = mesh.shape["dp"], mesh.shape["tensor"]

    def program(tokens, *rest):
        cfg = Cfg(n_dp, n_t, tokens.shape[0])
        return body(cfg, tokens, *rest)

    both = ("dp", "tensor")
    return jax.shard_map(
        program,
        mesh=mesh,
        in_specs=(
            P(both, None),
            P("dp", None),
            P(None, both),
            P(None, both),
            P(both),
            P("dp", None, "tensor"),
            P("tensor", "dp"),
            P("dp", "tensor"),
            P("tensor", "dp"),
            P(both, None),
        ),
        out_specs=(
            P(both, None),
            P(both, None),
            P("dp", None, "tensor"),
            P("tensor", "dp"),
            P("dp", "tensor"),
            P("tensor", "dp"),
            P(None, both),
            P(None, both),
            P(both),
        ),
        check_vma=False,
    )
```

```python
import math

import jax
import jax.numpy as jnp
from jax import lax
from jax.experimental import pallas as pl
from jax.experimental.pallas import tpu as pltpu
from jax.sharding import Mesh
from jax.sharding import PartitionSpec as P

D = 1280
HD = 80
HEADS = 16
FF = 5120
TOK_IMG = 257
IMG_DEV = 8
TOTAL = IMG_DEV * TOK_IMG
EPS = 1e-06
PT = 272
F32 = jnp.float32
BF16 = jnp.bfloat16
NEG = -1e30
VMEM_LIMIT = 56 * 1024 * 1024


class Cfg:
    def __init__(self, n_dp, n_t, block_rows):
        self.n_dp, self.n_t, self.block = n_dp, n_t, block_rows
        self.n_p = n_dp // 2
        self.imgs = IMG_DEV // n_t
        self.ni = 2 * self.imgs
        self.rows = self.imgs * TOK_IMG
        self.m = self.ni * PT
        self.pd = D // n_dp
        self.hh = HEADS // n_t // 2
        self.hc = self.hh * HD
        self.f2 = FF // n_t // 2
        assert 4 * self.hc == self.f2
        self.caps = self._caps()

    def _caps(self):
        n, b, r = self.n_t, self.block, self.rows
        low = [max(t, TOTAL - (n - t) * b) for t in range(n + 1)]
        high = [min(t * b, TOTAL - (n - t)) for t in range(n + 1)]
        caps = {}
        for t in range(n):
            for dest in range(n):
                size = min(high[t + 1], r * (dest + 1)) - max(low[t], r * dest)
                size = min(size, b, r)
                if size > 0 and dest != t:
                    caps[dest - t] = max(caps.get(dest - t, 0), size)
        return {s: min(-(-c // 16) * 16, b, r) for s, c in sorted(caps.items())}


def dot(a, b):
    return lax.dot_general(a, b, (((1,), (0,)), ((), ())), preferred_element_type=F32)


def dot_nt(a, b):
    return lax.dot_general(a, b, (((1,), (1,)), ((), ())), preferred_element_type=F32)


def dot_tn(a, b):
    return lax.dot_general(a, b, (((0,), (0,)), ((), ())), preferred_element_type=F32)


def norm(values):
    mean = jnp.mean(values, axis=-1, keepdims=True)
    centred = values - mean
    spread = jnp.mean(centred * centred, axis=-1, keepdims=True)
    inverse = lax.rsqrt(spread + EPS)
    return centred * inverse, inverse


def norm_back(upstream, normed, inverse, gain):
    scaled = upstream * gain
    return inverse * (
        scaled
        - jnp.mean(scaled, axis=-1, keepdims=True)
        - normed * jnp.mean(scaled * normed, axis=-1, keepdims=True)
    )


CHIPS = ("p", "t")
ALL = ("p", "c", "t")


def swap_core(value):
    return lax.ppermute(value, "c", [(0, 1), (1, 0)])


def step_tensor(value, shift, cfg):
    pairs = [(i, i + shift) for i in range(cfg.n_t) if 0 <= i + shift < cfg.n_t]
    return lax.ppermute(value, "t", pairs)


def scatter_chips(value):
    return lax.psum_scatter(value, CHIPS, scatter_dimension=0, tiled=False)


def gather_small(value, cfg, where):
    for axis, size in (("t", cfg.n_t), ("c", 2), ("p", cfg.n_p)):
        value = value[None]
        bit = 1
        while bit < size:
            other = lax.ppermute(value, axis, [(i, i ^ bit) for i in range(size)])
            first = (where[axis] & bit) == 0
            value = jnp.concatenate([jnp.where(first, value, other), jnp.where(first, other, value)])
            bit *= 2
    return value


def scatter_small(value, cfg, where):
    for axis, size in (("p", cfg.n_p), ("c", 2), ("t", cfg.n_t)):
        bit = size // 2
        while bit >= 1:
            half = value.shape[0] // 2
            first = (where[axis] & bit) == 0
            keep = jnp.where(first, value[:half], value[half:])
            send = jnp.where(first, value[half:], value[:half])
            value = keep + lax.ppermute(send, axis, [(i, i ^ bit) for i in range(size)])
            bit //= 2
        value = value[0]
    return value


def pick(positions, limit):
    return (positions[:, None] == jnp.arange(limit, dtype=jnp.int32)[None, :]).astype(BF16)


def window_start(starts, t, dest, size, cfg):
    return jnp.clip(cfg.rows * dest - starts[t], 0, cfg.block - size)


def to_images(block, starts, ends, z, cfg):
    slot = jnp.arange(cfg.imgs * PT, dtype=jnp.int32)
    within = slot % PT
    place = cfg.rows * z + (slot // PT) * TOK_IMG + within
    valid = within < TOK_IMG
    owner = jnp.sum((place[:, None] >= ends[None, :]).astype(jnp.int32), axis=1)
    padded = jnp.where(valid & (owner == z), place - starts[z], -1)
    total = dot(pick(padded, cfg.block), block)
    for shift, size in cfg.caps.items():
        dest = jnp.clip(z + shift, 0, cfg.n_t - 1)
        sent = lax.dynamic_slice_in_dim(block, window_start(starts, z, dest, size, cfg), size)
        got = step_tensor(sent, shift, cfg)
        source = jnp.clip(z - shift, 0, cfg.n_t - 1)
        offset = place - starts[source] - window_start(starts, source, z, size, cfg)
        offset = jnp.where(valid & (owner == z - shift), offset, -1)
        total = total + dot(pick(offset, size), got)
    return total.astype(BF16)


def to_blocks(images, starts, ends, z, cfg):
    row = jnp.arange(cfg.block, dtype=jnp.int32)
    place = starts[z] + row
    valid = place < ends[z]
    owner = place // cfg.rows
    local = place - cfg.rows * z
    slots = (local // TOK_IMG) * PT + local % TOK_IMG
    total = dot(pick(jnp.where(valid & (owner == z), slots, -1), cfg.imgs * PT), images)
    for shift, size in cfg.caps.items():
        block_to = jnp.clip(z - shift, 0, cfg.n_t - 1)
        begin = jnp.clip(starts[block_to] - cfg.rows * z, 0, cfg.rows - size)
        want = begin + jnp.arange(size, dtype=jnp.int32)
        want = (want // TOK_IMG) * PT + want % TOK_IMG
        sent = dot(pick(want, cfg.imgs * PT), images).astype(BF16)
        got = step_tensor(sent, -shift, cfg)
        source = jnp.clip(z + shift, 0, cfg.n_t - 1)
        begin_there = jnp.clip(starts[z] - cfg.rows * source, 0, cfg.rows - size)
        offset = place - cfg.rows * source - begin_there
        offset = jnp.where(valid & (owner == z + shift), offset, -1)
        total = total + dot(pick(offset, size), got)
    return total.astype(BF16)


def params(**more):
    return pltpu.CompilerParams(vmem_limit_bytes=VMEM_LIMIT, **more)


def fixed(shape):
    return pl.BlockSpec(
        shape, lambda i, *s: (0,) * len(shape), pipeline_mode=pl.Buffered(1)
    )


def image_spec(width):
    return pl.BlockSpec((1, PT, width), lambda i, *s: (i, 0, 0))


def chunk_image_spec(n_t, width):
    return pl.BlockSpec((n_t, 1, PT, width), lambda i, *s: (0, i, 0, 0))


def row_spec(count=1, width=D):
    return pl.BlockSpec((count, width), lambda i, *s: (0, 0))


MESH = pl.DeviceIdType.MESH


def neighbours(cfg):
    p, t = lax.axis_index("p"), lax.axis_index("t")
    found = [{"t": lax.rem(t + k, cfg.n_t)} for k in range(1, cfg.n_t)]
    return found + [{"p": p ^ m} for m in range(1, cfg.n_p)]


def enter(cfg):
    barrier = pltpu.get_barrier_semaphore()
    found = neighbours(cfg)
    for device in found:
        pl.semaphore_signal(barrier, inc=1, device_id=device, device_id_type=MESH)
    pl.semaphore_wait(barrier, len(found))


def gather_and_attend(x, gain, shift, query_bias, value_bias, blocks, cfg):
    n_t, n_p, ni, hc, hh, f2, pd = cfg.n_t, cfg.n_p, cfg.ni, cfg.hc, cfg.hh, cfg.f2, cfg.pd

    def kernel(
        x_ref, gain_ref, shift_ref, qb_ref, vb_ref, blk_ref,
        in_ref, qkv_ref, att_ref, lse_ref, out_ref, g0_ref, g_ref,
        w, z_send, z_recv, p_send, p_recv, own_sem, out_sem,
    ):
        p, core, z = (lax.axis_index(axis) for axis in ALL)

        def own(group):
            return blk_ref.at[0] if group == 0 else blk_ref.at[pl.ds(1, 2)]

        def place(group, k, m):
            t = lax.rem(z - k + n_t, n_t)
            rows = pl.ds(pl.multiple_of((p ^ m) * 2 * pd, 16), 2 * pd)
            return w.at[t, rows, :] if group == 0 else g_ref.at[:, t, rows, :]

        def remote(source, target, sems, index, device):
            return pltpu.make_async_remote_copy(
                src_ref=source,
                dst_ref=target,
                send_sem=sems[0].at[index],
                recv_sem=sems[1].at[index],
                device_id=device,
                device_id_type=MESH,
            )

        def z_copy(group, k):
            return remote(
                own(group), place(group, 0, 0), (z_send, z_recv), (group, k),
                {"t": lax.rem(z + k, n_t)},
            )

        def p_copy(group, k, m):
            source = own(group) if k == 0 else place(group, k, 0)
            return remote(
                source, place(group, k, 0), (p_send, p_recv), (group, k, m), {"p": p ^ m}
            )

        def d_copies(group, k):
            if n_p != 4:
                return []
            t = lax.rem(z - k + n_t, n_t)

            def rows(m):
                return pl.ds(pl.multiple_of((p ^ m) * 2 * pd, 16), 2 * pd)

            if group == 0:
                via = 1 + k % 2
                ref = w.at[t, rows(via), :]
                return [remote(ref, ref, (p_send, p_recv), (group, k, 3), {"p": p ^ (3 - via)})]
            ref_1, ref_2 = g_ref.at[0, t, rows(1), :], g_ref.at[1, t, rows(2), :]
            return [
                remote(ref_1, ref_1, (p_send, p_recv), (group, k, 3), {"p": p ^ 2}),
                remote(ref_2, ref_2, (p_send, p_recv), (group, k, 0), {"p": p ^ 1}),
            ]

        direct = (1, 2) if n_p == 4 else tuple(range(1, n_p))

        def send_z(group):
            for k in range(1, n_t):
                z_copy(group, k).start()

        def send_p(group, k):
            if k > 0:
                z_copy(group, k).wait_recv()
            for m in direct:
                p_copy(group, k, m).start()

        def send_d(group, k):
            for m in direct:
                p_copy(group, k, m).wait_recv()
            for copy in d_copies(group, k):
                copy.start()

        def finish(group):
            for k in range(n_t):
                for copy in d_copies(group, k):
                    copy.wait_recv()
                    copy.wait_send()
                for m in direct:
                    p_copy(group, k, m).wait_send()
                if k > 0:
                    z_copy(group, k).wait_send()

        keep_0 = pltpu.make_async_copy(own(0), place(0, 0, 0), own_sem.at[0])
        keep_1 = pltpu.make_async_copy(own(1), place(1, 0, 0), own_sem.at[1])
        keep_0.start()
        keep_1.start()
        enter(cfg)
        send_z(0)
        send_p(0, 0)
        for k in range(1, n_t):
            send_p(0, k)
            if k == 1:
                send_z(1)
            send_d(0, k - 1)
        send_p(1, 0)
        send_d(0, n_t - 1)
        finish(0)
        keep_0.wait()
        kept = pltpu.make_async_copy(w, g0_ref, out_sem)
        kept.start()

        steps = []
        for k in range(1, n_t):
            steps += [lambda k=k: send_p(1, k), lambda k=k: send_d(1, k - 1)]
        steps.append(lambda: send_d(1, n_t - 1))
        early = 2 * len(steps) // 5
        keyed = lax.broadcasted_iota(jnp.int32, (PT, PT), 1) < TOK_IMG

        def image(i, carry):
            normed, _ = norm(x_ref[i].astype(F32))
            attn_in = (normed * gain_ref[...] + shift_ref[...]).astype(BF16)
            in_ref[i] = attn_in
            for k in range(n_t):
                block = 2 * k + core
                qkv = dot(attn_in, w[k, :, : 3 * hc])
                query = (qkv[:, :hc] + qb_ref[pl.ds(block, 1), :]).astype(BF16)
                keys = qkv[:, hc : 2 * hc].astype(BF16)
                values = (qkv[:, 2 * hc :] + vb_ref[pl.ds(block, 1), :]).astype(BF16)
                qkv_ref[k, i, :, :hc] = query
                qkv_ref[k, i, :, hc : 2 * hc] = keys
                qkv_ref[k, i, :, 2 * hc :] = values
                for h in range(hh):
                    cols = slice(h * HD, (h + 1) * HD)
                    scores = dot_nt(query[:, cols], keys[:, cols]) * (HD**-0.5)
                    scores = jnp.where(keyed, scores, NEG)
                    top = jnp.max(scores, axis=-1, keepdims=True)
                    expo = jnp.exp(scores - top)
                    summed = jnp.sum(expo, axis=-1, keepdims=True)
                    probs = (expo / summed).astype(BF16)
                    att_ref[k, i, :, cols] = dot(probs, values[:, cols]).astype(BF16)
                    j = k * hh + h
                    lse_ref[i, :, j : j + 1] = top + jnp.log(summed)
                part = dot_nt(att_ref[k, i], w[k, :, 3 * hc :])
                if k == 0:
                    out_ref[i] = part
                else:
                    out_ref[i] += part
            for j in range(early):

                @pl.when(i == (j + 1) * ni // early - 1)
                def _(j=j):
                    steps[j]()

            return carry

        lax.fori_loop(0, ni, image, 0)
        for step in steps[early:]:
            step()
        finish(1)
        keep_1.wait()
        kept.wait()

    vmem = pl.BlockSpec(memory_space=pltpu.VMEM)
    anywhere = pl.BlockSpec(memory_space=pl.ANY)
    dma = pltpu.SemaphoreType.DMA
    return pl.pallas_call(
        kernel,
        in_specs=[vmem] * 5 + [anywhere],
        out_specs=[vmem] * 5 + [anywhere] * 2,
        out_shape=[
            jax.ShapeDtypeStruct((ni, PT, D), BF16),
            jax.ShapeDtypeStruct((n_t, ni, PT, 3 * hc), BF16),
            jax.ShapeDtypeStruct((n_t, ni, PT, hc), BF16),
            jax.ShapeDtypeStruct((ni, PT, n_t * hh), F32),
            jax.ShapeDtypeStruct((ni, PT, D), F32),
            jax.ShapeDtypeStruct((n_t, D, f2), BF16),
            jax.ShapeDtypeStruct((2, n_t, D, f2), BF16),
        ],
        scratch_shapes=[
            pltpu.VMEM((n_t, D, f2), BF16),
            dma((2, n_t)),
            dma((2, n_t)),
            dma((2, n_t, n_p)),
            dma((2, n_t, n_p)),
            dma((2,)),
            dma,
        ],
        compiler_params=params(collective_id=0, has_side_effects=True),
        cost_estimate=pl.CostEstimate(
            flops=2 * cfg.m * D * f2 * n_t,
            bytes_accessed=2 * n_t * D * f2 + 12 * cfg.m * D,
            transcendentals=cfg.m * PT * n_t * hh,
        ),
        name="gather_and_attend",
    )(x, gain, shift, query_bias, value_bias, blocks)


def attention_backward(grad_hidden, qkv, attended, lse, weights, cfg):
    n_t, hc, hh = cfg.n_t, cfg.hc, cfg.hh
    scale = HD**-0.5

    def kernel(gh_ref, qkv_ref, att_ref, lse_ref, w_ref, gqkv_ref, out_ref, dq_ref, dv_ref):
        @pl.when(pl.program_id(0) == 0)
        def _():
            dq_ref[...] = jnp.zeros_like(dq_ref)
            dv_ref[...] = jnp.zeros_like(dv_ref)

        keyed = lax.broadcasted_iota(jnp.int32, (PT, PT), 1) < TOK_IMG
        grad_hidden_b = gh_ref[0]
        out = jnp.zeros((PT, D), F32)
        for k in range(n_t):
            w = w_ref[k]
            grad_att = dot(grad_hidden_b, w[:, 3 * hc :]).astype(BF16)
            for h in range(hh):
                cols = slice(h * HD, (h + 1) * HD)
                key_cols = slice(hc + h * HD, hc + (h + 1) * HD)
                value_cols = slice(2 * hc + h * HD, 2 * hc + (h + 1) * HD)
                query = qkv_ref[k, 0, :, cols]
                keys = qkv_ref[k, 0, :, key_cols]
                values = qkv_ref[k, 0, :, value_cols]
                grad = grad_att[:, cols]
                j = k * hh + h
                scores = dot_nt(query, keys) * scale - lse_ref[0, :, j : j + 1]
                probs = jnp.exp(jnp.where(keyed, scores, NEG))
                delta = jnp.sum(
                    grad.astype(F32) * att_ref[k, 0, :, cols].astype(F32), axis=-1, keepdims=True
                )
                grad_v = dot_tn(probs.astype(BF16), grad)
                grad_s = (probs * (dot_nt(grad, values) - delta) * scale).astype(BF16)
                grad_q = dot(grad_s, keys)
                grad_k = dot_tn(grad_s, query)
                dq_ref[k : k + 1, cols] += jnp.sum(grad_q, axis=0, keepdims=True)
                dv_ref[k : k + 1, cols] += jnp.sum(grad_v, axis=0, keepdims=True)
                gqkv_ref[k, 0, :, cols] = grad_q.astype(BF16)
                gqkv_ref[k, 0, :, key_cols] = grad_k.astype(BF16)
                gqkv_ref[k, 0, :, value_cols] = grad_v.astype(BF16)
            out = out + dot_nt(gqkv_ref[k, 0], w[:, : 3 * hc])
        out_ref[0] = out

    return pl.pallas_call(
        kernel,
        grid=(cfg.ni,),
        in_specs=[
            image_spec(D),
            chunk_image_spec(n_t, 3 * hc),
            chunk_image_spec(n_t, hc),
            image_spec(n_t * hh),
            fixed((n_t, D, cfg.f2)),
        ],
        out_specs=[
            chunk_image_spec(n_t, 3 * hc),
            image_spec(D),
            row_spec(n_t, hc),
            row_spec(n_t, hc),
        ],
        out_shape=[
            jax.ShapeDtypeStruct((n_t, cfg.ni, PT, 3 * hc), BF16),
            jax.ShapeDtypeStruct((cfg.ni, PT, D), F32),
            jax.ShapeDtypeStruct((n_t, hc), F32),
            jax.ShapeDtypeStruct((n_t, hc), F32),
        ],
        compiler_params=params(),
        cost_estimate=pl.CostEstimate(
            flops=2 * cfg.m * D * cfg.f2 * n_t + 10 * cfg.m * PT * HD * n_t * hh,
            bytes_accessed=2 * n_t * D * cfg.f2 + 12 * cfg.m * D,
            transcendentals=cfg.m * PT * n_t * hh,
        ),
        name="attention_backward",
    )(grad_hidden, qkv, attended, lse, weights)


def attention_weights(attn_in_t, grad_t, gqkv, attended, cfg):
    hc, n_p, n_t = cfg.hc, cfg.n_p, cfg.n_t

    def kernel(in_ref, gt_ref, gqkv_ref, att_ref, out_ref):
        left = dot(in_ref[...], gqkv_ref[0]).astype(BF16)
        right = dot(gt_ref[...], att_ref[0]).astype(BF16)
        out_ref[:, 0, :, : 3 * hc] = left.reshape(n_p, 2 * cfg.pd, 3 * hc)
        out_ref[:, 0, :, 3 * hc :] = right.reshape(n_p, 2 * cfg.pd, hc)

    return pl.pallas_call(
        kernel,
        grid=(n_t,),
        in_specs=[
            fixed((D, cfg.m)),
            fixed((D, cfg.m)),
            pl.BlockSpec((1, cfg.m, 3 * hc), lambda i: (i, 0, 0)),
            pl.BlockSpec((1, cfg.m, hc), lambda i: (i, 0, 0)),
        ],
        out_specs=pl.BlockSpec((n_p, 1, 2 * cfg.pd, cfg.f2), lambda i: (0, i, 0, 0)),
        out_shape=jax.ShapeDtypeStruct((n_p, n_t, 2 * cfg.pd, cfg.f2), BF16),
        compiler_params=params(),
        cost_estimate=pl.CostEstimate(
            flops=2 * cfg.m * D * cfg.f2 * n_t,
            bytes_accessed=4 * cfg.m * D + 2 * D * cfg.f2 * n_t,
            transcendentals=0,
        ),
        name="attention_weights",
    )(
        attn_in_t,
        grad_t,
        gqkv.reshape(n_t, cfg.m, 3 * hc),
        attended.reshape(n_t, cfg.m, hc),
    )


def mlp_pass(scalars, mlp_in, cot, mlp_in_t, cot_t, fc1, weights, cfg):
    n_p, n_t, m, pd, w = cfg.n_p, cfg.n_t, cfg.m, cfg.pd, cfg.f2

    def kernel(
        s, in_ref, cot_ref, in_t_ref, cot_t_ref, fc1_ref, w1_ref, w2_ref,
        act_ref, sum_ref, grad_ref, back_ref, gpre_all,
    ):
        step = pl.program_id(0)
        w1, w2 = w1_ref[0, 0], w2_ref[0, 0]
        total = jnp.zeros((1, w), F32)
        for i in range(cfg.ni):
            rows = slice(i * PT, (i + 1) * PT)
            pre = dot(in_ref[rows, :], w1) + fc1_ref[pl.ds(2 * step + s[0], 1), :]
            phi = 0.5 * (1.0 + lax.erf(pre * (1.0 / math.sqrt(2.0))))
            act_ref[0, rows, :] = (pre * phi).astype(BF16)
            slope = phi + pre * jnp.exp(-0.5 * pre * pre) * (1.0 / math.sqrt(2.0 * math.pi))
            gpre = dot(cot_ref[rows, :], w2) * slope
            total = total + jnp.sum(gpre, axis=0, keepdims=True)
            gpre_all[rows, :] = gpre.astype(BF16)
        sum_ref[0] = total
        grad_ref[:, 0, 0] = dot(in_t_ref[...], gpre_all[...]).astype(BF16).reshape(n_p, 2 * pd, w)
        grad_ref[:, 0, 1] = dot(cot_t_ref[...], act_ref[0]).astype(BF16).reshape(n_p, 2 * pd, w)
        back = dot_nt(gpre_all[...], w1)

        @pl.when(step == 0)
        def _():
            back_ref[...] = back

        @pl.when(step > 0)
        def _():
            back_ref[...] += back

    def half_spec(unit):
        return pl.BlockSpec((1, 1, D, w), lambda i, s: (unit, i, 0, 0))

    full = fixed((m, D))
    return pl.pallas_call(
        kernel,
        grid_spec=pltpu.PrefetchScalarGridSpec(
            num_scalar_prefetch=1,
            grid=(n_t,),
            in_specs=[full, full, fixed((D, m)), fixed((D, m)), row_spec(2 * n_t, w)]
            + [half_spec(0), half_spec(1)],
            out_specs=[
                pl.BlockSpec((1, m, w), lambda i, s: (i, 0, 0)),
                pl.BlockSpec((1, 1, w), lambda i, s: (i, 0, 0)),
                pl.BlockSpec((n_p, 1, 2, 2 * pd, w), lambda i, s: (0, i, 0, 0, 0)),
                pl.BlockSpec((m, D), lambda i, s: (0, 0)),
            ],
            scratch_shapes=[pltpu.VMEM((m, w), BF16)],
        ),
        out_shape=[
            jax.ShapeDtypeStruct((n_t, m, w), BF16),
            jax.ShapeDtypeStruct((n_t, 1, w), F32),
            jax.ShapeDtypeStruct((n_p, n_t, 2, 2 * pd, w), BF16),
            jax.ShapeDtypeStruct((m, D), F32),
        ],
        compiler_params=params(),
        cost_estimate=pl.CostEstimate(
            flops=10 * m * D * w * n_t,
            bytes_accessed=12 * m * D + 8 * D * w * n_t + 2 * m * w * n_t,
            transcendentals=2 * m * w * n_t,
        ),
        name="mlp_pass",
    )(scalars, mlp_in, cot, mlp_in_t, cot_t, fc1, weights, weights)


def mlp_output(act, weights, cfg):
    n_t, m, f2 = cfg.n_t, cfg.m, cfg.f2

    def kernel(act_ref, w_ref, out_ref):
        total = dot_nt(act_ref[0], w_ref[0, 0])

        @pl.when(pl.program_id(0) == 0)
        def _():
            out_ref[...] = total

        @pl.when(pl.program_id(0) > 0)
        def _():
            out_ref[...] += total

    return pl.pallas_call(
        kernel,
        grid=(n_t,),
        in_specs=[
            pl.BlockSpec((1, m, f2), lambda i: (i, 0, 0)),
            pl.BlockSpec((1, 1, D, f2), lambda i: (1, i, 0, 0)),
        ],
        out_specs=pl.BlockSpec((m, D), lambda i: (0, 0)),
        out_shape=jax.ShapeDtypeStruct((m, D), F32),
        compiler_params=params(),
        cost_estimate=pl.CostEstimate(
            flops=2 * m * D * f2 * n_t,
            bytes_accessed=4 * m * D + 2 * D * f2 * n_t,
            transcendentals=0,
        ),
        name="mlp_output",
    )(act, weights)


def second_norm(x, part, other, shift_o, gain, shift, cfg):
    def kernel(x_ref, part_ref, other_ref, so_ref, gain_ref, shift_ref, hidden_ref, in_ref):
        hidden = x_ref[0].astype(F32) + (part_ref[0] + other_ref[0]) + so_ref[...]
        hidden_ref[0] = hidden
        normed, _ = norm(hidden)
        in_ref[0] = (normed * gain_ref[...] + shift_ref[...]).astype(BF16)

    return pl.pallas_call(
        kernel,
        grid=(cfg.imgs,),
        in_specs=[image_spec(D)] * 3 + [row_spec()] * 3,
        out_specs=[image_spec(D)] * 2,
        out_shape=[
            jax.ShapeDtypeStruct((cfg.imgs, PT, D), F32),
            jax.ShapeDtypeStruct((cfg.imgs, PT, D), BF16),
        ],
        compiler_params=params(),
        cost_estimate=pl.CostEstimate(
            flops=0, bytes_accessed=16 * cfg.imgs * PT * D, transcendentals=0
        ),
        name="second_norm",
    )(x, part, other, shift_o, gain, shift)


def second_norm_back(part, other, hidden, cot, gain, cfg):
    def kernel(part_ref, other_ref, hidden_ref, cot_ref, gain_ref, grad_ref, gradb_ref, sum_ref):
        @pl.when(pl.program_id(0) == 0)
        def _():
            sum_ref[...] = jnp.zeros_like(sum_ref)

        up = part_ref[0] + other_ref[0]
        normed, inverse = norm(hidden_ref[0])
        cot_f = cot_ref[0].astype(F32)
        grad = cot_f + norm_back(up, normed, inverse, gain_ref[...])
        grad_ref[0] = grad
        gradb_ref[0] = grad.astype(BF16)
        sum_ref[0:1, :] += jnp.sum(up * normed, axis=0, keepdims=True)
        sum_ref[1:2, :] += jnp.sum(up, axis=0, keepdims=True)
        sum_ref[2:3, :] += jnp.sum(grad, axis=0, keepdims=True)
        sum_ref[3:4, :] += jnp.sum(cot_f, axis=0, keepdims=True)

    return pl.pallas_call(
        kernel,
        grid=(cfg.imgs,),
        in_specs=[image_spec(D)] * 4 + [row_spec()],
        out_specs=[image_spec(D), image_spec(D), row_spec(4)],
        out_shape=[
            jax.ShapeDtypeStruct((cfg.imgs, PT, D), F32),
            jax.ShapeDtypeStruct((cfg.imgs, PT, D), BF16),
            jax.ShapeDtypeStruct((4, D), F32),
        ],
        compiler_params=params(),
        cost_estimate=pl.CostEstimate(
            flops=0, bytes_accessed=20 * cfg.imgs * PT * D, transcendentals=0
        ),
        name="second_norm_back",
    )(part, other, hidden, cot, gain)


def first_norm_back(part, other, x, grad_hidden, gain, cfg):
    def kernel(part_ref, other_ref, x_ref, grad_ref, gain_ref, out_ref, sum_ref):
        @pl.when(pl.program_id(0) == 0)
        def _():
            sum_ref[...] = jnp.zeros_like(sum_ref)

        up = part_ref[0] + other_ref[0]
        normed, inverse = norm(x_ref[0].astype(F32))
        grad = grad_ref[0] + norm_back(up, normed, inverse, gain_ref[...])
        out_ref[0] = grad.astype(BF16)
        sum_ref[0:1, :] += jnp.sum(up * normed, axis=0, keepdims=True)
        sum_ref[1:2, :] += jnp.sum(up, axis=0, keepdims=True)

    return pl.pallas_call(
        kernel,
        grid=(cfg.imgs,),
        in_specs=[image_spec(D)] * 4 + [row_spec()],
        out_specs=[image_spec(D), row_spec(2)],
        out_shape=[
            jax.ShapeDtypeStruct((cfg.imgs, PT, D), BF16),
            jax.ShapeDtypeStruct((2, D), F32),
        ],
        compiler_params=params(),
        cost_estimate=pl.CostEstimate(
            flops=0, bytes_accessed=16 * cfg.imgs * PT * D, transcendentals=0
        ),
        name="first_norm_back",
    )(part, other, x, grad_hidden, gain)


def body(cfg, tokens, counts, gains, biases, fc1_bias, w_qkv, w_o, w_1, w_2, cotangent):
    n_t, n_p, pd, f2, hc, imgs, m = cfg.n_t, cfg.n_p, cfg.pd, cfg.f2, cfg.hc, cfg.imgs, cfg.m
    where = {axis: lax.axis_index(axis) for axis in ALL}
    core, z = where["c"], where["t"]
    scalars = core[None].astype(jnp.int32)
    ends = jnp.cumsum(counts[0]).astype(jnp.int32)
    starts = ends - counts[0]
    first_core = core == 0

    def traded(halves):
        mine = jnp.where(first_core, halves[0], halves[1])
        theirs = swap_core(jnp.where(first_core, halves[1], halves[0]))
        rows = jnp.where(
            first_core, jnp.stack([mine, theirs], axis=-3), jnp.stack([theirs, mine], axis=-3)
        )
        return rows.reshape(rows.shape[:-3] + (2 * pd, rows.shape[-1]))

    blocks = traded(
        jnp.stack(
            [
                jnp.concatenate(
                    [
                        w_qkv.reshape(pd, 3, 2, hc).transpose(2, 0, 1, 3).reshape(2, pd, 3 * hc),
                        w_o.T.reshape(pd, 2, hc).transpose(1, 0, 2),
                    ],
                    axis=2,
                ),
                w_1.reshape(pd, 2, f2).transpose(1, 0, 2),
                w_2.T.reshape(pd, 2, f2).transpose(1, 0, 2),
            ],
            axis=1,
        )
    )

    def paired(value):
        return jnp.concatenate([value, swap_core(value)])

    small = jnp.concatenate([gains, biases, fc1_bias.reshape(4, -1)])
    small = gather_small(small, cfg, where).reshape(cfg.n_dp * n_t, 12, -1)
    rows = small[:, :8].transpose(1, 0, 2).reshape(8, D)
    gain_all, shift_all = rows[:2], rows[2:]
    fc1_all = small[:, 8:].reshape(2 * n_t, f2)

    x_own = to_images(tokens, starts, ends, z, cfg).reshape(imgs, PT, D)
    x = paired(x_own)
    cot_own = to_images(cotangent, starts, ends, z, cfg).reshape(imgs, PT, D)
    cot = paired(cot_own).reshape(m, D)
    cot_t = cot.T

    attn_in, qkv, attended, lse, attn_out, attn_w, mlp_w = gather_and_attend(
        x,
        gain_all[0:1],
        shift_all[0:1],
        shift_all[2].reshape(2 * n_t, hc),
        shift_all[3].reshape(2 * n_t, hc),
        blocks,
        cfg,
    )
    hidden, mlp_in_own = second_norm(
        x_own,
        attn_out[:imgs],
        swap_core(attn_out[imgs:]),
        shift_all[4:5],
        gain_all[1:2],
        shift_all[1:2],
        cfg,
    )
    mlp_in = paired(mlp_in_own).reshape(m, D)
    mlp_in_t = mlp_in.T

    act, fc1_sums, mlp_grads, back = mlp_pass(
        scalars, mlp_in, cot, mlp_in_t, cot_t, fc1_all, mlp_w, cfg
    )
    mlp_grads = scatter_chips(mlp_grads.reshape(n_p * n_t, 2, 2 * pd, f2))

    back = back.reshape(2, imgs, PT, D)
    grad_hidden, grad_hidden_b, sums_2 = second_norm_back(
        back[0], swap_core(back[1]), hidden, cot_own, gain_all[1:2], cfg
    )
    grad_hidden_b = paired(grad_hidden_b)
    gqkv, grad_in, dq, dv = attention_backward(
        grad_hidden_b, qkv, attended, lse, attn_w, cfg
    )
    d_images, sums_1 = first_norm_back(
        grad_in[:imgs], swap_core(grad_in[imgs:]), x_own, grad_hidden, gain_all[0:1], cfg
    )
    attn_grads = attention_weights(
        attn_in.reshape(m, D).T, grad_hidden_b.reshape(m, D).T, gqkv, attended, cfg
    )
    attn_grads = scatter_chips(attn_grads.reshape(n_p * n_t, 2 * pd, f2))

    out = mlp_output(act, mlp_w, cfg).reshape(2, imgs, PT, D)
    mixed_own = (hidden + (out[0] + swap_core(out[1])) + shift_all[5]).astype(BF16)
    mixed = to_blocks(mixed_own.reshape(imgs * PT, D), starts, ends, z, cfg)
    d_tokens = to_blocks(d_images.reshape(imgs * PT, D), starts, ends, z, cfg)

    def untraded(rows):
        rows = rows.reshape(rows.shape[:-2] + (2, pd, rows.shape[-1]))
        mine = jnp.where(first_core, rows[..., 0, :, :], rows[..., 1, :, :])
        theirs = swap_core(jnp.where(first_core, rows[..., 1, :, :], rows[..., 0, :, :]))
        return (
            jnp.where(first_core, mine, theirs).astype(F32),
            jnp.where(first_core, theirs, mine).astype(F32),
        )

    half_0, half_1 = untraded(attn_grads)
    d_qkv = jnp.stack(
        [half_0[:, : 3 * hc].reshape(pd, 3, hc), half_1[:, : 3 * hc].reshape(pd, 3, hc)], axis=2
    ).reshape(pd, 3, 2 * hc)
    d_o = jnp.concatenate([half_0[:, 3 * hc :], half_1[:, 3 * hc :]], axis=1).T
    both = jnp.concatenate(untraded(mlp_grads), axis=-1)
    d_1, d_2 = both[0], both[1].T

    def placed(chunks):
        on_core = (jnp.arange(2) == core)[None, :, None]
        return jnp.where(on_core, chunks[:, None, :], 0.0)

    vectors = jnp.stack(
        [
            sums_1[0],
            sums_2[0],
            sums_1[1],
            sums_2[1],
            placed(dq).reshape(D),
            placed(dv).reshape(D),
            sums_2[2],
            sums_2[3],
        ]
    )
    vectors = vectors.reshape(8, n_p, 2, n_t, -1).transpose(1, 2, 3, 0, 4)
    fc1_terms = placed(fc1_sums[:, 0]).reshape(n_p, 2, n_t, 4, -1)
    small = scatter_small(jnp.concatenate([vectors, fc1_terms], axis=3), cfg, where)
    return (
        mixed,
        d_tokens,
        d_qkv,
        d_o,
        d_1,
        d_2,
        small[:2],
        small[2:8],
        small[8:].reshape(-1),
    )


def solution(mesh):
    n_dp, n_t = mesh.shape["dp"], mesh.shape["tensor"]
    split = Mesh(mesh.devices.reshape(n_dp // 2, 2, n_t), ALL)

    def program(tokens, *rest):
        cfg = Cfg(n_dp, n_t, tokens.shape[0])
        return body(cfg, tokens, *rest)

    dp = ("p", "c")
    return jax.shard_map(
        program,
        mesh=split,
        in_specs=(
            P(ALL, None),
            P(dp, None),
            P(None, ALL),
            P(None, ALL),
            P(ALL),
            P(dp, None, "t"),
            P("t", dp),
            P(dp, "t"),
            P("t", dp),
            P(ALL, None),
        ),
        out_specs=(
            P(ALL, None),
            P(ALL, None),
            P(dp, None, "t"),
            P("t", dp),
            P(dp, "t"),
            P("t", dp),
            P(None, ALL),
            P(None, ALL),
            P(ALL),
        ),
        check_vma=False,
    )
```

```python
import math

import jax
import jax.numpy as jnp
from jax import lax
from jax.experimental import pallas as pl
from jax.experimental.pallas import tpu as pltpu
from jax.sharding import Mesh
from jax.sharding import PartitionSpec as P

D = 1280
HD = 80
HEADS = 16
FF = 5120
TOK_IMG = 257
IMG_DEV = 8
TOTAL = IMG_DEV * TOK_IMG
EPS = 1e-06
PT = 272
F32 = jnp.float32
BF16 = jnp.bfloat16
NEG = -1e30
VMEM_LIMIT = 61 * 1024 * 1024


class Cfg:
    def __init__(self, n_dp, n_t, block_rows):
        self.n_dp, self.n_t, self.block = n_dp, n_t, block_rows
        self.n_p = n_dp // 2
        self.imgs = IMG_DEV // n_t
        self.ni = 2 * self.imgs
        self.rows = self.imgs * TOK_IMG
        self.m = self.ni * PT
        self.pd = D // n_dp
        self.hh = HEADS // n_t // 2
        self.hc = self.hh * HD
        self.f2 = FF // n_t // 2
        assert 4 * self.hc == self.f2
        self.caps = self._caps()

    def _caps(self):
        n, b, r = self.n_t, self.block, self.rows
        low = [max(t, TOTAL - (n - t) * b) for t in range(n + 1)]
        high = [min(t * b, TOTAL - (n - t)) for t in range(n + 1)]
        caps = {}
        for t in range(n):
            for dest in range(n):
                size = min(high[t + 1], r * (dest + 1)) - max(low[t], r * dest)
                size = min(size, b, r)
                if size > 0 and dest != t:
                    caps[dest - t] = max(caps.get(dest - t, 0), size)
        return {s: min(-(-c // 16) * 16, b) for s, c in sorted(caps.items())}


def dot(a, b):
    return lax.dot_general(a, b, (((1,), (0,)), ((), ())), preferred_element_type=F32)


def dot_nt(a, b):
    return lax.dot_general(a, b, (((1,), (1,)), ((), ())), preferred_element_type=F32)


def dot_tn(a, b):
    return lax.dot_general(a, b, (((0,), (0,)), ((), ())), preferred_element_type=F32)


def norm(values):
    mean = jnp.mean(values, axis=-1, keepdims=True)
    centred = values - mean
    spread = jnp.mean(centred * centred, axis=-1, keepdims=True)
    inverse = lax.rsqrt(spread + EPS)
    return centred * inverse, inverse


def norm_back(upstream, normed, inverse, gain):
    scaled = upstream * gain
    return inverse * (
        scaled
        - jnp.mean(scaled, axis=-1, keepdims=True)
        - normed * jnp.mean(scaled * normed, axis=-1, keepdims=True)
    )


ALL = ("p", "c", "t")


def params(**more):
    return pltpu.CompilerParams(vmem_limit_bytes=VMEM_LIMIT, **more)


def fixed(shape):
    return pl.BlockSpec(
        shape, lambda i, *s: (0,) * len(shape), pipeline_mode=pl.Buffered(1)
    )


MESH = pl.DeviceIdType.MESH


def enter(cfg):
    p, c, t = (lax.axis_index(axis) for axis in ALL)
    found = [{"c": 1 - c}]
    found += [{"t": lax.rem(t + k, cfg.n_t)} for k in range(1, cfg.n_t)]
    found += [{"p": p ^ m} for m in range(1, cfg.n_p)]
    barrier = pltpu.get_barrier_semaphore()
    for device in found:
        pl.semaphore_signal(barrier, inc=1, device_id=device, device_id_type=MESH)
    pl.semaphore_wait(barrier, len(found))


def greet_pair():
    barrier = pltpu.get_barrier_semaphore()
    other = {"c": 1 - lax.axis_index("c")}
    pl.semaphore_signal(barrier, inc=1, device_id=other, device_id_type=MESH)
    pl.semaphore_wait(barrier, 1)


def remote(source, target, sems, index, device):
    return pltpu.make_async_remote_copy(
        src_ref=source,
        dst_ref=target,
        send_sem=sems[0].at[index],
        recv_sem=sems[1].at[index],
        device_id=device,
        device_id_type=MESH,
    )


class Layout:
    def __init__(self, counts_ref, cfg):
        self.counts, self.cfg = counts_ref, cfg
        self.z = lax.axis_index("t")

    def start(self, block):
        total = 0
        for j in range(self.cfg.n_t):
            total = total + jnp.where(block > j, self.counts[0, j], 0)
        return total

    def end(self, block):
        return self.start(block + 1)

    def has(self, block):
        return (block >= 0) & (block < self.cfg.n_t)

    def window(self, block, dest, size):
        return jnp.clip(self.cfg.rows * dest - self.start(block), 0, self.cfg.block - size)

    def window_back(self, dest, block, size):
        return jnp.clip(self.start(block) - self.cfg.rows * dest, 0, max(0, self.cfg.rows - size))


def one_hot(positions, limit):
    columns = lax.broadcasted_iota(jnp.int32, (positions.shape[0], limit), 1)
    return jnp.where(columns == positions, 1.0, 0.0).astype(BF16)


def row_ids(count):
    return lax.broadcasted_iota(jnp.int32, (count, 1), 0)


def gather_and_attend(counts, tokens, cotangent, small, halves, cfg):
    n_t, n_p, ni, hc, hh, f2, pd, imgs, m = (
        cfg.n_t, cfg.n_p, cfg.ni, cfg.hc, cfg.hh, cfg.f2, cfg.pd, cfg.imgs, cfg.m,
    )
    n_dev = 2 * n_p * n_t
    piece = D // n_dev
    caps = list(cfg.caps.items())
    widest = max(size for _, size in caps)

    def kernel(
        counts_ref, tok_ref, ct_ref, small_ref, half_ref,
        x_ref, cot_ref, in_ref, qkv_ref, att_ref, lse_ref, out_ref, vec_ref, fc1_ref, g0_ref, g_ref,
        w, sent, got, parts, q_bias, v_bias,
        z_send, z_recv, p_send, p_recv, r_send, r_recv, c_send, c_recv, v_send, v_recv, own_sem, out_sem,
    ):
        p, core, z = (lax.axis_index(axis) for axis in ALL)
        layout = Layout(counts_ref, cfg)
        pair = {"c": 1 - core}

        def part_rows(plane, member):
            return pl.ds(pl.multiple_of((plane * 2 + member) * pd, 16), pd)

        def place(group, k, mask):
            rows = pl.ds(pl.multiple_of((p ^ mask) * 2 * pd, 16), 2 * pd)
            return w.at[k, rows, :] if group == 0 else g_ref.at[:, k, rows, :]

        def half(group, member):
            return half_ref.at[member, 0] if group == 0 else half_ref.at[member, pl.ds(1, 2)]

        def half_place(group):
            rows = part_rows(p, core)
            return w.at[0, rows, :] if group == 0 else g_ref.at[:, 0, rows, :]

        def keep(group):
            return pltpu.make_async_copy(half(group, core), half_place(group), own_sem.at[group])

        def trade(group):
            return remote(half(group, 1 - core), half_place(group), (c_send, c_recv), group, pair)

        def z_copy(group, k):
            target = {"t": lax.rem(z + 1, n_t)}
            return remote(place(group, k - 1, 0), place(group, k, 0), (z_send, z_recv), (group, k), target)

        def p_copy(group, k, mask):
            ref = place(group, k, 0)
            return remote(ref, ref, (p_send, p_recv), (group, k, mask), {"p": p ^ mask})

        def d_copies(group, k):
            if n_p != 4:
                return []

            def rows(mask):
                return pl.ds(pl.multiple_of((p ^ mask) * 2 * pd, 16), 2 * pd)

            if group == 0:
                via = 1 + k % 2
                ref = w.at[k, rows(via), :]
                return [remote(ref, ref, (p_send, p_recv), (group, k, 3), {"p": p ^ (3 - via)})]
            ref_1, ref_2 = g_ref.at[0, k, rows(1), :], g_ref.at[1, k, rows(2), :]
            return [
                remote(ref_1, ref_1, (p_send, p_recv), (group, k, 3), {"p": p ^ 2}),
                remote(ref_2, ref_2, (p_send, p_recv), (group, k, 0), {"p": p ^ 1}),
            ]

        direct = (1, 2) if n_p == 4 else tuple(range(1, n_p))

        def have_own(group):
            keep(group).wait()
            trade(group).wait()

        def send_p(group, k):
            if k > 0:
                z_copy(group, k).wait_recv()
            if k + 1 < n_t:
                z_copy(group, k + 1).start()
            for mask in direct:
                p_copy(group, k, mask).start()

        def send_d(group, k):
            for mask in direct:
                p_copy(group, k, mask).wait_recv()
            for copy in d_copies(group, k):
                copy.start()

        def finish(group):
            for k in range(n_t):
                for copy in d_copies(group, k):
                    copy.wait_recv()
                    copy.wait_send()
                for mask in direct:
                    p_copy(group, k, mask).wait_send()
                if k > 0:
                    z_copy(group, k).wait_send()

        def row_copy(which, s):
            shift, size = caps[s]
            rows = pl.ds(0, size)
            return remote(
                sent.at[which, s, rows], got.at[which, s, rows], (r_send, r_recv), (which, s),
                {"t": jnp.clip(z + shift, 0, n_t - 1)},
            )

        def send_rows(which, block_ref):
            for s, (shift, size) in enumerate(caps):

                @pl.when(layout.has(z + shift))
                def _(s=s, shift=shift, size=size):
                    begin = layout.window(z, z + shift, size)
                    picked = dot(one_hot(begin + row_ids(size), cfg.block), block_ref[...])
                    sent[which, s, :size] = picked.astype(BF16)
                    row_copy(which, s).start()

        def take_rows(which, block_ref, images_ref):
            for i in range(imgs):
                row = row_ids(PT)
                position = cfg.rows * z + i * TOK_IMG + row
                valid = row < TOK_IMG
                mine = valid & (position < layout.end(z))
                spots = jnp.where(mine, position - layout.start(z), -1)
                images_ref[i] = dot(one_hot(spots, cfg.block), block_ref[...]).astype(BF16)
            for s, (shift, size) in enumerate(caps):
                source = z - shift

                @pl.when(layout.has(source))
                def _(s=s, size=size, source=source):
                    row_copy(which, s).wait_recv()
                    for i in range(imgs):
                        row = row_ids(PT)
                        position = cfg.rows * z + i * TOK_IMG + row
                        mine = (row < TOK_IMG) & (position < layout.end(source))
                        mine = mine & (position >= layout.start(source))
                        spots = position - layout.start(source) - layout.window(source, z, size)
                        picked = dot(one_hot(jnp.where(mine, spots, -1), size), got[which, s, :size])
                        images_ref[i] += picked.astype(BF16)

                @pl.when(layout.has(z + shift))
                def _(s=s):
                    row_copy(which, s).wait_send()

        def pair_rows(which, images_ref):
            mine, other = pl.ds(0, imgs), pl.ds(imgs, imgs)
            return remote(images_ref.at[mine], images_ref.at[other], (c_send, c_recv), 2 + which, pair)

        device = (2 * p + core) * n_t + z

        def part_copies(stage):
            if stage == 0:
                ref = parts.at[device]
                targets = [(k, {"t": lax.rem(z + k, n_t)}) for k in range(1, n_t)]
            elif stage == 1:
                ref = parts.at[pl.ds((2 * p + core) * n_t, n_t)]
                targets = [(n_t, pair)]
            else:
                ref = parts.at[pl.ds(2 * p * n_t, 2 * n_t)]
                targets = [(n_t + mask, {"p": p ^ mask}) for mask in range(1, n_p)]
            return [remote(ref, ref, (v_send, v_recv), index, target) for index, target in targets]

        def part_stage(stage):
            if stage > 0:
                for copy in part_copies(stage - 1):
                    copy.wait()
            if stage < 3:
                for copy in part_copies(stage):
                    copy.start()

        def spread():
            for d in range(n_dev):
                vec_ref[:, d * piece : (d + 1) * piece] = parts[d, :8, :piece]
            for k in range(n_t):
                block = 2 * lax.rem(z - k + n_t, n_t) + core
                for j in range(hc // piece):
                    cols = slice(j * piece, (j + 1) * piece)
                    owner = block * (hc // piece) + j
                    q_bias[k : k + 1, cols] = parts[owner, 4:5, :piece]
                    v_bias[k : k + 1, cols] = parts[owner, 5:6, :piece]
                for j in range(f2 // (4 * piece)):
                    owner = block * (f2 // (4 * piece)) + j
                    for r in range(4):
                        begin = (4 * j + r) * piece
                        fc1_ref[k : k + 1, begin : begin + piece] = parts[owner, 8 + r : 9 + r, :piece]

        for group in range(2):
            keep(group).start()
        parts[device] = small_ref[...]
        enter(cfg)
        for group in range(2):
            trade(group).start()
        part_stage(0)
        send_rows(0, tok_ref)
        have_own(0)
        send_p(0, 0)
        part_stage(1)
        send_rows(1, ct_ref)
        part_stage(2)
        send_p(0, 1)
        send_d(0, 0)
        take_rows(0, tok_ref, x_ref)
        pair_rows(0, x_ref).start()
        have_own(1)
        part_stage(3)
        spread()
        for k in range(2, n_t):
            send_p(0, k)
            send_d(0, k - 1)
        send_p(1, 0)
        take_rows(1, ct_ref, cot_ref)
        pair_rows(1, cot_ref).start()
        send_d(0, n_t - 1)
        pair_rows(0, x_ref).wait()
        finish(0)
        kept = pltpu.make_async_copy(w, g0_ref, out_sem)
        kept.start()

        steps = []
        for k in range(1, n_t):
            steps += [lambda k=k: send_p(1, k), lambda k=k: send_d(1, k - 1)]
        steps.append(lambda: send_d(1, n_t - 1))
        early = 2 * len(steps) // 5
        keyed = lax.broadcasted_iota(jnp.int32, (PT, PT), 1) < TOK_IMG

        def image(i, carry):
            normed, _ = norm(x_ref[i].astype(F32))
            attn_in = (normed * vec_ref[0:1, :] + vec_ref[2:3, :]).astype(BF16)
            in_ref[i] = attn_in
            for k in range(n_t):
                qkv = dot(attn_in, w[k, :, : 3 * hc])
                query = (qkv[:, :hc] + q_bias[k : k + 1, :]).astype(BF16)
                keys = qkv[:, hc : 2 * hc].astype(BF16)
                values = (qkv[:, 2 * hc :] + v_bias[k : k + 1, :]).astype(BF16)
                qkv_ref[k, i, :, :hc] = query
                qkv_ref[k, i, :, hc : 2 * hc] = keys
                qkv_ref[k, i, :, 2 * hc :] = values
                for h in range(hh):
                    cols = slice(h * HD, (h + 1) * HD)
                    scores = dot_nt(query[:, cols], keys[:, cols]) * (HD**-0.5)
                    scores = jnp.where(keyed, scores, NEG)
                    top = jnp.max(scores, axis=-1, keepdims=True)
                    expo = jnp.exp(scores - top)
                    summed = jnp.sum(expo, axis=-1, keepdims=True)
                    probs = (expo / summed).astype(BF16)
                    att_ref[k, i, :, cols] = dot(probs, values[:, cols]).astype(BF16)
                    lse_ref[k, i, :, h : h + 1] = top + jnp.log(summed)
                part = dot_nt(att_ref[k, i], w[k, :, 3 * hc :])
                if k == 0:
                    out_ref[i] = part
                else:
                    out_ref[i] += part
            for j in range(early):

                @pl.when(i == (j + 1) * ni // early - 1)
                def _(j=j):
                    steps[j]()

            return carry

        lax.fori_loop(0, ni, image, 0)
        pair_rows(1, cot_ref).wait()
        for step in steps[early:]:
            step()
        finish(1)
        kept.wait()

    vmem = pl.BlockSpec(memory_space=pltpu.VMEM)
    smem = pl.BlockSpec(memory_space=pltpu.SMEM)
    anywhere = pl.BlockSpec(memory_space=pl.ANY)
    dma = pltpu.SemaphoreType.DMA
    return pl.pallas_call(
        kernel,
        in_specs=[smem, vmem, vmem, vmem, anywhere],
        out_specs=[vmem] * 9 + [anywhere] * 2,
        out_shape=[
            jax.ShapeDtypeStruct((ni, PT, D), BF16),
            jax.ShapeDtypeStruct((ni, PT, D), BF16),
            jax.ShapeDtypeStruct((ni, PT, D), BF16),
            jax.ShapeDtypeStruct((n_t, ni, PT, 3 * hc), BF16),
            jax.ShapeDtypeStruct((n_t, ni, PT, hc), BF16),
            jax.ShapeDtypeStruct((n_t, ni, PT, hh), F32),
            jax.ShapeDtypeStruct((ni, PT, D), F32),
            jax.ShapeDtypeStruct((8, D), F32),
            jax.ShapeDtypeStruct((n_t, f2), F32),
            jax.ShapeDtypeStruct((n_t, D, f2), BF16),
            jax.ShapeDtypeStruct((2, n_t, D, f2), BF16),
        ],
        scratch_shapes=[
            pltpu.VMEM((n_t, D, f2), BF16),
            pltpu.VMEM((2, len(caps), widest, D), BF16),
            pltpu.VMEM((2, len(caps), widest, D), BF16),
            pltpu.VMEM((n_dev, 16, 128), F32),
            pltpu.VMEM((n_t, hc), F32),
            pltpu.VMEM((n_t, hc), F32),
            dma((2, n_t)),
            dma((2, n_t)),
            dma((2, n_t, n_p)),
            dma((2, n_t, n_p)),
            dma((2, len(caps))),
            dma((2, len(caps))),
            dma((4,)),
            dma((4,)),
            dma((n_t + n_p,)),
            dma((n_t + n_p,)),
            dma((2,)),
            dma,
        ],
        compiler_params=params(collective_id=0, has_side_effects=True),
        cost_estimate=pl.CostEstimate(
            flops=2 * m * D * f2 * n_t,
            bytes_accessed=2 * n_t * D * f2 + 12 * m * D,
            transcendentals=m * PT * n_t * hh,
        ),
        name="gather_and_attend",
    )(counts, tokens, cotangent, small, halves)


def reduce_and_attend_back(
    counts, grad_hidden, attn_in, qkv, attended, lse, weights, mlp_grads, residual, x, mixed, vectors, sums, fc1_sums, cfg
):
    n_t, n_p, ni, hc, hh, f2, pd, m, imgs = (
        cfg.n_t, cfg.n_p, cfg.ni, cfg.hc, cfg.hh, cfg.f2, cfg.pd, cfg.m, cfg.imgs,
    )
    scale = HD**-0.5
    square = n_p == 4
    plane = (2, 2) if square else (n_p,)
    jobs = [((k, k), k) for k in range(n_t)] + [((k, k + 1), None) for k in range(0, n_t, 2)]
    n_jobs = len(jobs)
    n_got = 2 if square else n_p - 1
    n_dev = 2 * n_p * n_t
    width = D // n_dev
    caps = list(cfg.caps.items())
    widest = max(size for _, size in caps)
    to_z = {}
    for n, (chunks, _) in enumerate(jobs):
        for part in range(2):
            if chunks[part] > 0:
                to_z[n, part] = len(to_z)

    def kernel(
        counts_ref, gh_ref, in_ref, qkv_ref, att_ref, lse_ref, w_ref, g_ref, res_ref, x_ref, mix_ref, vec_ref,
        sums_ref, fsum_ref,
        half_ref, mixed_ref, dtok_ref, small_ref, own_grads, rows_got, in_other, got_z,
        gqkv, stage, held, got, got_2, total, out, dq, dv,
        images, sent, taken, block, res_in, other_in, parts, parts_p, parts_c, parts_t,
        stage_sem, held_sem, s_send, s_recv, t_send, t_recv, z_send, z_recv, r_send, r_recv, c_send, c_recv,
        v_send, v_recv, in_sem, out_sem,
    ):
        p, core, z = (lax.axis_index(axis) for axis in ALL)
        py, px = p >> 1, p & 1
        pair = {"c": 1 - core}
        step = pl.program_id(0)
        layout = Layout(counts_ref, cfg)

        def pieces(n, part, *index):
            (chunks, k) = jobs[n]
            if k is None:
                return own_grads.at[(chunks[part], *index)]
            return g_ref.at[(*index, k, part)]

        def first_copies(n):
            if square:
                return [
                    remote(pieces(n, 0, slice(None), px ^ 1), got.at[n, 0], (s_send, s_recv), (n, 0, 0), {"p": p ^ 1}),
                    remote(pieces(n, 1, py ^ 1, slice(None)), got.at[n, 1], (s_send, s_recv), (n, 1, 0), {"p": p ^ 2}),
                ]
            return [
                remote(pieces(n, part, p ^ q), got.at[n, part, q - 1], (s_send, s_recv), (n, part, q - 1), {"p": p ^ q})
                for part in range(2)
                for q in range(1, n_p)
            ]

        def second_copies(n):
            if not square:
                return []
            return [
                remote(got.at[n, 0, py ^ 1], got_2.at[n, 0], (t_send, t_recv), (n, 0), {"p": p ^ 2}),
                remote(got.at[n, 1, px ^ 1], got_2.at[n, 1], (t_send, t_recv), (n, 1), {"p": p ^ 1}),
            ]

        def z_copy(n, part):
            k = jobs[n][0][part]
            source = got.at[n, part, (py, px)[part] if square else 0]
            target = {"t": lax.rem(z - k + n_t, n_t)}
            index = to_z[n, part]
            return remote(source, got_z.at[index], (z_send, z_recv), index, target)

        def loads(n):
            if square:
                sources = [pieces(n, 0, slice(None), px), pieces(n, 1, py, slice(None))]
            else:
                sources = [pieces(n, 0, p), pieces(n, 1, p)]
            return [
                pltpu.make_async_copy(
                    source, held.at[n % 2, part] if square else held.at[n % 2, part, 0], held_sem.at[n % 2, part]
                )
                for part, source in enumerate(sources)
            ]

        def begin(n):
            for copy in first_copies(n):
                copy.start()

        def fetch(n):
            for copy in loads(n):
                copy.start()

        def middle(n):
            for copy in loads(n):
                copy.wait()
            for copy in first_copies(n):
                copy.wait_recv()
            if square:
                for part, here in enumerate((py, px)):
                    there = here ^ 1
                    both = held[n % 2, part, there].astype(F32) + got[n, part, there].astype(F32)
                    got[n, part, there] = both.astype(BF16)
                for copy in second_copies(n):
                    copy.start()

        def last(n):
            for copy in second_copies(n):
                copy.wait_recv()
            chunks, k = jobs[n]
            for part, here in enumerate((py, px)):
                if square:
                    whole = held[n % 2, part, here].astype(F32) + got[n, part, here].astype(F32)
                    whole = whole + got_2[n, part].astype(F32)
                else:
                    whole = held[n % 2, part, 0].astype(F32)
                    for q in range(n_p - 1):
                        whole = whole + got[n, part, q].astype(F32)
                if chunks[part] == 0:
                    total[0 if k is None else 1 + part] = whole
                else:
                    got[n, part, here if square else 0] = whole.astype(BF16)
                    z_copy(n, part).start()

        def tick(n):
            middle(n)
            if n > 0:
                last(n - 1)
                if n + 1 < n_jobs:
                    fetch(n + 1)
            if n + 2 < n_jobs:
                begin(n + 2)

        def stage_copy(k):
            return pltpu.make_async_copy(stage, own_grads.at[k], stage_sem)

        def finish():
            last(n_jobs - 1)
            for n in range(n_jobs):
                for copy in first_copies(n) + second_copies(n):
                    copy.wait_send()
                for part in range(2):
                    if (n, part) in to_z:
                        z_copy(n, part).wait()
            reads = [
                pltpu.make_async_copy(got_z.at[index], got.at[n, part, 0], z_recv.at[index])
                for (n, part), index in to_z.items()
            ]
            for read in reads:
                read.start()
            for read in reads:
                read.wait()
            for unit in range(3):
                whole = total[unit]
                for n, part in to_z:
                    if unit == (0 if jobs[n][1] is None else 1 + part):
                        whole = whole + got[n, part, 0].astype(F32)
                total[unit] = whole

            def rows(member):
                return total.at[:, pl.ds(pl.multiple_of(member * pd, 16), pd), :]

            kept = pltpu.make_async_copy(rows(core), half_ref.at[core], out_sem)
            traded = remote(rows(1 - core), half_ref.at[core], (c_send, c_recv), 1, pair)
            kept.start()
            traded.start()
            kept.wait()
            traded.wait()

        def row_copy(which, s):
            shift, size = caps[s]
            return remote(
                sent.at[s, pl.ds(0, size)], rows_got.at[which, s, pl.ds(0, size)], (r_send, r_recv), (which, s),
                {"t": jnp.clip(z - shift, 0, n_t - 1)},
            )

        def of_images(positions, valid):
            rows = None
            for i in range(imgs):
                spots = positions - i * TOK_IMG
                spots = jnp.where(valid & (spots >= 0) & (spots < TOK_IMG), spots, -1)
                picked = dot(one_hot(spots, PT), images[i])
                rows = picked if rows is None else rows + picked
            return rows.astype(BF16)

        def send_rows(which):
            for s, (shift, size) in enumerate(caps):

                @pl.when(layout.has(z - shift))
                def _(s=s, shift=shift, size=size):
                    want = layout.window_back(z, z - shift, size) + row_ids(size)
                    sent[s, :size] = of_images(want, want >= 0)
                    row_copy(which, s).start()

        def take_rows(which, target):
            row = row_ids(cfg.block)
            position = layout.start(z) + row
            valid = position < layout.end(z)
            block[...] = of_images(position - cfg.rows * z, valid)
            for s, (shift, size) in enumerate(caps):
                source = z + shift

                @pl.when(layout.has(source))
                def _(s=s, size=size, source=source):
                    row_copy(which, s).wait_recv()
                    load = pltpu.make_async_copy(
                        rows_got.at[which, s, pl.ds(0, size)], taken.at[pl.ds(0, size)], in_sem.at[0]
                    )
                    load.start()
                    load.wait()
                    local = position - cfg.rows * source
                    mine = valid & (local >= 0) & (local < cfg.rows)
                    spots = jnp.where(mine, local - layout.window_back(source, z, size), -1)
                    block[...] += dot(one_hot(spots, size), taken[:size]).astype(BF16)

                @pl.when(layout.has(z - shift))
                def _(s=s):
                    row_copy(which, s).wait_send()

            store = pltpu.make_async_copy(block, target, in_sem.at[0])
            store.start()
            store.wait()

        device = (2 * p + core) * n_t + z

        def gather_parts(gain, shift):
            parts[...] = jnp.zeros_like(parts)
            rows = [gain, sums_ref[0:1, :], shift, sums_ref[1:2, :], sums_ref[2:3, :], sums_ref[3:4, :]]
            for d in range(n_dev):
                cols = slice(d * width, (d + 1) * width)
                for r, value in zip((0, 1, 2, 3, 6, 7), rows):
                    parts[d, r : r + 1, :width] = value[:, cols]
            for k in range(n_t):
                chunk = 2 * lax.rem(z - k + n_t, n_t) + core
                for j in range(hc // width):
                    cols = slice(j * width, (j + 1) * width)
                    owner = chunk * (hc // width) + j
                    parts[owner, 4:5, :width] = dq[k : k + 1, cols]
                    parts[owner, 5:6, :width] = dv[k : k + 1, cols]
                for j in range(f2 // (4 * width)):
                    owner = chunk * (f2 // (4 * width)) + j
                    for r in range(4):
                        begin_at = (4 * j + r) * width
                        parts[owner, 8 + r : 9 + r, :width] = fsum_ref[k, :, begin_at : begin_at + width]

        def plane_parts(index):
            return pl.ds(2 * index * n_t, 2 * n_t)

        def core_parts(member):
            return pl.ds((2 * p + member) * n_t, n_t)

        def part_copies(hop):
            if hop == 0:
                return [
                    remote(parts.at[plane_parts(p ^ q)], parts_p.at[q - 1], (v_send, v_recv), q - 1, {"p": p ^ q})
                    for q in range(1, n_p)
                ]
            if hop == 1:
                return [remote(parts.at[core_parts(1 - core)], parts_c, (v_send, v_recv), n_p - 1, pair)]
            copies = []
            for k in range(1, n_t):
                to = lax.rem(z + k, n_t)
                source = parts.at[(2 * p + core) * n_t + to]
                copies.append(remote(source, parts_t.at[k], (v_send, v_recv), n_p - 1 + k, {"t": to}))
            return copies

        def part_hop(hop):
            if hop > 0:
                for copy in part_copies(hop - 1):
                    copy.wait()
            if hop == 1:
                for q in range(n_p - 1):
                    parts[plane_parts(p)] += parts_p[q]
            if hop == 2:
                parts[core_parts(core)] += parts_c[...]
            if hop == 3:
                mine = parts[device]
                for k in range(1, n_t):
                    mine = mine + parts_t[k]
                small_ref[...] = mine
            if hop < 3:
                for copy in part_copies(hop):
                    copy.start()

        def in_copy():
            return remote(out.at[pl.ds(imgs, imgs)], in_other, (c_send, c_recv), 0, pair)

        def first_norm_back():
            in_copy().wait()
            gain, shift = jnp.zeros((1, D), F32), jnp.zeros((1, D), F32)
            for i in range(imgs):
                reads = [
                    pltpu.make_async_copy(res_ref.at[i], res_in, in_sem.at[0]),
                    pltpu.make_async_copy(in_other.at[i], other_in, in_sem.at[1]),
                    pltpu.make_async_copy(x_ref.at[i], taken.at[pl.ds(0, PT)], in_sem.at[2]),
                ]
                for read in reads:
                    read.start()
                for read in reads:
                    read.wait()
                up = out[i] + other_in[...]
                normed, inverse = norm(taken[:PT].astype(F32))
                grad = res_in[...] + norm_back(up, normed, inverse, vec_ref[0:1, :])
                images[i] = grad.astype(BF16)
                gain = gain + jnp.sum(up * normed, axis=0, keepdims=True)
                shift = shift + jnp.sum(up, axis=0, keepdims=True)
            gather_parts(gain, shift)

        @pl.when(step == 0)
        def _():
            fetch(0)
            fetch(1)
            read = pltpu.make_async_copy(mix_ref, images, in_sem.at[0])
            read.start()
            enter(cfg)
            begin(0)
            begin(1)
            read.wait()
            send_rows(0)

        keyed = lax.broadcasted_iota(jnp.int32, (PT, PT), 1) < TOK_IMG
        total_q, total_v = jnp.zeros((1, hc), F32), jnp.zeros((1, hc), F32)
        for i in range(ni):
            grad_att = dot(gh_ref[i], w_ref[0, :, 3 * hc :]).astype(BF16)
            sums_q, sums_v = [], []
            for h in range(hh):
                cols = slice(h * HD, (h + 1) * HD)
                key_cols = slice(hc + h * HD, hc + (h + 1) * HD)
                value_cols = slice(2 * hc + h * HD, 2 * hc + (h + 1) * HD)
                query = qkv_ref[0, i, :, cols]
                keys = qkv_ref[0, i, :, key_cols]
                values = qkv_ref[0, i, :, value_cols]
                grad = grad_att[:, cols]
                scores = dot_nt(query, keys) * scale - lse_ref[0, i, :, h : h + 1]
                probs = jnp.exp(jnp.where(keyed, scores, NEG))
                delta = jnp.sum(
                    grad.astype(F32) * att_ref[0, i, :, cols].astype(F32), axis=-1, keepdims=True
                )
                grad_v = dot_tn(probs.astype(BF16), grad)
                grad_s = (probs * (dot_nt(grad, values) - delta) * scale).astype(BF16)
                grad_q = dot(grad_s, keys)
                grad_k = dot_tn(grad_s, query)
                sums_q.append(jnp.sum(grad_q, axis=0, keepdims=True))
                sums_v.append(jnp.sum(grad_v, axis=0, keepdims=True))
                gqkv[i, :, cols] = grad_q.astype(BF16)
                gqkv[i, :, key_cols] = grad_k.astype(BF16)
                gqkv[i, :, value_cols] = grad_v.astype(BF16)
            total_q = total_q + jnp.concatenate(sums_q, axis=1)
            total_v = total_v + jnp.concatenate(sums_v, axis=1)
            part = dot_nt(gqkv[i], w_ref[0, :, : 3 * hc])

            @pl.when(step == 0)
            def _(i=i, part=part):
                out[i] = part

            @pl.when(step > 0)
            def _(i=i, part=part):
                out[i] += part

            for n in range(n_t - 2):
                if i == min(2 * n + 1, ni - 1):

                    @pl.when(step == n + 1)
                    def _(n=n):
                        tick(n)

        dq[pl.ds(step, 1), :] = total_q
        dv[pl.ds(step, 1), :] = total_v

        @pl.when(step == n_t - 1)
        def _():
            in_copy().start()

        left = dot_tn(in_ref[...].reshape(m, D), gqkv[...].reshape(m, 3 * hc)).astype(BF16)
        right = dot_tn(gh_ref[...].reshape(m, D), att_ref[0].reshape(m, hc)).astype(BF16)

        @pl.when(step > 0)
        def _():
            stage_copy(0).wait()

        ahead = [slice(None)] * (len(plane) + 1)
        stage[(*ahead, slice(0, 3 * hc))] = left.reshape((*plane, 2 * pd, 3 * hc))
        stage[(*ahead, slice(3 * hc, f2))] = right.reshape((*plane, 2 * pd, hc))
        for k in range(n_t):

            @pl.when(step == k)
            def _(k=k):
                stage_copy(k).start()

        @pl.when(step == n_t - 2)
        def _():
            take_rows(0, mixed_ref)

        @pl.when(step == n_t - 1)
        def _():
            stage_copy(0).wait()
            tick(n_t - 2)
            first_norm_back()
            send_rows(1)
            part_hop(0)
            tick(n_t - 1)
            part_hop(1)
            for n in range(n_t, n_jobs - 1):
                tick(n)
            part_hop(2)
            take_rows(1, dtok_ref)
            tick(n_jobs - 1)
            part_hop(3)
            finish()

    dma = pltpu.SemaphoreType.DMA
    chunk = (2 * pd, f2)
    vmem = pltpu.VMEM

    def chunk_block(last):
        return pl.BlockSpec((1, ni, PT, last), lambda k: (k, 0, 0, 0))

    anywhere = pl.BlockSpec(memory_space=pl.ANY)
    shape = jax.ShapeDtypeStruct
    n_v = n_p - 1 + n_t
    outs = pl.pallas_call(
        kernel,
        grid=(n_t,),
        in_specs=[
            pl.BlockSpec(memory_space=pltpu.SMEM),
            fixed((ni, PT, D)),
            fixed((ni, PT, D)),
            chunk_block(3 * hc),
            chunk_block(hc),
            chunk_block(hh),
            pl.BlockSpec((1, D, f2), lambda k: (k, 0, 0)),
            anywhere,
            anywhere,
            anywhere,
            anywhere,
            fixed((8, D)),
            fixed((4, D)),
            fixed((n_t, 1, f2)),
        ],
        out_specs=[anywhere] * 3 + [fixed((16, 128))] + [anywhere] * 4,
        out_shape=[
            shape((2, 3, pd, f2), F32),
            shape((cfg.block, D), BF16),
            shape((cfg.block, D), BF16),
            shape((16, 128), F32),
            shape((n_t, *plane, *chunk), BF16),
            shape((2, len(caps), widest, D), BF16),
            shape((imgs, PT, D), F32),
            shape((len(to_z), *chunk), BF16),
        ],
        scratch_shapes=[
            vmem((ni, PT, 3 * hc), BF16),
            vmem((*plane, *chunk), BF16),
            vmem((2, 2, 2 if square else 1, *chunk), BF16),
            vmem((n_jobs, 2, n_got, *chunk), BF16),
            vmem((n_jobs, 2, *(chunk if square else (16, 128))), BF16),
            vmem((3, *chunk), F32),
            vmem((ni, PT, D), F32),
            vmem((n_t, hc), F32),
            vmem((n_t, hc), F32),
            vmem((imgs, PT, D), BF16),
            vmem((len(caps), widest, D), BF16),
            vmem((max(widest, PT), D), BF16),
            vmem((cfg.block, D), BF16),
            vmem((PT, D), F32),
            vmem((PT, D), F32),
            vmem((n_dev, 16, 128), F32),
            vmem((n_p - 1, 2 * n_t, 16, 128), F32),
            vmem((n_t, 16, 128), F32),
            vmem((n_t, 16, 128), F32),
            dma,
            dma((2, 2)),
            dma((n_jobs, 2, 1 if square else n_p - 1)),
            dma((n_jobs, 2, 1 if square else n_p - 1)),
            dma((n_jobs, 2)),
            dma((n_jobs, 2)),
            dma((len(to_z),)),
            dma((len(to_z),)),
            dma((2, len(caps))),
            dma((2, len(caps))),
            dma((2,)),
            dma((2,)),
            dma((n_v,)),
            dma((n_v,)),
            dma((3,)),
            dma,
        ],
        compiler_params=params(collective_id=1, has_side_effects=True),
        cost_estimate=pl.CostEstimate(
            flops=4 * m * D * f2 * n_t + 10 * m * PT * HD * n_t * hh,
            bytes_accessed=4 * n_t * D * f2 + 20 * m * D,
            transcendentals=m * PT * n_t * hh,
        ),
        name="reduce_and_attend_back",
    )(
        counts,
        grad_hidden,
        attn_in,
        qkv,
        attended,
        lse,
        weights,
        mlp_grads.reshape((*plane, n_t, 2, *chunk)),
        residual,
        x,
        mixed,
        vectors,
        sums,
        fc1_sums,
    )
    return outs[:4]


def mlp_pass(x, attn_out, vectors, cot, fc1, weights, cfg):
    n_p, n_t, m, pd, w, ni, imgs = cfg.n_p, cfg.n_t, cfg.m, cfg.pd, cfg.f2, cfg.ni, cfg.imgs

    def kernel(
        x_ref, outs_ref, vec_ref, cot_ref, fc1_ref, w1_ref, w2_ref,
        sum_ref, grad_ref, res_ref, gh_ref, sums_ref, mixed_ref,
        other, other_y, mlp_in, act_all, gpre_all, back, y, gh, c_send, c_recv, own_sem,
    ):
        step = pl.program_id(0)
        pair = {"c": 1 - lax.axis_index("c")}
        mine, theirs = pl.ds(0, imgs), pl.ds(imgs, imgs)

        def pair_copy(index, source, target):
            return remote(source, target, (c_send, c_recv), index, pair)

        def back_copy():
            return pair_copy(2, back.at[theirs], other)

        def y_copy():
            return pair_copy(3, y.at[theirs], other_y)

        @pl.when(step == 0)
        def _():
            own_part = pltpu.make_async_copy(outs_ref.at[mine], res_ref, own_sem)
            own_part.start()
            greet_pair()
            out_copy = pair_copy(0, outs_ref.at[theirs], other)
            out_copy.start()
            own_part.wait()
            out_copy.wait()
            for i in range(imgs):
                value = x_ref[i].astype(F32) + (res_ref[i] + other[i]) + vec_ref[6:7, :]
                res_ref[i] = value
                normed, _ = norm(value)
                mlp_in[i] = (normed * vec_ref[1:2, :] + vec_ref[3:4, :]).astype(BF16)
            in_copy = pair_copy(1, mlp_in.at[mine], mlp_in.at[theirs])
            in_copy.start()
            in_copy.wait()

        w1, w2 = w1_ref[0, 0], w2_ref[0, 0]
        total = jnp.zeros((1, w), F32)
        for i in range(ni):
            rows = slice(i * PT, (i + 1) * PT)
            pre = dot(mlp_in[i], w1) + fc1_ref[0]
            phi = 0.5 * (1.0 + lax.erf(pre * (1.0 / math.sqrt(2.0))))
            act_all[rows, :] = (pre * phi).astype(BF16)
            slope = phi + pre * jnp.exp(-0.5 * pre * pre) * (1.0 / math.sqrt(2.0 * math.pi))
            gpre = dot(cot_ref[i], w2) * slope
            total = total + jnp.sum(gpre, axis=0, keepdims=True)
            gpre_all[rows, :] = gpre.astype(BF16)
        sum_ref[0] = total

        def add(target, left, right):
            value = dot_nt(left, right).reshape(ni, PT, D)

            @pl.when(step == 0)
            def _():
                target[...] = value

            @pl.when(step > 0)
            def _():
                target[...] += value

        add(back, gpre_all[...], w1)

        @pl.when(step == n_t - 1)
        def _():
            back_copy().start()

        add(y, act_all[...], w2)

        @pl.when(step == n_t - 1)
        def _():
            y_copy().start()

        grad_1 = dot_tn(mlp_in[...].reshape(m, D), gpre_all[...]).astype(BF16)
        grad_ref[:, 0, 0] = grad_1.reshape(n_p, 2 * pd, w)
        grad_2 = dot_tn(cot_ref[...].reshape(m, D), act_all[...]).astype(BF16)
        grad_ref[:, 0, 1] = grad_2.reshape(n_p, 2 * pd, w)

        @pl.when(step == n_t - 1)
        def _():
            back_copy().wait()
            sums = [jnp.zeros((1, D), F32)] * 4
            for i in range(imgs):
                up = back[i] + other[i]
                hidden = res_ref[i]
                other[i] = hidden
                normed, inverse = norm(hidden)
                cot_f = cot_ref[i].astype(F32)
                grad = cot_f + norm_back(up, normed, inverse, vec_ref[1:2, :])
                res_ref[i] = grad
                gh[i] = grad.astype(BF16)
                terms = (up * normed, up, grad, cot_f)
                sums = [s + jnp.sum(t, axis=0, keepdims=True) for s, t in zip(sums, terms)]
            grad_copy = pair_copy(4, gh.at[mine], gh.at[theirs])
            grad_copy.start()
            for r in range(4):
                sums_ref[r : r + 1, :] = sums[r]
            y_copy().wait()
            for i in range(imgs):
                mixed_ref[i] = (other[i] + (y[i] + other_y[i]) + vec_ref[7:8, :]).astype(BF16)
            grad_copy.wait()
            store = pltpu.make_async_copy(gh, gh_ref, own_sem)
            store.start()
            store.wait()

    def half_spec(unit):
        return pl.BlockSpec((1, 1, D, w), lambda i: (unit, i, 0, 0))

    full = fixed((ni, PT, D))
    own = fixed((imgs, PT, D))
    shape, vmem, dma = jax.ShapeDtypeStruct, pltpu.VMEM, pltpu.SemaphoreType.DMA
    return pl.pallas_call(
        kernel,
        grid=(n_t,),
        in_specs=[
            own,
            pl.BlockSpec(memory_space=pl.ANY),
            fixed((8, D)),
            full,
            pl.BlockSpec((1, 1, w), lambda i: (i, 0, 0)),
            half_spec(0),
            half_spec(1),
        ],
        out_specs=[
            pl.BlockSpec((1, 1, w), lambda i: (i, 0, 0)),
            pl.BlockSpec((n_p, 1, 2, 2 * pd, w), lambda i: (0, i, 0, 0, 0)),
            own,
            pl.BlockSpec(memory_space=pl.ANY),
            fixed((4, D)),
            own,
        ],
        out_shape=[
            shape((n_t, 1, w), F32),
            shape((n_p, n_t, 2, 2 * pd, w), BF16),
            shape((imgs, PT, D), F32),
            shape((ni, PT, D), BF16),
            shape((4, D), F32),
            shape((imgs, PT, D), BF16),
        ],
        scratch_shapes=[
            vmem((imgs, PT, D), F32),
            vmem((imgs, PT, D), F32),
            vmem((ni, PT, D), BF16),
            vmem((m, w), BF16),
            vmem((m, w), BF16),
            vmem((ni, PT, D), F32),
            vmem((ni, PT, D), F32),
            vmem((ni, PT, D), BF16),
            dma((5,)),
            dma((5,)),
            dma,
        ],
        compiler_params=params(collective_id=2, has_side_effects=True),
        cost_estimate=pl.CostEstimate(
            flops=12 * m * D * w * n_t,
            bytes_accessed=12 * m * D + 8 * D * w * n_t,
            transcendentals=2 * m * w * n_t,
        ),
        name="mlp_pass",
    )(x, attn_out, vectors, cot, fc1.reshape(n_t, 1, w), weights, weights)


def body(cfg, tokens, counts, gains, biases, fc1_bias, w_qkv, w_o, w_1, w_2, cotangent):
    pd, f2, hc = cfg.pd, cfg.f2, cfg.hc
    halves = jnp.stack(
        [
            jnp.concatenate(
                [
                    w_qkv.reshape(pd, 3, 2, hc).transpose(2, 0, 1, 3).reshape(2, pd, 3 * hc),
                    w_o.T.reshape(pd, 2, hc).transpose(1, 0, 2),
                ],
                axis=2,
            ),
            w_1.reshape(pd, 2, f2).transpose(1, 0, 2),
            w_2.T.reshape(pd, 2, f2).transpose(1, 0, 2),
        ],
        axis=1,
    )
    small = jnp.concatenate([gains, biases, fc1_bias.reshape(4, -1)])
    small = jnp.pad(small, ((0, 4), (0, 128 - small.shape[1])))

    x, cot, attn_in, qkv, attended, lse, attn_out, vectors, fc1, attn_w, mlp_w = gather_and_attend(
        counts, tokens, cotangent, small, halves, cfg
    )
    fc1_sums, mlp_grads, residual, grad_hidden, sums, mixed = mlp_pass(
        x, attn_out, vectors, cot, fc1, mlp_w, cfg
    )
    both, mixed, d_tokens, small = reduce_and_attend_back(
        counts, grad_hidden, attn_in, qkv, attended, lse, attn_w, mlp_grads, residual, x, mixed, vectors, sums,
        fc1_sums, cfg,
    )
    d_qkv = both[:, 0, :, : 3 * hc].reshape(2, pd, 3, hc).transpose(1, 2, 0, 3).reshape(pd, 3, 2 * hc)
    d_o = both[:, 0, :, 3 * hc :].transpose(0, 2, 1).reshape(2 * hc, pd)
    d_1 = both[:, 1].transpose(1, 0, 2).reshape(pd, 2 * f2)
    d_2 = both[:, 2].transpose(0, 2, 1).reshape(2 * f2, pd)
    piece = D // (cfg.n_dp * cfg.n_t)
    small = small[:, :piece]
    return (
        mixed,
        d_tokens,
        d_qkv,
        d_o,
        d_1,
        d_2,
        small[:2],
        small[2:8],
        small[8:12].reshape(-1),
    )


def solution(mesh):
    n_dp, n_t = mesh.shape["dp"], mesh.shape["tensor"]
    split = Mesh(mesh.devices.reshape(n_dp // 2, 2, n_t), ALL)

    def program(tokens, *rest):
        cfg = Cfg(n_dp, n_t, tokens.shape[0])
        return body(cfg, tokens, *rest)

    dp = ("p", "c")
    return jax.shard_map(
        program,
        mesh=split,
        in_specs=(
            P(ALL, None),
            P(dp, None),
            P(None, ALL),
            P(None, ALL),
            P(ALL),
            P(dp, None, "t"),
            P("t", dp),
            P(dp, "t"),
            P("t", dp),
            P(ALL, None),
        ),
        out_specs=(
            P(ALL, None),
            P(ALL, None),
            P(dp, None, "t"),
            P("t", dp),
            P(dp, "t"),
            P("t", dp),
            P(None, ALL),
            P(None, ALL),
            P(ALL),
        ),
        check_vma=False,
    )
```

```python
import math

import jax
import jax.numpy as jnp
from jax import lax
from jax.experimental import pallas as pl
from jax.experimental.pallas import tpu as pltpu
from jax.sharding import Mesh
from jax.sharding import PartitionSpec as P

D = 1280
HD = 80
HEADS = 16
FF = 5120
TOK_IMG = 257
IMG_DEV = 8
TOTAL = IMG_DEV * TOK_IMG
EPS = 1e-06
PT = 272
F32 = jnp.float32
BF16 = jnp.bfloat16
NEG = -1e30
VMEM_LIMIT = 61 * 1024 * 1024


class Cfg:
    def __init__(self, n_dp, n_t, block_rows):
        self.n_dp, self.n_t, self.block = n_dp, n_t, block_rows
        self.n_p = n_dp // 2
        self.imgs = IMG_DEV // n_t
        self.ni = 2 * self.imgs
        self.rows = self.imgs * TOK_IMG
        self.m = self.ni * PT
        self.pd = D // n_dp
        self.hh = HEADS // n_t // 2
        self.hc = self.hh * HD
        self.f2 = FF // n_t // 2
        assert 4 * self.hc == self.f2
        self.early = n_t // 2
        self.caps = self._caps()

    def _caps(self):
        n, b, r = self.n_t, self.block, self.rows
        low = [max(t, TOTAL - (n - t) * b) for t in range(n + 1)]
        high = [min(t * b, TOTAL - (n - t)) for t in range(n + 1)]
        caps = {}
        for t in range(n):
            for dest in range(n):
                size = min(high[t + 1], r * (dest + 1)) - max(low[t], r * dest)
                size = min(size, b, r)
                if size > 0 and dest != t:
                    caps[dest - t] = max(caps.get(dest - t, 0), size)
        return {s: min(-(-c // 16) * 16, b) for s, c in sorted(caps.items())}


def dot(a, b):
    return lax.dot_general(a, b, (((1,), (0,)), ((), ())), preferred_element_type=F32)


def dot_nt(a, b):
    return lax.dot_general(a, b, (((1,), (1,)), ((), ())), preferred_element_type=F32)


def dot_tn(a, b):
    return lax.dot_general(a, b, (((0,), (0,)), ((), ())), preferred_element_type=F32)


def norm(values):
    mean = jnp.mean(values, axis=-1, keepdims=True)
    centred = values - mean
    spread = jnp.mean(centred * centred, axis=-1, keepdims=True)
    inverse = lax.rsqrt(spread + EPS)
    return centred * inverse, inverse


def norm_back(upstream, normed, inverse, gain):
    scaled = upstream * gain
    return inverse * (
        scaled
        - jnp.mean(scaled, axis=-1, keepdims=True)
        - normed * jnp.mean(scaled * normed, axis=-1, keepdims=True)
    )


ALL = ("p", "c", "t")


def params(**more):
    return pltpu.CompilerParams(vmem_limit_bytes=VMEM_LIMIT, **more)


def fixed(shape):
    return pl.BlockSpec(
        shape, lambda i, *s: (0,) * len(shape), pipeline_mode=pl.Buffered(1)
    )


MESH = pl.DeviceIdType.MESH


def enter(cfg):
    p, c, t = (lax.axis_index(axis) for axis in ALL)
    found = [{"c": 1 - c}]
    found += [{"t": lax.rem(t + k, cfg.n_t)} for k in range(1, cfg.n_t)]
    found += [{"p": p ^ m} for m in range(1, cfg.n_p)]
    barrier = pltpu.get_barrier_semaphore()
    for device in found:
        pl.semaphore_signal(barrier, inc=1, device_id=device, device_id_type=MESH)
    pl.semaphore_wait(barrier, len(found))


def remote(source, target, sems, index, device):
    return pltpu.make_async_remote_copy(
        src_ref=source,
        dst_ref=target,
        send_sem=sems[0].at[index],
        recv_sem=sems[1].at[index],
        device_id=device,
        device_id_type=MESH,
    )


class Layout:
    def __init__(self, counts_ref, cfg):
        self.counts, self.cfg = counts_ref, cfg
        self.z = lax.axis_index("t")

    def start(self, block):
        total = 0
        for j in range(self.cfg.n_t):
            total = total + jnp.where(block > j, self.counts[0, j], 0)
        return total

    def end(self, block):
        return self.start(block + 1)

    def has(self, block):
        return (block >= 0) & (block < self.cfg.n_t)

    def window(self, block, dest, size):
        return jnp.clip(self.cfg.rows * dest - self.start(block), 0, self.cfg.block - size)

    def window_back(self, dest, block, size):
        return jnp.clip(self.start(block) - self.cfg.rows * dest, 0, max(0, self.cfg.rows - size))


def one_hot(positions, limit):
    columns = lax.broadcasted_iota(jnp.int32, (positions.shape[0], limit), 1)
    return jnp.where(columns == positions, 1.0, 0.0).astype(BF16)


def row_ids(count):
    return lax.broadcasted_iota(jnp.int32, (count, 1), 0)


def gather_and_attend(counts, tokens, cotangent, small, halves, cfg):
    n_t, n_p, ni, hc, hh, f2, pd, imgs, m = (
        cfg.n_t, cfg.n_p, cfg.ni, cfg.hc, cfg.hh, cfg.f2, cfg.pd, cfg.imgs, cfg.m,
    )
    n_dev = 2 * n_p * n_t
    piece = D // n_dev
    caps = list(cfg.caps.items())
    widest = max(size for _, size in caps)

    def kernel(
        counts_ref, tok_ref, ct_ref, small_ref, half_ref,
        x_out, cot_out, in_out, qkv_out, att_out, lse_out, hidden_out, mlp_out, vec_ref, fc1_ref, g0_ref, g_ref,
        x_ref, cot_ref, in_ref, qkv_ref, att_ref, lse_ref, out_ref, other, mlp_in, w, sent, got, parts, q_bias, v_bias,
        z_send, z_recv, p_send, p_recv, r_send, r_recv, c_send, c_recv, v_send, v_recv, own_sem, out_sem, image_sem,
    ):
        p, core, z = (lax.axis_index(axis) for axis in ALL)
        layout = Layout(counts_ref, cfg)
        pair = {"c": 1 - core}

        def part_rows(plane, member):
            return pl.ds(pl.multiple_of((plane * 2 + member) * pd, 16), pd)

        def place(group, k, mask):
            rows = pl.ds(pl.multiple_of((p ^ mask) * 2 * pd, 16), 2 * pd)
            return w.at[k, rows, :] if group == 0 else g_ref.at[:, k, rows, :]

        def half(group, member):
            return half_ref.at[member, 0] if group == 0 else half_ref.at[member, pl.ds(1, 2)]

        def half_place(group):
            rows = part_rows(p, core)
            return w.at[0, rows, :] if group == 0 else g_ref.at[:, 0, rows, :]

        def keep(group):
            return pltpu.make_async_copy(half(group, core), half_place(group), own_sem.at[group])

        def trade(group):
            return remote(half(group, 1 - core), half_place(group), (c_send, c_recv), group, pair)

        def z_copy(group, k):
            target = {"t": lax.rem(z + 1, n_t)}
            return remote(place(group, k - 1, 0), place(group, k, 0), (z_send, z_recv), (group, k), target)

        def p_copy(group, k, mask):
            ref = place(group, k, 0)
            return remote(ref, ref, (p_send, p_recv), (group, k, mask), {"p": p ^ mask})

        def d_copies(group, k):
            if n_p != 4:
                return []

            def rows(mask):
                return pl.ds(pl.multiple_of((p ^ mask) * 2 * pd, 16), 2 * pd)

            if group == 0:
                via = 1 + k % 2
                ref = w.at[k, rows(via), :]
                return [remote(ref, ref, (p_send, p_recv), (group, k, 3), {"p": p ^ (3 - via)})]
            ref_1, ref_2 = g_ref.at[0, k, rows(1), :], g_ref.at[1, k, rows(2), :]
            return [
                remote(ref_1, ref_1, (p_send, p_recv), (group, k, 3), {"p": p ^ 2}),
                remote(ref_2, ref_2, (p_send, p_recv), (group, k, 0), {"p": p ^ 1}),
            ]

        direct = (1, 2) if n_p == 4 else tuple(range(1, n_p))

        def have_own(group):
            keep(group).wait()
            trade(group).wait()

        def send_p(group, k):
            for mask in direct:
                p_copy(group, k, mask).start()

        def send_z(group, k):
            if k > 1:
                z_copy(group, k - 1).wait_recv()
            z_copy(group, k).start()

        def send_d(group, k):
            for mask in direct:
                p_copy(group, k, mask).wait_recv()
            for copy in d_copies(group, k):
                copy.start()

        def finish(group, chunks):
            for k in chunks:
                for copy in d_copies(group, k):
                    copy.wait_recv()
                    copy.wait_send()
                for mask in direct:
                    p_copy(group, k, mask).wait_send()
            for k in range(1, n_t if group == 0 else cfg.early + 1):
                z_copy(group, k).wait_send()

        def row_copy(which, s):
            shift, size = caps[s]
            rows = pl.ds(0, size)
            return remote(
                sent.at[which, s, rows], got.at[which, s, rows], (r_send, r_recv), (which, s),
                {"t": jnp.clip(z + shift, 0, n_t - 1)},
            )

        def send_rows(which, block_ref):
            for s, (shift, size) in enumerate(caps):

                @pl.when(layout.has(z + shift))
                def _(s=s, shift=shift, size=size):
                    begin = layout.window(z, z + shift, size)
                    picked = dot(one_hot(begin + row_ids(size), cfg.block), block_ref[...])
                    sent[which, s, :size] = picked.astype(BF16)
                    row_copy(which, s).start()

        def take_rows(which, block_ref, images_ref):
            for i in range(imgs):
                row = row_ids(PT)
                position = cfg.rows * z + i * TOK_IMG + row
                valid = row < TOK_IMG
                mine = valid & (position < layout.end(z))
                spots = jnp.where(mine, position - layout.start(z), -1)
                images_ref[i] = dot(one_hot(spots, cfg.block), block_ref[...]).astype(BF16)
            for s, (shift, size) in enumerate(caps):
                source = z - shift

                @pl.when(layout.has(source))
                def _(s=s, size=size, source=source):
                    row_copy(which, s).wait_recv()
                    for i in range(imgs):
                        row = row_ids(PT)
                        position = cfg.rows * z + i * TOK_IMG + row
                        mine = (row < TOK_IMG) & (position < layout.end(source))
                        mine = mine & (position >= layout.start(source))
                        spots = position - layout.start(source) - layout.window(source, z, size)
                        picked = dot(one_hot(jnp.where(mine, spots, -1), size), got[which, s, :size])
                        images_ref[i] += picked.astype(BF16)

                @pl.when(layout.has(z + shift))
                def _(s=s):
                    row_copy(which, s).wait_send()

        def pair_rows(which, images_ref):
            mine, other = pl.ds(0, imgs), pl.ds(imgs, imgs)
            return remote(images_ref.at[mine], images_ref.at[other], (c_send, c_recv), 2 + which, pair)

        device = (2 * p + core) * n_t + z

        def part_copies(stage):
            if stage == 0:
                ref = parts.at[device]
                targets = [(k, {"t": lax.rem(z + k, n_t)}) for k in range(1, n_t)]
            elif stage == 1:
                ref = parts.at[pl.ds((2 * p + core) * n_t, n_t)]
                targets = [(n_t, pair)]
            else:
                ref = parts.at[pl.ds(2 * p * n_t, 2 * n_t)]
                targets = [(n_t + mask, {"p": p ^ mask}) for mask in range(1, n_p)]
            return [remote(ref, ref, (v_send, v_recv), index, target) for index, target in targets]

        def part_stage(stage):
            if stage > 0:
                for copy in part_copies(stage - 1):
                    copy.wait()
            if stage < 3:
                for copy in part_copies(stage):
                    copy.start()

        def spread():
            for d in range(n_dev):
                vec_ref[:, d * piece : (d + 1) * piece] = parts[d, :8, :piece]
            for k in range(n_t):
                block = 2 * lax.rem(z - k + n_t, n_t) + core
                for j in range(hc // piece):
                    cols = slice(j * piece, (j + 1) * piece)
                    owner = block * (hc // piece) + j
                    q_bias[k : k + 1, cols] = parts[owner, 4:5, :piece]
                    v_bias[k : k + 1, cols] = parts[owner, 5:6, :piece]
                for j in range(f2 // (4 * piece)):
                    owner = block * (f2 // (4 * piece)) + j
                    for r in range(4):
                        begin = (4 * j + r) * piece
                        fc1_ref[k : k + 1, begin : begin + piece] = parts[owner, 8 + r : 9 + r, :piece]

        for group in range(2):
            keep(group).start()
        parts[device] = small_ref[...]
        enter(cfg)
        for group in range(2):
            trade(group).start()
        part_stage(0)
        send_rows(0, tok_ref)
        have_own(0)
        send_p(0, 0)
        send_z(0, 1)
        have_own(1)
        send_p(1, 0)
        part_stage(1)
        send_d(0, 0)
        part_stage(2)
        take_rows(0, tok_ref, x_ref)
        pair_rows(0, x_ref).start()
        z_last = n_t - 1
        for k in range(1, n_t):
            if k < z_last:
                send_z(0, k + 1)
            else:
                z_copy(0, k).wait_recv()
            if k == z_last - 1:
                send_z(1, 1)
            send_p(0, k)
            if k == 1:
                send_d(1, 0)
                part_stage(3)
                spread()
            else:
                send_d(0, k - 1)
        send_d(0, z_last)
        steps = []
        for k in range(1, cfg.early + 1):
            if k < cfg.early:
                steps.append(lambda k=k: send_z(1, k + 1))
                steps.append(lambda k=k: send_p(1, k))
            else:
                steps.append(lambda k=k: z_copy(1, k).wait_recv())
            if k > 1:
                steps.append(lambda k=k: send_d(1, k - 1))
        for step in steps[:2]:
            step()
        steps = steps[2:]
        send_rows(1, ct_ref)
        pair_rows(0, x_ref).wait()
        finish(0, range(n_t))
        kept = pltpu.make_async_copy(w, g0_ref, out_sem.at[0])
        kept.start()
        x_copy = pltpu.make_async_copy(x_ref, x_out, out_sem.at[1])
        x_copy.start()
        early = len(steps)

        def image_copies(i):
            return [
                pltpu.make_async_copy(in_ref.at[i], in_out.at[i], image_sem.at[0, i]),
                pltpu.make_async_copy(qkv_ref.at[:, i], qkv_out.at[:, i], image_sem.at[1, i]),
                pltpu.make_async_copy(att_ref.at[:, i], att_out.at[:, i], image_sem.at[2, i]),
                pltpu.make_async_copy(lse_ref.at[:, i], lse_out.at[:, i], image_sem.at[3, i]),
            ]

        keyed = lax.broadcasted_iota(jnp.int32, (PT, PT), 1) < TOK_IMG

        mine, theirs = pl.ds(0, imgs), pl.ds(imgs, imgs)

        def out_copy():
            return remote(out_ref.at[theirs], other, (c_send, c_recv), 4, pair)

        def image(turn, carry):
            i = lax.rem(turn + imgs, ni)
            normed, _ = norm(x_ref[i].astype(F32))
            attn_in = (normed * vec_ref[0:1, :] + vec_ref[2:3, :]).astype(BF16)
            in_ref[i] = attn_in
            for k in range(n_t):
                qkv = dot(attn_in, w[k, :, : 3 * hc])
                query = (qkv[:, :hc] + q_bias[k : k + 1, :]).astype(BF16)
                keys = qkv[:, hc : 2 * hc].astype(BF16)
                values = (qkv[:, 2 * hc :] + v_bias[k : k + 1, :]).astype(BF16)
                qkv_ref[k, i, :, :hc] = query
                qkv_ref[k, i, :, hc : 2 * hc] = keys
                qkv_ref[k, i, :, 2 * hc :] = values
                for h in range(hh):
                    cols = slice(h * HD, (h + 1) * HD)
                    scores = dot_nt(query[:, cols], keys[:, cols]) * (HD**-0.5)
                    scores = jnp.where(keyed, scores, NEG)
                    top = jnp.max(scores, axis=-1, keepdims=True)
                    expo = jnp.exp(scores - top)
                    summed = jnp.sum(expo, axis=-1, keepdims=True)
                    probs = (expo / summed).astype(BF16)
                    att_ref[k, i, :, cols] = dot(probs, values[:, cols]).astype(BF16)
                    lse_ref[k, i, :, h : h + 1] = top + jnp.log(summed)
                part = dot_nt(att_ref[k, i], w[k, :, 3 * hc :])
                if k == 0:
                    out_ref[i] = part
                else:
                    out_ref[i] += part
            for copy in image_copies(i):
                copy.start()

            @pl.when(turn == imgs - 1)
            def _():
                out_copy().start()

            for j in range(early):

                @pl.when(turn == min(j, ni - 1))
                def _(j=j):
                    steps[j]()

            return carry

        lax.fori_loop(0, ni, image, 0)
        out_copy().wait()
        for i in range(imgs):
            hidden = x_ref[i].astype(F32) + (out_ref[i] + other[i]) + vec_ref[6:7, :]
            out_ref[i] = hidden
            normed, _ = norm(hidden)
            mlp_in[i] = (normed * vec_ref[1:2, :] + vec_ref[3:4, :]).astype(BF16)
        in_copy = remote(mlp_in.at[mine], mlp_in.at[theirs], (c_send, c_recv), 5, pair)
        in_copy.start()
        hidden_copy = pltpu.make_async_copy(out_ref.at[mine], hidden_out, out_sem.at[3])
        hidden_copy.start()
        take_rows(1, ct_ref, cot_ref)
        pair_rows(1, cot_ref).start()
        in_copy.wait()
        mlp_copy = pltpu.make_async_copy(mlp_in, mlp_out, out_sem.at[4])
        mlp_copy.start()
        finish(1, range(cfg.early))
        pair_rows(1, cot_ref).wait()
        cot_copy = pltpu.make_async_copy(cot_ref, cot_out, out_sem.at[2])
        cot_copy.start()
        kept.wait()
        x_copy.wait()
        hidden_copy.wait()
        mlp_copy.wait()
        for i in range(ni):
            for copy in image_copies(i):
                copy.wait()
        cot_copy.wait()

    vmem = pl.BlockSpec(memory_space=pltpu.VMEM)
    smem = pl.BlockSpec(memory_space=pltpu.SMEM)
    anywhere = pl.BlockSpec(memory_space=pl.ANY)
    dma = pltpu.SemaphoreType.DMA
    return pl.pallas_call(
        kernel,
        in_specs=[smem, vmem, vmem, vmem, anywhere],
        out_specs=[anywhere] * 8 + [vmem] * 2 + [anywhere] * 2,
        out_shape=[
            jax.ShapeDtypeStruct((ni, PT, D), BF16),
            jax.ShapeDtypeStruct((ni, PT, D), BF16),
            jax.ShapeDtypeStruct((ni, PT, D), BF16),
            jax.ShapeDtypeStruct((n_t, ni, PT, 3 * hc), BF16),
            jax.ShapeDtypeStruct((n_t, ni, PT, hc), BF16),
            jax.ShapeDtypeStruct((n_t, ni, PT, hh), F32),
            jax.ShapeDtypeStruct((imgs, PT, D), F32),
            jax.ShapeDtypeStruct((ni, PT, D), BF16),
            jax.ShapeDtypeStruct((8, D), F32),
            jax.ShapeDtypeStruct((n_t, f2), F32),
            jax.ShapeDtypeStruct((n_t, D, f2), BF16),
            jax.ShapeDtypeStruct((2, n_t, D, f2), BF16),
        ],
        scratch_shapes=[
            pltpu.VMEM((ni, PT, D), BF16),
            pltpu.VMEM((ni, PT, D), BF16),
            pltpu.VMEM((ni, PT, D), BF16),
            pltpu.VMEM((n_t, ni, PT, 3 * hc), BF16),
            pltpu.VMEM((n_t, ni, PT, hc), BF16),
            pltpu.VMEM((n_t, ni, PT, hh), F32),
            pltpu.VMEM((ni, PT, D), F32),
            pltpu.VMEM((imgs, PT, D), F32),
            pltpu.VMEM((ni, PT, D), BF16),
            pltpu.VMEM((n_t, D, f2), BF16),
            pltpu.VMEM((2, len(caps), widest, D), BF16),
            pltpu.VMEM((2, len(caps), widest, D), BF16),
            pltpu.VMEM((n_dev, 16, 128), F32),
            pltpu.VMEM((n_t, hc), F32),
            pltpu.VMEM((n_t, hc), F32),
            dma((2, n_t)),
            dma((2, n_t)),
            dma((2, n_t, n_p)),
            dma((2, n_t, n_p)),
            dma((2, len(caps))),
            dma((2, len(caps))),
            dma((6,)),
            dma((6,)),
            dma((n_t + n_p,)),
            dma((n_t + n_p,)),
            dma((2,)),
            dma((5,)),
            dma((4, ni)),
        ],
        compiler_params=params(collective_id=0, has_side_effects=True),
        cost_estimate=pl.CostEstimate(
            flops=2 * m * D * f2 * n_t,
            bytes_accessed=2 * n_t * D * f2 + 12 * m * D,
            transcendentals=m * PT * n_t * hh,
        ),
        name="gather_and_attend",
    )(counts, tokens, cotangent, small, halves)


def reduce_and_attend_back(
    counts, grad_hidden, attn_in, qkv, attended, lse, weights, mlp_grads, residual, x, mixed, vectors, sums, fc1_sums, cfg
):
    n_t, n_p, ni, hc, hh, f2, pd, m, imgs = (
        cfg.n_t, cfg.n_p, cfg.ni, cfg.hc, cfg.hh, cfg.f2, cfg.pd, cfg.m, cfg.imgs,
    )
    scale = HD**-0.5
    square = n_p == 4
    plane = (2, 2) if square else (n_p,)
    order = list(range(n_t))[::-1]
    jobs = [((k, k), k) for k in order[:-1]]
    jobs += [((k, k - 1), None) for k in order[::2]] + [((0, 0), 0)]
    n_jobs = len(jobs)
    n_got = 2 if square else n_p - 1
    n_dev = 2 * n_p * n_t
    width = D // n_dev
    caps = list(cfg.caps.items())
    widest = max(size for _, size in caps)
    to_z = {}
    for n, (chunks, _) in enumerate(jobs):
        for part in range(2):
            if chunks[part] > 0:
                to_z[n, part] = len(to_z)

    def kernel(
        counts_ref, gh_ref, in_ref, qkv_ref, att_ref, lse_ref, w_ref, g_ref, res_ref, x_ref, mix_ref, vec_ref,
        sums_ref, fsum_ref,
        half_ref, mixed_ref, dtok_ref, small_ref, own_grads, rows_got, in_other, got_z,
        gqkv, stage, held, got, got_2, got_step, total, out, dq, dv,
        images, sent, taken, block, res_in, other_in, parts, parts_p, parts_c, parts_t,
        stage_sem, held_sem, s_send, s_recv, t_send, t_recv, z_send, z_recv, r_send, r_recv, c_send, c_recv,
        v_send, v_recv, in_sem, out_sem,
    ):
        p, core, z = (lax.axis_index(axis) for axis in ALL)
        py, px = p >> 1, p & 1
        pair = {"c": 1 - core}
        step = pl.program_id(0)
        layout = Layout(counts_ref, cfg)

        def pieces(n, part, *index):
            (chunks, k) = jobs[n]
            if k is None:
                return own_grads.at[(chunks[part], *index)]
            return g_ref.at[(*index, k, part)]

        def first_copies(n):
            if square:
                return [
                    remote(pieces(n, 0, slice(None), px ^ 1), got.at[n, 0], (s_send, s_recv), (n, 0, 0), {"p": p ^ 1}),
                    remote(pieces(n, 1, py ^ 1, slice(None)), got.at[n, 1], (s_send, s_recv), (n, 1, 0), {"p": p ^ 2}),
                ]
            return [
                remote(pieces(n, part, p ^ q), got.at[n, part, q - 1], (s_send, s_recv), (n, part, q - 1), {"p": p ^ q})
                for part in range(2)
                for q in range(1, n_p)
            ]

        def second_copies(n):
            if not square:
                return []
            return [
                remote(got.at[n, 0, py ^ 1], got_2.at[n, 0], (t_send, t_recv), (n, 0), {"p": p ^ 2}),
                remote(got.at[n, 1, px ^ 1], got_2.at[n, 1], (t_send, t_recv), (n, 1), {"p": p ^ 1}),
            ]

        def z_copy(n, part):
            k = jobs[n][0][part]
            source = got.at[n, part, (py, px)[part] if square else 0]
            target = {"t": lax.rem(z - k + n_t, n_t)}
            index = to_z[n, part]
            if jobs[n][1] is not None:
                target = {"t": lax.rem(z - 1 + n_t, n_t)}
                return remote(source, got_step.at[index], (z_send, z_recv), index, target)
            return remote(source, got_z.at[index], (z_send, z_recv), index, target)

        def loads(n):
            if square:
                sources = [pieces(n, 0, slice(None), px), pieces(n, 1, py, slice(None))]
            else:
                sources = [pieces(n, 0, p), pieces(n, 1, p)]
            return [
                pltpu.make_async_copy(
                    source, held.at[n % 2, part] if square else held.at[n % 2, part, 0], held_sem.at[n % 2, part]
                )
                for part, source in enumerate(sources)
            ]

        def begin(n):
            for copy in first_copies(n):
                copy.start()

        def fetch(n):
            for copy in loads(n):
                copy.start()

        def middle(n):
            for copy in loads(n):
                copy.wait()
            for copy in first_copies(n):
                copy.wait_recv()
            if square:
                for part, here in enumerate((py, px)):
                    there = here ^ 1
                    both = held[n % 2, part, there].astype(F32) + got[n, part, there].astype(F32)
                    got[n, part, there] = both.astype(BF16)
                for copy in second_copies(n):
                    copy.start()

        def last(n):
            for copy in second_copies(n):
                copy.wait_recv()
            chunks, k = jobs[n]
            for part, here in enumerate((py, px)):
                if square:
                    whole = held[n % 2, part, here].astype(F32) + got[n, part, here].astype(F32)
                    whole = whole + got_2[n, part].astype(F32)
                else:
                    whole = held[n % 2, part, 0].astype(F32)
                    for q in range(n_p - 1):
                        whole = whole + got[n, part, q].astype(F32)
                if k is not None and k < n_t - 1:
                    before = n - 1 if k > 0 else n_t - 2
                    z_copy(before, part).wait_recv()
                    whole = whole + got_step[to_z[before, part]].astype(F32)
                if chunks[part] == 0:
                    total[0 if k is None else 1 + part] = whole
                else:
                    got[n, part, here if square else 0] = whole.astype(BF16)
                    z_copy(n, part).start()

        def tick(n):
            middle(n)
            if n > 0:
                last(n - 1)
                if n + 1 < n_jobs:
                    fetch(n + 1)
            if n + 2 < n_jobs:
                begin(n + 2)

        def finish():
            last(n_jobs - 1)
            for n in range(n_jobs):
                for copy in first_copies(n) + second_copies(n):
                    copy.wait_send()
                for part in range(2):
                    if (n, part) in to_z:
                        z_copy(n, part).wait_send()
                        if jobs[n][1] is None:
                            z_copy(n, part).wait_recv()
            direct = [(n, part) for n, part in to_z if jobs[n][1] is None]
            reads = [
                pltpu.make_async_copy(got_z.at[to_z[spot]], got.at[(*spot, 0)], z_recv.at[to_z[spot]])
                for spot in direct
            ]
            for read in reads:
                read.start()
            for read in reads:
                read.wait()
            whole = total[0]
            for spot in direct:
                whole = whole + got[(*spot, 0)].astype(F32)
            total[0] = whole

            def rows(member):
                return total.at[:, pl.ds(pl.multiple_of(member * pd, 16), pd), :]

            kept = pltpu.make_async_copy(rows(core), half_ref.at[core], out_sem)
            traded = remote(rows(1 - core), half_ref.at[core], (c_send, c_recv), 1, pair)
            kept.start()
            traded.start()
            kept.wait()
            traded.wait()

        def row_copy(which, s):
            shift, size = caps[s]
            return remote(
                sent.at[s, pl.ds(0, size)], rows_got.at[which, s, pl.ds(0, size)], (r_send, r_recv), (which, s),
                {"t": jnp.clip(z - shift, 0, n_t - 1)},
            )

        def of_images(positions, valid):
            rows = None
            for i in range(imgs):
                spots = positions - i * TOK_IMG
                spots = jnp.where(valid & (spots >= 0) & (spots < TOK_IMG), spots, -1)
                picked = dot(one_hot(spots, PT), images[i])
                rows = picked if rows is None else rows + picked
            return rows.astype(BF16)

        def send_rows(which):
            for s, (shift, size) in enumerate(caps):

                @pl.when(layout.has(z - shift))
                def _(s=s, shift=shift, size=size):
                    want = layout.window_back(z, z - shift, size) + row_ids(size)
                    sent[s, :size] = of_images(want, want >= 0)
                    row_copy(which, s).start()

        def take_rows(which, target):
            row = row_ids(cfg.block)
            position = layout.start(z) + row
            valid = position < layout.end(z)
            block[...] = of_images(position - cfg.rows * z, valid)
            for s, (shift, size) in enumerate(caps):
                source = z + shift

                @pl.when(layout.has(source))
                def _(s=s, size=size, source=source):
                    row_copy(which, s).wait_recv()
                    load = pltpu.make_async_copy(
                        rows_got.at[which, s, pl.ds(0, size)], taken.at[pl.ds(0, size)], in_sem.at[0]
                    )
                    load.start()
                    load.wait()
                    local = position - cfg.rows * source
                    mine = valid & (local >= 0) & (local < cfg.rows)
                    spots = jnp.where(mine, local - layout.window_back(source, z, size), -1)
                    block[...] += dot(one_hot(spots, size), taken[:size]).astype(BF16)

                @pl.when(layout.has(z - shift))
                def _(s=s):
                    row_copy(which, s).wait_send()

            store = pltpu.make_async_copy(block, target, in_sem.at[0])
            store.start()
            store.wait()

        device = (2 * p + core) * n_t + z

        def gather_parts(gain, shift):
            parts[...] = jnp.zeros_like(parts)
            rows = [gain, sums_ref[0:1, :], shift, sums_ref[1:2, :], sums_ref[2:3, :], sums_ref[3:4, :]]
            for d in range(n_dev):
                cols = slice(d * width, (d + 1) * width)
                for r, value in zip((0, 1, 2, 3, 6, 7), rows):
                    parts[d, r : r + 1, :width] = value[:, cols]
            for k in range(n_t):
                chunk = 2 * lax.rem(z - k + n_t, n_t) + core
                for j in range(hc // width):
                    cols = slice(j * width, (j + 1) * width)
                    owner = chunk * (hc // width) + j
                    parts[owner, 4:5, :width] = dq[k : k + 1, cols]
                    parts[owner, 5:6, :width] = dv[k : k + 1, cols]
                for j in range(f2 // (4 * width)):
                    owner = chunk * (f2 // (4 * width)) + j
                    for r in range(4):
                        begin_at = (4 * j + r) * width
                        parts[owner, 8 + r : 9 + r, :width] = fsum_ref[k, :, begin_at : begin_at + width]

        def plane_parts(index):
            return pl.ds(2 * index * n_t, 2 * n_t)

        def core_parts(member):
            return pl.ds((2 * p + member) * n_t, n_t)

        def part_copies(hop):
            if hop == 0:
                return [
                    remote(parts.at[plane_parts(p ^ q)], parts_p.at[q - 1], (v_send, v_recv), q - 1, {"p": p ^ q})
                    for q in range(1, n_p)
                ]
            if hop == 1:
                return [remote(parts.at[core_parts(1 - core)], parts_c, (v_send, v_recv), n_p - 1, pair)]
            copies = []
            for k in range(1, n_t):
                to = lax.rem(z + k, n_t)
                source = parts.at[(2 * p + core) * n_t + to]
                copies.append(remote(source, parts_t.at[k], (v_send, v_recv), n_p - 1 + k, {"t": to}))
            return copies

        def part_hop(hop):
            if hop > 0:
                for copy in part_copies(hop - 1):
                    copy.wait()
            if hop == 1:
                for q in range(n_p - 1):
                    parts[plane_parts(p)] += parts_p[q]
            if hop == 2:
                parts[core_parts(core)] += parts_c[...]
            if hop == 3:
                mine = parts[device]
                for k in range(1, n_t):
                    mine = mine + parts_t[k]
                small_ref[...] = mine
            if hop < 3:
                for copy in part_copies(hop):
                    copy.start()

        def in_copy():
            return remote(out.at[pl.ds(imgs, imgs)], in_other, (c_send, c_recv), 0, pair)

        def first_norm_back():
            in_copy().wait()
            gain, shift = jnp.zeros((1, D), F32), jnp.zeros((1, D), F32)
            for i in range(imgs):
                reads = [
                    pltpu.make_async_copy(res_ref.at[i], res_in, in_sem.at[0]),
                    pltpu.make_async_copy(in_other.at[i], other_in, in_sem.at[1]),
                    pltpu.make_async_copy(x_ref.at[i], taken.at[pl.ds(0, PT)], in_sem.at[2]),
                ]
                for read in reads:
                    read.start()
                for read in reads:
                    read.wait()
                up = out[i] + other_in[...]
                normed, inverse = norm(taken[:PT].astype(F32))
                grad = res_in[...] + norm_back(up, normed, inverse, vec_ref[0:1, :])
                images[i] = grad.astype(BF16)
                gain = gain + jnp.sum(up * normed, axis=0, keepdims=True)
                shift = shift + jnp.sum(up, axis=0, keepdims=True)
            gather_parts(gain, shift)

        @pl.when(step == 0)
        def _():
            fetch(0)
            fetch(1)
            read = pltpu.make_async_copy(mix_ref, images, in_sem.at[0])
            read.start()
            enter(cfg)
            begin(0)
            begin(1)
            read.wait()
            send_rows(0)

        keyed = lax.broadcasted_iota(jnp.int32, (PT, PT), 1) < TOK_IMG
        total_q, total_v = jnp.zeros((1, hc), F32), jnp.zeros((1, hc), F32)
        for i in range(ni):
            grad_att = dot(gh_ref[i], w_ref[0, :, 3 * hc :]).astype(BF16)
            sums_q, sums_v = [], []
            for h in range(hh):
                cols = slice(h * HD, (h + 1) * HD)
                key_cols = slice(hc + h * HD, hc + (h + 1) * HD)
                value_cols = slice(2 * hc + h * HD, 2 * hc + (h + 1) * HD)
                query = qkv_ref[0, i, :, cols]
                keys = qkv_ref[0, i, :, key_cols]
                values = qkv_ref[0, i, :, value_cols]
                grad = grad_att[:, cols]
                scores = dot_nt(query, keys) * scale - lse_ref[0, i, :, h : h + 1]
                probs = jnp.exp(jnp.where(keyed, scores, NEG))
                delta = jnp.sum(
                    grad.astype(F32) * att_ref[0, i, :, cols].astype(F32), axis=-1, keepdims=True
                )
                grad_v = dot_tn(probs.astype(BF16), grad)
                grad_s = (probs * (dot_nt(grad, values) - delta) * scale).astype(BF16)
                grad_q = dot(grad_s, keys)
                grad_k = dot_tn(grad_s, query)
                sums_q.append(jnp.sum(grad_q, axis=0, keepdims=True))
                sums_v.append(jnp.sum(grad_v, axis=0, keepdims=True))
                gqkv[i, :, cols] = grad_q.astype(BF16)
                gqkv[i, :, key_cols] = grad_k.astype(BF16)
                gqkv[i, :, value_cols] = grad_v.astype(BF16)
            total_q = total_q + jnp.concatenate(sums_q, axis=1)
            total_v = total_v + jnp.concatenate(sums_v, axis=1)
            part = dot_nt(gqkv[i], w_ref[0, :, : 3 * hc])

            @pl.when(step == 0)
            def _(i=i, part=part):
                out[i] = part

            @pl.when(step > 0)
            def _(i=i, part=part):
                out[i] += part

            for n in range(n_t - 2):
                if i == min(2 * n + 1, ni - 1):

                    @pl.when(step == n + 1)
                    def _(n=n):
                        tick(n)

        dq[pl.ds(n_t - 1 - step, 1), :] = total_q
        dv[pl.ds(n_t - 1 - step, 1), :] = total_v

        @pl.when(step == n_t - 1)
        def _():
            in_copy().start()

        for side in range(2):
            cols = slice(side * D // 2, (side + 1) * D // 2)
            ahead = (side,) if square else (slice(side * n_p // 2, (side + 1) * n_p // 2),)
            ahead = ahead + (slice(None),) * len(plane)
            for lhs, rhs, lanes in (
                (in_ref, gqkv[...].reshape(m, 3 * hc), slice(0, 3 * hc)),
                (gh_ref, att_ref[0].reshape(m, hc), slice(3 * hc, f2)),
            ):
                value = dot_tn(lhs[:, :, cols].reshape(m, D // 2), rhs).astype(BF16)
                stage[(*ahead, lanes)] = value.reshape(
                    (n_p // 2, 2 * pd, lanes.stop - lanes.start)
                )
        store = pltpu.make_async_copy(stage, own_grads.at[n_t - 1 - step], stage_sem)
        store.start()
        store.wait()

        @pl.when(step == n_t - 2)
        def _():
            take_rows(0, mixed_ref)

        @pl.when(step == n_t - 1)
        def _():
            tick(n_t - 2)
            first_norm_back()
            send_rows(1)
            part_hop(0)
            tick(n_t - 1)
            part_hop(1)
            for n in range(n_t, n_jobs - 1):
                tick(n)
            part_hop(2)
            tick(n_jobs - 1)
            take_rows(1, dtok_ref)
            part_hop(3)
            finish()

    dma = pltpu.SemaphoreType.DMA
    chunk = (2 * pd, f2)
    vmem = pltpu.VMEM

    def chunk_block(last):
        return pl.BlockSpec((1, ni, PT, last), lambda k: (n_t - 1 - k, 0, 0, 0))

    anywhere = pl.BlockSpec(memory_space=pl.ANY)
    shape = jax.ShapeDtypeStruct
    n_v = n_p - 1 + n_t
    outs = pl.pallas_call(
        kernel,
        grid=(n_t,),
        in_specs=[
            pl.BlockSpec(memory_space=pltpu.SMEM),
            fixed((ni, PT, D)),
            fixed((ni, PT, D)),
            chunk_block(3 * hc),
            chunk_block(hc),
            chunk_block(hh),
            pl.BlockSpec((1, D, f2), lambda k: (n_t - 1 - k, 0, 0)),
            anywhere,
            anywhere,
            anywhere,
            anywhere,
            fixed((8, D)),
            fixed((4, D)),
            fixed((n_t, 1, f2)),
        ],
        out_specs=[anywhere] * 3 + [fixed((16, 128))] + [anywhere] * 4,
        out_shape=[
            shape((2, 3, pd, f2), F32),
            shape((cfg.block, D), BF16),
            shape((cfg.block, D), BF16),
            shape((16, 128), F32),
            shape((n_t, *plane, *chunk), BF16),
            shape((2, len(caps), widest, D), BF16),
            shape((imgs, PT, D), F32),
            shape((len(to_z), *chunk), BF16),
        ],
        scratch_shapes=[
            vmem((ni, PT, 3 * hc), BF16),
            vmem((*plane, *chunk), BF16),
            vmem((2, 2, 2 if square else 1, *chunk), BF16),
            vmem((n_jobs, 2, n_got, *chunk), BF16),
            vmem((n_jobs, 2, *(chunk if square else (16, 128))), BF16),
            vmem((2 * (n_t - 1), *chunk), BF16),
            vmem((3, *chunk), F32),
            vmem((ni, PT, D), F32),
            vmem((n_t, hc), F32),
            vmem((n_t, hc), F32),
            vmem((imgs, PT, D), BF16),
            vmem((len(caps), widest, D), BF16),
            vmem((max(widest, PT), D), BF16),
            vmem((cfg.block, D), BF16),
            vmem((PT, D), F32),
            vmem((PT, D), F32),
            vmem((n_dev, 16, 128), F32),
            vmem((n_p - 1, 2 * n_t, 16, 128), F32),
            vmem((n_t, 16, 128), F32),
            vmem((n_t, 16, 128), F32),
            dma,
            dma((2, 2)),
            dma((n_jobs, 2, 1 if square else n_p - 1)),
            dma((n_jobs, 2, 1 if square else n_p - 1)),
            dma((n_jobs, 2)),
            dma((n_jobs, 2)),
            dma((len(to_z),)),
            dma((len(to_z),)),
            dma((2, len(caps))),
            dma((2, len(caps))),
            dma((2,)),
            dma((2,)),
            dma((n_v,)),
            dma((n_v,)),
            dma((3,)),
            dma,
        ],
        compiler_params=params(collective_id=1, has_side_effects=True),
        cost_estimate=pl.CostEstimate(
            flops=4 * m * D * f2 * n_t + 10 * m * PT * HD * n_t * hh,
            bytes_accessed=4 * n_t * D * f2 + 20 * m * D,
            transcendentals=m * PT * n_t * hh,
        ),
        name="reduce_and_attend_back",
    )(
        counts,
        grad_hidden,
        attn_in,
        qkv,
        attended,
        lse,
        weights,
        mlp_grads.reshape((*plane, n_t, 2, *chunk)),
        residual,
        x,
        mixed,
        vectors,
        sums,
        fc1_sums,
    )
    return outs[:4]


def mlp_pass(hidden, mlp_in, vectors, cot, fc1, weights, cfg):
    n_p, n_t, m, pd, w, ni, imgs = cfg.n_p, cfg.n_t, cfg.m, cfg.pd, cfg.f2, cfg.ni, cfg.imgs
    early = cfg.early

    def kernel(
        hidden_ref, mlp_in, vec_ref, cot_ref, fc1_ref, g_ref,
        sum_ref, grad_ref, res_ref, gh_ref, sums_ref, mixed_ref, late_ref,
        other, other_y, act_all, gpre_all, back, y, gh, w_all,
        c_send, c_recv, own_sem, load_sem, keep_sem, z_send, z_recv, p_send, p_recv,
    ):
        step = pl.program_id(0)
        p, z = lax.axis_index("p"), lax.axis_index("t")
        pair = {"c": 1 - lax.axis_index("c")}

        def rows(mask):
            return pl.ds(pl.multiple_of((p ^ mask) * 2 * pd, 16), 2 * pd)

        def own_rows(j):
            return g_ref.at[:, early, rows(0), :] if j == 0 else late_ref.at[:, j, rows(0), :]

        def keep():
            return pltpu.make_async_copy(own_rows(0), late_ref.at[:, 0, rows(0), :], keep_sem)

        def z_copy(j):
            target = {"t": lax.rem(z + 1, n_t)}
            return remote(own_rows(j - 1), own_rows(j), (z_send, z_recv), j, target)

        def p_copy(j, mask):
            target = late_ref.at[:, j, rows(0), :]
            return remote(own_rows(j), target, (p_send, p_recv), (j, mask), {"p": p ^ mask})

        def d_copies(j):
            if n_p != 4:
                return []
            ref_1, ref_2 = late_ref.at[0, j, rows(1), :], late_ref.at[1, j, rows(2), :]
            return [
                remote(ref_1, ref_1, (p_send, p_recv), (j, 3), {"p": p ^ 2}),
                remote(ref_2, ref_2, (p_send, p_recv), (j, 0), {"p": p ^ 1}),
            ]

        direct = (1, 2) if n_p == 4 else tuple(range(1, n_p))

        def send_p(j):
            if j > 0:
                z_copy(j).wait_recv()
            if early + j + 1 < n_t:
                z_copy(j + 1).start()
            for mask in direct:
                p_copy(j, mask).start()

        def send_d(j):
            for mask in direct:
                p_copy(j, mask).wait_recv()
            for copy in d_copies(j):
                copy.start()
            if early + j + 1 < n_t:
                send_p(j + 1)

        def complete(j):
            if j == 0:
                keep().wait()
            for copy in d_copies(j):
                copy.wait_recv()

        def load(k):
            source = g_ref.at[:, k] if k < early else late_ref.at[:, k - early]
            return pltpu.make_async_copy(source, w_all.at[k % 2], load_sem.at[k % 2])
        mine, theirs = pl.ds(0, imgs), pl.ds(imgs, imgs)

        def pair_copy(index, source, target):
            return remote(source, target, (c_send, c_recv), index, pair)

        def back_copy():
            return pair_copy(0, back.at[theirs], other)

        def y_copy():
            return pair_copy(1, y.at[theirs], other_y)

        @pl.when(step == 0)
        def _():
            pltpu.make_async_copy(hidden_ref, res_ref, own_sem).start()
            keep().start()
            for k in range(min(2, early)):
                load(k).start()
            enter(cfg)
            send_p(0)
        slot = lax.rem(step, 2)
        for k in range(n_t):

            @pl.when(step == k)
            def _(k=k):
                load(k).wait()

        w1, w2 = w_all[slot, 0], w_all[slot, 1]
        total = jnp.zeros((1, w), F32)
        for i in range(ni):
            rows_i = slice(i * PT, (i + 1) * PT)
            pre = dot(mlp_in[i], w1) + fc1_ref[0]
            phi = 0.5 * (1.0 + lax.erf(pre * (1.0 / math.sqrt(2.0))))
            act_all[rows_i, :] = (pre * phi).astype(BF16)
            slope = phi + pre * jnp.exp(-0.5 * pre * pre) * (1.0 / math.sqrt(2.0 * math.pi))
            gpre = dot(cot_ref[i], w2) * slope
            total = total + jnp.sum(gpre, axis=0, keepdims=True)
            gpre_all[rows_i, :] = gpre.astype(BF16)
            if i == min(1, ni - 1):
                for j in range(n_t - early):

                    @pl.when(step == j)
                    def _(j=j):
                        send_d(j)

        sum_ref[0] = total
        for k in range(2, n_t):

            @pl.when(step == k - 1)
            def _(k=k):
                if k >= early:
                    complete(k - early)
                load(k).start()

        def add(target, left, right):
            value = dot_nt(left, right).reshape(ni, PT, D)

            @pl.when(step == 0)
            def _():
                target[...] = value

            @pl.when(step > 0)
            def _():
                target[...] += value

        add(back, gpre_all[...], w1)

        @pl.when(step == n_t - 1)
        def _():
            back_copy().start()

        add(y, act_all[...], w2)

        @pl.when(step == n_t - 1)
        def _():
            y_copy().start()

        grad_1 = dot_tn(mlp_in[...].reshape(m, D), gpre_all[...]).astype(BF16)
        grad_ref[:, 0, 0] = grad_1.reshape(n_p, 2 * pd, w)
        grad_2 = dot_tn(cot_ref[...].reshape(m, D), act_all[...]).astype(BF16)
        grad_ref[:, 0, 1] = grad_2.reshape(n_p, 2 * pd, w)

        @pl.when(step == n_t - 1)
        def _():
            pltpu.make_async_copy(hidden_ref, res_ref, own_sem).wait()
            back_copy().wait()
            sums = [jnp.zeros((1, D), F32)] * 4
            for i in range(imgs):
                up = back[i] + other[i]
                hidden = res_ref[i]
                other[i] = hidden
                normed, inverse = norm(hidden)
                cot_f = cot_ref[i].astype(F32)
                grad = cot_f + norm_back(up, normed, inverse, vec_ref[1:2, :])
                res_ref[i] = grad
                gh[i] = grad.astype(BF16)
                terms = (up * normed, up, grad, cot_f)
                sums = [s + jnp.sum(t, axis=0, keepdims=True) for s, t in zip(sums, terms)]
            grad_copy = pair_copy(2, gh.at[mine], gh.at[theirs])
            grad_copy.start()
            for r in range(4):
                sums_ref[r : r + 1, :] = sums[r]
            y_copy().wait()
            for i in range(imgs):
                mixed_ref[i] = (other[i] + (y[i] + other_y[i]) + vec_ref[7:8, :]).astype(BF16)
            grad_copy.wait()
            store = pltpu.make_async_copy(gh, gh_ref, own_sem)
            store.start()
            for j in range(n_t - early):
                for copy in d_copies(j):
                    copy.wait_send()
                for mask in direct:
                    p_copy(j, mask).wait_send()
                if j > 0:
                    z_copy(j).wait_send()
            store.wait()

    full = fixed((ni, PT, D))
    own = fixed((imgs, PT, D))
    shape, vmem, dma = jax.ShapeDtypeStruct, pltpu.VMEM, pltpu.SemaphoreType.DMA
    return pl.pallas_call(
        kernel,
        grid=(n_t,),
        in_specs=[
            pl.BlockSpec(memory_space=pl.ANY),
            full,
            fixed((8, D)),
            full,
            pl.BlockSpec((1, 1, w), lambda i: (i, 0, 0)),
            pl.BlockSpec(memory_space=pl.ANY),
        ],
        out_specs=[
            pl.BlockSpec((1, 1, w), lambda i: (i, 0, 0)),
            pl.BlockSpec((n_p, 1, 2, 2 * pd, w), lambda i: (0, i, 0, 0, 0)),
            own,
            pl.BlockSpec(memory_space=pl.ANY),
            fixed((4, D)),
            own,
            pl.BlockSpec(memory_space=pl.ANY),
        ],
        out_shape=[
            shape((n_t, 1, w), F32),
            shape((n_p, n_t, 2, 2 * pd, w), BF16),
            shape((imgs, PT, D), F32),
            shape((ni, PT, D), BF16),
            shape((4, D), F32),
            shape((imgs, PT, D), BF16),
            shape((2, n_t - early, D, w), BF16),
        ],
        scratch_shapes=[
            vmem((imgs, PT, D), F32),
            vmem((imgs, PT, D), F32),
            vmem((m, w), BF16),
            vmem((m, w), BF16),
            vmem((ni, PT, D), F32),
            vmem((ni, PT, D), F32),
            vmem((ni, PT, D), BF16),
            vmem((2, 2, D, w), BF16),
            dma((3,)),
            dma((3,)),
            dma,
            dma((2,)),
            dma,
            dma((n_t - early,)),
            dma((n_t - early,)),
            dma((n_t - early, n_p)),
            dma((n_t - early, n_p)),
        ],
        compiler_params=params(collective_id=2, has_side_effects=True),
        cost_estimate=pl.CostEstimate(
            flops=12 * m * D * w * n_t,
            bytes_accessed=12 * m * D + 8 * D * w * n_t,
            transcendentals=2 * m * w * n_t,
        ),
        name="mlp_pass",
    )(hidden, mlp_in, vectors, cot, fc1.reshape(n_t, 1, w), weights)[:-1]


def body(cfg, tokens, counts, gains, biases, fc1_bias, w_qkv, w_o, w_1, w_2, cotangent):
    pd, f2, hc = cfg.pd, cfg.f2, cfg.hc
    halves = jnp.stack(
        [
            jnp.concatenate(
                [
                    w_qkv.reshape(pd, 3, 2, hc).transpose(2, 0, 1, 3).reshape(2, pd, 3 * hc),
                    w_o.T.reshape(pd, 2, hc).transpose(1, 0, 2),
                ],
                axis=2,
            ),
            w_1.reshape(pd, 2, f2).transpose(1, 0, 2),
            w_2.T.reshape(pd, 2, f2).transpose(1, 0, 2),
        ],
        axis=1,
    )
    small = jnp.concatenate([gains, biases, fc1_bias.reshape(4, -1)])
    small = jnp.pad(small, ((0, 4), (0, 128 - small.shape[1])))

    x, cot, attn_in, qkv, attended, lse, hidden, mlp_in, vectors, fc1, attn_w, mlp_w = gather_and_attend(
        counts, tokens, cotangent, small, halves, cfg
    )
    fc1_sums, mlp_grads, residual, grad_hidden, sums, mixed = mlp_pass(
        hidden, mlp_in, vectors, cot, fc1, mlp_w, cfg
    )
    both, mixed, d_tokens, small = reduce_and_attend_back(
        counts, grad_hidden, attn_in, qkv, attended, lse, attn_w, mlp_grads, residual, x, mixed, vectors, sums,
        fc1_sums, cfg,
    )
    d_qkv = both[:, 0, :, : 3 * hc].reshape(2, pd, 3, hc).transpose(1, 2, 0, 3).reshape(pd, 3, 2 * hc)
    d_o = both[:, 0, :, 3 * hc :].transpose(0, 2, 1).reshape(2 * hc, pd)
    d_1 = both[:, 1].transpose(1, 0, 2).reshape(pd, 2 * f2)
    d_2 = both[:, 2].transpose(0, 2, 1).reshape(2 * f2, pd)
    piece = D // (cfg.n_dp * cfg.n_t)
    small = small[:, :piece]
    return (
        mixed,
        d_tokens,
        d_qkv,
        d_o,
        d_1,
        d_2,
        small[:2],
        small[2:8],
        small[8:12].reshape(-1),
    )


def solution(mesh):
    n_dp, n_t = mesh.shape["dp"], mesh.shape["tensor"]
    split = Mesh(mesh.devices.reshape(n_dp // 2, 2, n_t), ALL)

    def program(tokens, *rest):
        cfg = Cfg(n_dp, n_t, tokens.shape[0])
        return body(cfg, tokens, *rest)

    dp = ("p", "c")
    return jax.shard_map(
        program,
        mesh=split,
        in_specs=(
            P(ALL, None),
            P(dp, None),
            P(None, ALL),
            P(None, ALL),
            P(ALL),
            P(dp, None, "t"),
            P("t", dp),
            P(dp, "t"),
            P("t", dp),
            P(ALL, None),
        ),
        out_specs=(
            P(ALL, None),
            P(ALL, None),
            P(dp, None, "t"),
            P("t", dp),
            P(dp, "t"),
            P("t", dp),
            P(None, ALL),
            P(None, ALL),
            P(ALL),
        ),
        check_vma=False,
    )
```

```python
import math

import jax
import jax.numpy as jnp
from jax import lax
from jax.experimental import pallas as pl
from jax.experimental.pallas import tpu as pltpu
from jax.sharding import Mesh
from jax.sharding import PartitionSpec as P

D = 1280
HD = 80
HEADS = 16
FF = 5120
TOK_IMG = 257
IMG_DEV = 8
TOTAL = IMG_DEV * TOK_IMG
EPS = 1e-06
PT = 272
F32 = jnp.float32
BF16 = jnp.bfloat16
NEG = -1e30
VMEM_LIMIT = 61 * 1024 * 1024


class Cfg:
    def __init__(self, n_dp, n_t, block_rows):
        self.n_dp, self.n_t, self.block = n_dp, n_t, block_rows
        self.n_p = n_dp // 2
        self.imgs = IMG_DEV // n_t
        self.ni = 2 * self.imgs
        self.rows = self.imgs * TOK_IMG
        self.m = self.ni * PT
        self.pd = D // n_dp
        self.hh = HEADS // n_t // 2
        self.hc = self.hh * HD
        self.f2 = FF // n_t // 2
        assert 4 * self.hc == self.f2
        self.early = n_t // 2
        self.caps = self._caps()

    def _caps(self):
        n, b, r = self.n_t, self.block, self.rows
        low = [max(t, TOTAL - (n - t) * b) for t in range(n + 1)]
        high = [min(t * b, TOTAL - (n - t)) for t in range(n + 1)]
        caps = {}
        for t in range(n):
            for dest in range(n):
                size = min(high[t + 1], r * (dest + 1)) - max(low[t], r * dest)
                size = min(size, b, r)
                if size > 0 and dest != t:
                    caps[dest - t] = max(caps.get(dest - t, 0), size)
        return {s: min(-(-c // 16) * 16, b) for s, c in sorted(caps.items())}


def dot(a, b):
    return lax.dot_general(a, b, (((1,), (0,)), ((), ())), preferred_element_type=F32)


def dot_nt(a, b):
    return lax.dot_general(a, b, (((1,), (1,)), ((), ())), preferred_element_type=F32)


def dot_tn(a, b):
    return lax.dot_general(a, b, (((0,), (0,)), ((), ())), preferred_element_type=F32)


def norm(values):
    mean = jnp.mean(values, axis=-1, keepdims=True)
    centred = values - mean
    spread = jnp.mean(centred * centred, axis=-1, keepdims=True)
    inverse = lax.rsqrt(spread + EPS)
    return centred * inverse, inverse


def norm_back(upstream, normed, inverse, gain):
    scaled = upstream * gain
    return inverse * (
        scaled
        - jnp.mean(scaled, axis=-1, keepdims=True)
        - normed * jnp.mean(scaled * normed, axis=-1, keepdims=True)
    )


ALL = ("p", "c", "t")


def params(**more):
    return pltpu.CompilerParams(vmem_limit_bytes=VMEM_LIMIT, **more)


def fixed(shape):
    return pl.BlockSpec(
        shape, lambda i, *s: (0,) * len(shape), pipeline_mode=pl.Buffered(1)
    )


MESH = pl.DeviceIdType.MESH


def enter(cfg):
    p, c, t = (lax.axis_index(axis) for axis in ALL)
    found = [{"c": 1 - c}]
    found += [{"t": lax.rem(t + k, cfg.n_t)} for k in range(1, cfg.n_t)]
    found += [{"p": p ^ m} for m in range(1, cfg.n_p)]
    barrier = pltpu.get_barrier_semaphore()
    for device in found:
        pl.semaphore_signal(barrier, inc=1, device_id=device, device_id_type=MESH)
    pl.semaphore_wait(barrier, len(found))


def remote(source, target, sems, index, device):
    return pltpu.make_async_remote_copy(
        src_ref=source,
        dst_ref=target,
        send_sem=sems[0].at[index],
        recv_sem=sems[1].at[index],
        device_id=device,
        device_id_type=MESH,
    )


class Layout:
    def __init__(self, counts_ref, cfg):
        self.counts, self.cfg = counts_ref, cfg
        self.z = lax.axis_index("t")

    def start(self, block):
        total = 0
        for j in range(self.cfg.n_t):
            total = total + jnp.where(block > j, self.counts[0, j], 0)
        return total

    def end(self, block):
        return self.start(block + 1)

    def has(self, block):
        return (block >= 0) & (block < self.cfg.n_t)

    def window(self, block, dest, size):
        return jnp.clip(self.cfg.rows * dest - self.start(block), 0, self.cfg.block - size)

    def window_back(self, dest, block, size):
        return jnp.clip(self.start(block) - self.cfg.rows * dest, 0, max(0, self.cfg.rows - size))


def one_hot(positions, limit):
    columns = lax.broadcasted_iota(jnp.int32, (positions.shape[0], limit), 1)
    return jnp.where(columns == positions, 1.0, 0.0).astype(BF16)


def row_ids(count):
    return lax.broadcasted_iota(jnp.int32, (count, 1), 0)


def gather_and_attend(counts, tokens, cotangent, small, halves, cfg):
    n_t, n_p, ni, hc, hh, f2, pd, imgs, m = (
        cfg.n_t, cfg.n_p, cfg.ni, cfg.hc, cfg.hh, cfg.f2, cfg.pd, cfg.imgs, cfg.m,
    )
    n_dev = 2 * n_p * n_t
    piece = D // n_dev
    caps = list(cfg.caps.items())
    widest = max(size for _, size in caps)

    def kernel(
        counts_ref, tok_ref, ct_ref, small_ref, half_ref,
        x_out, cot_out, in_out, qkv_out, att_out, lse_out, hidden_out, mlp_out, vec_ref, fc1_ref, g0_ref, g_ref,
        x_ref, cot_ref, in_ref, qkv_ref, att_ref, lse_ref, out_ref, other, mlp_in, w, sent, got, parts, q_bias, v_bias,
        z_send, z_recv, p_send, p_recv, r_send, r_recv, c_send, c_recv, v_send, v_recv, own_sem, out_sem, image_sem,
    ):
        p, core, z = (lax.axis_index(axis) for axis in ALL)
        layout = Layout(counts_ref, cfg)
        pair = {"c": 1 - core}

        def part_rows(plane, member):
            return pl.ds(pl.multiple_of((plane * 2 + member) * pd, 16), pd)

        def place(group, k, mask):
            rows = pl.ds(pl.multiple_of((p ^ mask) * 2 * pd, 16), 2 * pd)
            return w.at[k, rows, :] if group == 0 else g_ref.at[:, k, rows, :]

        def half(group, member):
            return half_ref.at[member, 0] if group == 0 else half_ref.at[member, pl.ds(1, 2)]

        def half_place(group):
            rows = part_rows(p, core)
            return w.at[0, rows, :] if group == 0 else g_ref.at[:, 0, rows, :]

        def keep(group):
            return pltpu.make_async_copy(half(group, core), half_place(group), own_sem.at[group])

        def trade(group):
            return remote(half(group, 1 - core), half_place(group), (c_send, c_recv), group, pair)

        def z_copy(group, k):
            target = {"t": lax.rem(z + 1, n_t)}
            return remote(place(group, k - 1, 0), place(group, k, 0), (z_send, z_recv), (group, k), target)

        def p_copy(group, k, mask):
            ref = place(group, k, 0)
            return remote(ref, ref, (p_send, p_recv), (group, k, mask), {"p": p ^ mask})

        def d_copies(group, k):
            if n_p != 4:
                return []

            def rows(mask):
                return pl.ds(pl.multiple_of((p ^ mask) * 2 * pd, 16), 2 * pd)

            if group == 0:
                via = 1 + k % 2
                ref = w.at[k, rows(via), :]
                return [remote(ref, ref, (p_send, p_recv), (group, k, 3), {"p": p ^ (3 - via)})]
            ref_1, ref_2 = g_ref.at[0, k, rows(1), :], g_ref.at[1, k, rows(2), :]
            return [
                remote(ref_1, ref_1, (p_send, p_recv), (group, k, 3), {"p": p ^ 2}),
                remote(ref_2, ref_2, (p_send, p_recv), (group, k, 0), {"p": p ^ 1}),
            ]

        direct = (1, 2) if n_p == 4 else tuple(range(1, n_p))

        def have_own(group):
            keep(group).wait()
            trade(group).wait()

        def send_p(group, k):
            for mask in direct:
                p_copy(group, k, mask).start()

        def send_z(group, k):
            if k > 1:
                z_copy(group, k - 1).wait_recv()
            z_copy(group, k).start()

        def send_d(group, k):
            for mask in direct:
                p_copy(group, k, mask).wait_recv()
            for copy in d_copies(group, k):
                copy.start()

        def finish(group, chunks):
            for k in chunks:
                for copy in d_copies(group, k):
                    copy.wait_recv()
                    copy.wait_send()
                for mask in direct:
                    p_copy(group, k, mask).wait_send()
            for k in range(1, n_t if group == 0 else cfg.early + 1):
                z_copy(group, k).wait_send()

        def row_copy(which, s):
            shift, size = caps[s]
            rows = pl.ds(0, size)
            return remote(
                sent.at[which, s, rows], got.at[which, s, rows], (r_send, r_recv), (which, s),
                {"t": jnp.clip(z + shift, 0, n_t - 1)},
            )

        def send_rows(which, block_ref):
            for s, (shift, size) in enumerate(caps):

                @pl.when(layout.has(z + shift))
                def _(s=s, shift=shift, size=size):
                    begin = layout.window(z, z + shift, size)
                    picked = dot(one_hot(begin + row_ids(size), cfg.block), block_ref[...])
                    sent[which, s, :size] = picked.astype(BF16)
                    row_copy(which, s).start()

        def take_rows(which, block_ref, images_ref):
            for i in range(imgs):
                row = row_ids(PT)
                position = cfg.rows * z + i * TOK_IMG + row
                valid = row < TOK_IMG
                mine = valid & (position < layout.end(z))
                spots = jnp.where(mine, position - layout.start(z), -1)
                images_ref[i] = dot(one_hot(spots, cfg.block), block_ref[...]).astype(BF16)
            for s, (shift, size) in enumerate(caps):
                source = z - shift

                @pl.when(layout.has(source))
                def _(s=s, size=size, source=source):
                    row_copy(which, s).wait_recv()
                    for i in range(imgs):
                        row = row_ids(PT)
                        position = cfg.rows * z + i * TOK_IMG + row
                        mine = (row < TOK_IMG) & (position < layout.end(source))
                        mine = mine & (position >= layout.start(source))
                        spots = position - layout.start(source) - layout.window(source, z, size)
                        picked = dot(one_hot(jnp.where(mine, spots, -1), size), got[which, s, :size])
                        images_ref[i] += picked.astype(BF16)

                @pl.when(layout.has(z + shift))
                def _(s=s):
                    row_copy(which, s).wait_send()

        def pair_rows(which, images_ref):
            mine, other = pl.ds(0, imgs), pl.ds(imgs, imgs)
            return remote(images_ref.at[mine], images_ref.at[other], (c_send, c_recv), 2 + which, pair)

        device = (2 * p + core) * n_t + z

        def part_copies(stage):
            if stage == 0:
                ref = parts.at[device]
                targets = [(k, {"t": lax.rem(z + k, n_t)}) for k in range(1, n_t)]
            elif stage == 1:
                ref = parts.at[pl.ds((2 * p + core) * n_t, n_t)]
                targets = [(n_t, pair)]
            else:
                ref = parts.at[pl.ds(2 * p * n_t, 2 * n_t)]
                targets = [(n_t + mask, {"p": p ^ mask}) for mask in range(1, n_p)]
            return [remote(ref, ref, (v_send, v_recv), index, target) for index, target in targets]

        def part_stage(stage):
            if stage > 0:
                for copy in part_copies(stage - 1):
                    copy.wait()
            if stage < 3:
                for copy in part_copies(stage):
                    copy.start()

        def spread():
            for d in range(n_dev):
                vec_ref[:, d * piece : (d + 1) * piece] = parts[d, :8, :piece]
            for k in range(n_t):
                block = 2 * lax.rem(z - k + n_t, n_t) + core
                for j in range(hc // piece):
                    cols = slice(j * piece, (j + 1) * piece)
                    owner = block * (hc // piece) + j
                    q_bias[k : k + 1, cols] = parts[owner, 4:5, :piece]
                    v_bias[k : k + 1, cols] = parts[owner, 5:6, :piece]
                for j in range(f2 // (4 * piece)):
                    owner = block * (f2 // (4 * piece)) + j
                    for r in range(4):
                        begin = (4 * j + r) * piece
                        fc1_ref[k : k + 1, begin : begin + piece] = parts[owner, 8 + r : 9 + r, :piece]

        for group in range(2):
            keep(group).start()
        parts[device] = small_ref[...]
        enter(cfg)
        for group in range(2):
            trade(group).start()
        part_stage(0)
        have_own(0)
        send_p(0, 0)
        send_z(0, 1)
        have_own(1)
        send_p(1, 0)
        send_rows(0, tok_ref)
        part_stage(1)
        send_d(0, 0)
        part_stage(2)
        z_last = n_t - 1
        for k in range(1, n_t):
            if k < z_last:
                send_z(0, k + 1)
            else:
                z_copy(0, k).wait_recv()
            if k == z_last - 1:
                send_z(1, 1)
            send_p(0, k)
            if k == 1:
                send_d(1, 0)
                part_stage(3)
                spread()
            else:
                send_d(0, k - 1)
            if k == z_last - 1:
                take_rows(0, tok_ref, x_ref)
                pair_rows(0, x_ref).start()
        send_d(0, z_last)
        steps = []
        for k in range(1, cfg.early + 1):
            if k < cfg.early:
                steps.append(lambda k=k: send_z(1, k + 1))
                steps.append(lambda k=k: send_p(1, k))
            else:
                steps.append(lambda k=k: z_copy(1, k).wait_recv())
            if k > 1:
                steps.append(lambda k=k: send_d(1, k - 1))
        for step in steps[:2]:
            step()
        steps = steps[2:]
        send_rows(1, ct_ref)
        pair_rows(0, x_ref).wait()
        finish(0, range(n_t))
        kept = pltpu.make_async_copy(w, g0_ref, out_sem.at[0])
        kept.start()
        x_copy = pltpu.make_async_copy(x_ref, x_out, out_sem.at[1])
        x_copy.start()
        early = len(steps)

        def image_copies(i):
            return [
                pltpu.make_async_copy(in_ref.at[i], in_out.at[i], image_sem.at[0, i]),
                pltpu.make_async_copy(qkv_ref.at[:, i], qkv_out.at[:, i], image_sem.at[1, i]),
                pltpu.make_async_copy(att_ref.at[:, i], att_out.at[:, i], image_sem.at[2, i]),
                pltpu.make_async_copy(lse_ref.at[:, i], lse_out.at[:, i], image_sem.at[3, i]),
            ]

        keyed = lax.broadcasted_iota(jnp.int32, (PT, PT), 1) < TOK_IMG

        mine, theirs = pl.ds(0, imgs), pl.ds(imgs, imgs)

        def out_copy():
            return remote(out_ref.at[theirs], other, (c_send, c_recv), 4, pair)

        def image(turn, carry):
            i = lax.rem(turn + imgs, ni)
            normed, _ = norm(x_ref[i].astype(F32))
            attn_in = (normed * vec_ref[0:1, :] + vec_ref[2:3, :]).astype(BF16)
            in_ref[i] = attn_in
            for k in range(n_t):
                qkv = dot(attn_in, w[k, :, : 3 * hc])
                query = (qkv[:, :hc] + q_bias[k : k + 1, :]).astype(BF16)
                keys = qkv[:, hc : 2 * hc].astype(BF16)
                values = (qkv[:, 2 * hc :] + v_bias[k : k + 1, :]).astype(BF16)
                qkv_ref[k, i, :, :hc] = query
                qkv_ref[k, i, :, hc : 2 * hc] = keys
                qkv_ref[k, i, :, 2 * hc :] = values
                for h in range(hh):
                    cols = slice(h * HD, (h + 1) * HD)
                    scores = dot_nt(query[:, cols], keys[:, cols]) * (HD**-0.5)
                    scores = jnp.where(keyed, scores, NEG)
                    top = jnp.max(scores, axis=-1, keepdims=True)
                    expo = jnp.exp(scores - top)
                    summed = jnp.sum(expo, axis=-1, keepdims=True)
                    probs = (expo / summed).astype(BF16)
                    att_ref[k, i, :, cols] = dot(probs, values[:, cols]).astype(BF16)
                    lse_ref[k, i, :, h : h + 1] = top + jnp.log(summed)
                part = dot_nt(att_ref[k, i], w[k, :, 3 * hc :])
                if k == 0:
                    out_ref[i] = part
                else:
                    out_ref[i] += part
            for copy in image_copies(i):
                copy.start()

            @pl.when(turn == imgs - 1)
            def _():
                out_copy().start()

            for j in range(early):

                @pl.when(turn == min(j, ni - 1))
                def _(j=j):
                    steps[j]()

            return carry

        lax.fori_loop(0, ni, image, 0)
        out_copy().wait()
        for i in range(imgs):
            hidden = x_ref[i].astype(F32) + (out_ref[i] + other[i]) + vec_ref[6:7, :]
            out_ref[i] = hidden
            normed, _ = norm(hidden)
            mlp_in[i] = (normed * vec_ref[1:2, :] + vec_ref[3:4, :]).astype(BF16)
        in_copy = remote(mlp_in.at[mine], mlp_in.at[theirs], (c_send, c_recv), 5, pair)
        in_copy.start()
        hidden_copy = pltpu.make_async_copy(out_ref.at[mine], hidden_out, out_sem.at[3])
        hidden_copy.start()
        take_rows(1, ct_ref, cot_ref)
        pair_rows(1, cot_ref).start()
        in_copy.wait()
        mlp_copy = pltpu.make_async_copy(mlp_in, mlp_out, out_sem.at[4])
        mlp_copy.start()
        finish(1, range(cfg.early))
        pair_rows(1, cot_ref).wait()
        cot_copy = pltpu.make_async_copy(cot_ref, cot_out, out_sem.at[2])
        cot_copy.start()
        kept.wait()
        x_copy.wait()
        hidden_copy.wait()
        mlp_copy.wait()
        for i in range(ni):
            for copy in image_copies(i):
                copy.wait()
        cot_copy.wait()

    vmem = pl.BlockSpec(memory_space=pltpu.VMEM)
    smem = pl.BlockSpec(memory_space=pltpu.SMEM)
    anywhere = pl.BlockSpec(memory_space=pl.ANY)
    dma = pltpu.SemaphoreType.DMA
    return pl.pallas_call(
        kernel,
        in_specs=[smem, vmem, vmem, vmem, anywhere],
        out_specs=[anywhere] * 8 + [vmem] * 2 + [anywhere] * 2,
        out_shape=[
            jax.ShapeDtypeStruct((ni, PT, D), BF16),
            jax.ShapeDtypeStruct((ni, PT, D), BF16),
            jax.ShapeDtypeStruct((ni, PT, D), BF16),
            jax.ShapeDtypeStruct((n_t, ni, PT, 3 * hc), BF16),
            jax.ShapeDtypeStruct((n_t, ni, PT, hc), BF16),
            jax.ShapeDtypeStruct((n_t, ni, PT, hh), F32),
            jax.ShapeDtypeStruct((imgs, PT, D), F32),
            jax.ShapeDtypeStruct((ni, PT, D), BF16),
            jax.ShapeDtypeStruct((8, D), F32),
            jax.ShapeDtypeStruct((n_t, f2), F32),
            jax.ShapeDtypeStruct((n_t, D, f2), BF16),
            jax.ShapeDtypeStruct((2, n_t, D, f2), BF16),
        ],
        scratch_shapes=[
            pltpu.VMEM((ni, PT, D), BF16),
            pltpu.VMEM((ni, PT, D), BF16),
            pltpu.VMEM((ni, PT, D), BF16),
            pltpu.VMEM((n_t, ni, PT, 3 * hc), BF16),
            pltpu.VMEM((n_t, ni, PT, hc), BF16),
            pltpu.VMEM((n_t, ni, PT, hh), F32),
            pltpu.VMEM((ni, PT, D), F32),
            pltpu.VMEM((imgs, PT, D), F32),
            pltpu.VMEM((ni, PT, D), BF16),
            pltpu.VMEM((n_t, D, f2), BF16),
            pltpu.VMEM((2, len(caps), widest, D), BF16),
            pltpu.VMEM((2, len(caps), widest, D), BF16),
            pltpu.VMEM((n_dev, 16, 128), F32),
            pltpu.VMEM((n_t, hc), F32),
            pltpu.VMEM((n_t, hc), F32),
            dma((2, n_t)),
            dma((2, n_t)),
            dma((2, n_t, n_p)),
            dma((2, n_t, n_p)),
            dma((2, len(caps))),
            dma((2, len(caps))),
            dma((6,)),
            dma((6,)),
            dma((n_t + n_p,)),
            dma((n_t + n_p,)),
            dma((2,)),
            dma((5,)),
            dma((4, ni)),
        ],
        compiler_params=params(collective_id=0, has_side_effects=True),
        cost_estimate=pl.CostEstimate(
            flops=2 * m * D * f2 * n_t,
            bytes_accessed=2 * n_t * D * f2 + 12 * m * D,
            transcendentals=m * PT * n_t * hh,
        ),
        name="gather_and_attend",
    )(counts, tokens, cotangent, small, halves)


def reduce_and_attend_back(
    counts, grad_hidden, attn_in, qkv, attended, lse, weights, mlp_grads, mlp_sums, residual, x, mixed, vectors, sums, fc1_sums, cfg
):
    n_t, n_p, ni, hc, hh, f2, pd, m, imgs = (
        cfg.n_t, cfg.n_p, cfg.ni, cfg.hc, cfg.hh, cfg.f2, cfg.pd, cfg.m, cfg.imgs,
    )
    scale = HD**-0.5
    square = n_p == 4
    plane = (2, 2) if square else (n_p,)
    order = list(range(n_t))[::-1]
    jobs = [((k, k), k) for k in order[:-1]] + [((k, k - 1), None) for k in order[::2]]
    n_jobs = len(jobs)
    n_got = 2 if square else n_p - 1
    n_dev = 2 * n_p * n_t
    width = D // n_dev
    caps = list(cfg.caps.items())
    widest = max(size for _, size in caps)
    to_z = {}
    for n, (chunks, _) in enumerate(jobs):
        for part in range(2):
            if chunks[part] > 0:
                to_z[n, part] = len(to_z)

    def kernel(
        counts_ref, gh_ref, in_ref, qkv_ref, att_ref, lse_ref, w_ref, g_ref, msum_ref, res_ref, x_ref, mix_ref, vec_ref,
        sums_ref, fsum_ref,
        half_ref, mixed_ref, dtok_ref, small_ref, own_grads, in_other, got_z,
        gqkv, stage, held, got, got_2, got_step, total, out, dq, dv,
        images, sent, rows_got, x_in, block, res_in, other_in, parts, parts_p, parts_c, parts_t,
        stage_sem, held_sem, s_send, s_recv, t_send, t_recv, z_send, z_recv, r_send, r_recv, c_send, c_recv,
        v_send, v_recv, in_sem, out_sem, block_sem,
    ):
        p, core, z = (lax.axis_index(axis) for axis in ALL)
        py, px = p >> 1, p & 1
        pair = {"c": 1 - core}
        step = pl.program_id(0)
        layout = Layout(counts_ref, cfg)

        def pieces(n, part, *index):
            (chunks, k) = jobs[n]
            if k is None:
                return own_grads.at[(chunks[part], *index)]
            return g_ref.at[(*index, k, part)]

        def first_copies(n):
            if square:
                return [
                    remote(pieces(n, 0, slice(None), px ^ 1), got.at[n, 0], (s_send, s_recv), (n, 0, 0), {"p": p ^ 1}),
                    remote(pieces(n, 1, py ^ 1, slice(None)), got.at[n, 1], (s_send, s_recv), (n, 1, 0), {"p": p ^ 2}),
                ]
            return [
                remote(pieces(n, part, p ^ q), got.at[n, part, q - 1], (s_send, s_recv), (n, part, q - 1), {"p": p ^ q})
                for part in range(2)
                for q in range(1, n_p)
            ]

        def second_copies(n):
            if not square:
                return []
            return [
                remote(got.at[n, 0, py ^ 1], got_2.at[n, 0], (t_send, t_recv), (n, 0), {"p": p ^ 2}),
                remote(got.at[n, 1, px ^ 1], got_2.at[n, 1], (t_send, t_recv), (n, 1), {"p": p ^ 1}),
            ]

        def z_copy(n, part):
            k = jobs[n][0][part]
            source = got.at[n, part, (py, px)[part] if square else 0]
            target = {"t": lax.rem(z - k + n_t, n_t)}
            index = to_z[n, part]
            if jobs[n][1] is not None:
                target = {"t": lax.rem(z - 1 + n_t, n_t)}
                return remote(source, got_step.at[index], (z_send, z_recv), index, target)
            return remote(source, got_z.at[index], (z_send, z_recv), index, target)

        def loads(n):
            if square:
                sources = [pieces(n, 0, slice(None), px), pieces(n, 1, py, slice(None))]
            else:
                sources = [pieces(n, 0, p), pieces(n, 1, p)]
            return [
                pltpu.make_async_copy(
                    source, held.at[n % 2, part] if square else held.at[n % 2, part, 0], held_sem.at[n % 2, part]
                )
                for part, source in enumerate(sources)
            ]

        def begin(n):
            for copy in first_copies(n):
                copy.start()

        def fetch(n):
            for copy in loads(n):
                copy.start()

        def middle(n):
            for copy in loads(n):
                copy.wait()
            for copy in first_copies(n):
                copy.wait_recv()
            if square:
                for part, here in enumerate((py, px)):
                    there = here ^ 1
                    both = held[n % 2, part, there].astype(F32) + got[n, part, there].astype(F32)
                    got[n, part, there] = both.astype(BF16)
                for copy in second_copies(n):
                    copy.start()

        def last(n):
            for copy in second_copies(n):
                copy.wait_recv()
            chunks, k = jobs[n]
            for part, here in enumerate((py, px)):
                if square:
                    whole = held[n % 2, part, here].astype(F32) + got[n, part, here].astype(F32)
                    whole = whole + got_2[n, part].astype(F32)
                else:
                    whole = held[n % 2, part, 0].astype(F32)
                    for q in range(n_p - 1):
                        whole = whole + got[n, part, q].astype(F32)
                if k is not None and k < n_t - 1:
                    z_copy(n - 1, part).wait_recv()
                    whole = whole + got_step[to_z[n - 1, part]].astype(F32)
                if chunks[part] == 0:
                    total[0] = whole
                else:
                    got[n, part, here if square else 0] = whole.astype(BF16)
                    z_copy(n, part).start()

        def tick(n):
            middle(n)
            if n > 0:
                last(n - 1)
                if n + 1 < n_jobs:
                    fetch(n + 1)
            if n + 2 < n_jobs:
                begin(n + 2)

        def sums_copy():
            return pltpu.make_async_copy(msum_ref, total.at[pl.ds(1, 2)], stage_sem.at[1])

        def finish():
            for s, (shift, _) in enumerate(caps):

                @pl.when(layout.has(z - shift))
                def _(s=s):
                    row_copy(1, s).wait_send()

            for n in range(n_jobs):
                for copy in first_copies(n) + second_copies(n):
                    copy.wait_send()
                for part in range(2):
                    if (n, part) in to_z:
                        z_copy(n, part).wait_send()
                        if jobs[n][1] is None:
                            z_copy(n, part).wait_recv()
            direct = [(n, part) for n, part in to_z if jobs[n][1] is None]
            reads = [
                pltpu.make_async_copy(got_z.at[to_z[spot]], got.at[(*spot, 0)], z_recv.at[to_z[spot]])
                for spot in direct
            ]
            for read in reads:
                read.start()
            for read in reads:
                read.wait()
            whole = total[0]
            for spot in direct:
                whole = whole + got[(*spot, 0)].astype(F32)
            total[0] = whole
            sums_copy().wait()
            for part in range(2):
                z_copy(n_t - 2, part).wait_recv()
                total[1 + part] += got_step[to_z[n_t - 2, part]].astype(F32)

            def rows(member):
                return total.at[:, pl.ds(pl.multiple_of(member * pd, 16), pd), :]

            kept = pltpu.make_async_copy(rows(core), half_ref.at[core], out_sem)
            traded = remote(rows(1 - core), half_ref.at[core], (c_send, c_recv), 1, pair)
            kept.start()
            traded.start()
            kept.wait()
            traded.wait()
            block_store(1).wait()

        def row_copy(which, s):
            shift, size = caps[s]
            return remote(
                sent.at[s, pl.ds(0, size)], rows_got.at[which, s, pl.ds(0, size)], (r_send, r_recv), (which, s),
                {"t": jnp.clip(z - shift, 0, n_t - 1)},
            )

        def of_images(positions, valid):
            rows = None
            for i in range(imgs):
                spots = positions - i * TOK_IMG
                spots = jnp.where(valid & (spots >= 0) & (spots < TOK_IMG), spots, -1)
                picked = dot(one_hot(spots, PT), images[i])
                rows = picked if rows is None else rows + picked
            return rows.astype(BF16)

        def send_rows(which):
            for s, (shift, size) in enumerate(caps):

                @pl.when(layout.has(z - shift))
                def _(s=s, shift=shift, size=size):
                    if which == 1:
                        row_copy(0, s).wait_send()
                    want = layout.window_back(z, z - shift, size) + row_ids(size)
                    sent[s, :size] = of_images(want, want >= 0)
                    row_copy(which, s).start()

        def block_store(which):
            return pltpu.make_async_copy(block, (mixed_ref, dtok_ref)[which], block_sem)

        def take_rows(which):
            if which == 1:
                block_store(0).wait()
            row = row_ids(-(-cfg.block // 16) * 16)
            position = layout.start(z) + row
            valid = position < layout.end(z)
            block[...] = of_images(position - cfg.rows * z, valid)[: cfg.block]
            for s, (shift, size) in enumerate(caps):
                source = z + shift

                @pl.when(layout.has(source))
                def _(s=s, size=size, source=source):
                    row_copy(which, s).wait_recv()
                    local = position - cfg.rows * source
                    mine = valid & (local >= 0) & (local < cfg.rows)
                    spots = jnp.where(mine, local - layout.window_back(source, z, size), -1)
                    block[...] += dot(one_hot(spots, size), rows_got[which, s, :size]).astype(BF16)[: cfg.block]

            block_store(which).start()

        device = (2 * p + core) * n_t + z

        def gather_parts(gain, shift):
            parts[...] = jnp.zeros_like(parts)
            rows = [gain, sums_ref[0:1, :], shift, sums_ref[1:2, :], sums_ref[2:3, :], sums_ref[3:4, :]]
            for d in range(n_dev):
                cols = slice(d * width, (d + 1) * width)
                for r, value in zip((0, 1, 2, 3, 6, 7), rows):
                    parts[d, r : r + 1, :width] = value[:, cols]
            for k in range(n_t):
                chunk = 2 * lax.rem(z - k + n_t, n_t) + core
                for j in range(hc // width):
                    cols = slice(j * width, (j + 1) * width)
                    owner = chunk * (hc // width) + j
                    parts[owner, 4:5, :width] = dq[k : k + 1, cols]
                    parts[owner, 5:6, :width] = dv[k : k + 1, cols]
                for j in range(f2 // (4 * width)):
                    owner = chunk * (f2 // (4 * width)) + j
                    for r in range(4):
                        begin_at = (4 * j + r) * width
                        parts[owner, 8 + r : 9 + r, :width] = fsum_ref[k, :, begin_at : begin_at + width]

        def plane_parts(index):
            return pl.ds(2 * index * n_t, 2 * n_t)

        def core_parts(member):
            return pl.ds((2 * p + member) * n_t, n_t)

        def part_copies(hop):
            if hop == 0:
                return [
                    remote(parts.at[plane_parts(p ^ q)], parts_p.at[q - 1], (v_send, v_recv), q - 1, {"p": p ^ q})
                    for q in range(1, n_p)
                ]
            if hop == 1:
                return [remote(parts.at[core_parts(1 - core)], parts_c, (v_send, v_recv), n_p - 1, pair)]
            copies = []
            for k in range(1, n_t):
                to = lax.rem(z + k, n_t)
                source = parts.at[(2 * p + core) * n_t + to]
                copies.append(remote(source, parts_t.at[k], (v_send, v_recv), n_p - 1 + k, {"t": to}))
            return copies

        def part_hop(hop):
            if hop > 0:
                for copy in part_copies(hop - 1):
                    copy.wait()
            if hop == 1:
                for q in range(n_p - 1):
                    parts[plane_parts(p)] += parts_p[q]
            if hop == 2:
                parts[core_parts(core)] += parts_c[...]
            if hop == 3:
                mine = parts[device]
                for k in range(1, n_t):
                    mine = mine + parts_t[k]
                small_ref[...] = mine
            if hop < 3:
                for copy in part_copies(hop):
                    copy.start()

        def in_copy():
            return remote(out.at[pl.ds(imgs, imgs)], in_other, (c_send, c_recv), 0, pair)

        def first_norm_back():
            in_copy().wait()
            gain, shift = jnp.zeros((1, D), F32), jnp.zeros((1, D), F32)
            half = PT // 2
            for i in range(imgs):
                for begin_at in (0, half):
                    some = pl.ds(begin_at, half)
                    reads = [
                        pltpu.make_async_copy(res_ref.at[i, some], res_in, in_sem.at[0]),
                        pltpu.make_async_copy(in_other.at[i, some], other_in, in_sem.at[1]),
                        pltpu.make_async_copy(x_ref.at[i, some], x_in, in_sem.at[2]),
                    ]
                    for read in reads:
                        read.start()
                    for read in reads:
                        read.wait()
                    up = out[i, begin_at : begin_at + half] + other_in[...]
                    normed, inverse = norm(x_in[...].astype(F32))
                    grad = res_in[...] + norm_back(up, normed, inverse, vec_ref[0:1, :])
                    images[i, begin_at : begin_at + half] = grad.astype(BF16)
                    gain = gain + jnp.sum(up * normed, axis=0, keepdims=True)
                    shift = shift + jnp.sum(up, axis=0, keepdims=True)
            gather_parts(gain, shift)

        @pl.when(step == 0)
        def _():
            sums_copy().start()
            fetch(0)
            fetch(1)
            read = pltpu.make_async_copy(mix_ref, images, in_sem.at[0])
            read.start()
            enter(cfg)
            begin(0)
            begin(1)
            read.wait()
            send_rows(0)

        keyed = lax.broadcasted_iota(jnp.int32, (PT, PT), 1) < TOK_IMG
        total_q, total_v = jnp.zeros((1, hc), F32), jnp.zeros((1, hc), F32)
        for i in range(ni):
            grad_att = dot(gh_ref[i], w_ref[0, :, 3 * hc :]).astype(BF16)
            sums_q, sums_v = [], []
            for h in range(hh):
                cols = slice(h * HD, (h + 1) * HD)
                key_cols = slice(hc + h * HD, hc + (h + 1) * HD)
                value_cols = slice(2 * hc + h * HD, 2 * hc + (h + 1) * HD)
                query = qkv_ref[0, i, :, cols]
                keys = qkv_ref[0, i, :, key_cols]
                values = qkv_ref[0, i, :, value_cols]
                grad = grad_att[:, cols]
                scores = dot_nt(query, keys) * scale - lse_ref[0, i, :, h : h + 1]
                probs = jnp.exp(jnp.where(keyed, scores, NEG))
                delta = jnp.sum(
                    grad.astype(F32) * att_ref[0, i, :, cols].astype(F32), axis=-1, keepdims=True
                )
                grad_v = dot_tn(probs.astype(BF16), grad)
                grad_s = (probs * (dot_nt(grad, values) - delta) * scale).astype(BF16)
                grad_q = dot(grad_s, keys)
                grad_k = dot_tn(grad_s, query)
                sums_q.append(jnp.sum(grad_q, axis=0, keepdims=True))
                sums_v.append(jnp.sum(grad_v, axis=0, keepdims=True))
                gqkv[i, :, cols] = grad_q.astype(BF16)
                gqkv[i, :, key_cols] = grad_k.astype(BF16)
                gqkv[i, :, value_cols] = grad_v.astype(BF16)
            total_q = total_q + jnp.concatenate(sums_q, axis=1)
            total_v = total_v + jnp.concatenate(sums_v, axis=1)
            part = dot_nt(gqkv[i], w_ref[0, :, : 3 * hc])

            @pl.when(step == 0)
            def _(i=i, part=part):
                out[i] = part

            @pl.when(step > 0)
            def _(i=i, part=part):
                out[i] += part

            for n in range(n_t - 2):
                if i == min(2 * n + 1, ni - 1):

                    @pl.when(step == n + 1)
                    def _(n=n):
                        tick(n)

        dq[pl.ds(n_t - 1 - step, 1), :] = total_q
        dv[pl.ds(n_t - 1 - step, 1), :] = total_v

        @pl.when(step == n_t - 1)
        def _():
            in_copy().start()

        for side in range(2):
            cols = slice(side * D // 2, (side + 1) * D // 2)
            ahead = (side,) if square else (slice(side * n_p // 2, (side + 1) * n_p // 2),)
            ahead = ahead + (slice(None),) * len(plane)
            for lhs, rhs, lanes in (
                (in_ref, gqkv[...].reshape(m, 3 * hc), slice(0, 3 * hc)),
                (gh_ref, att_ref[0].reshape(m, hc), slice(3 * hc, f2)),
            ):
                value = dot_tn(lhs[:, :, cols].reshape(m, D // 2), rhs).astype(BF16)
                stage[(*ahead, lanes)] = value.reshape(
                    (n_p // 2, 2 * pd, lanes.stop - lanes.start)
                )
        store = pltpu.make_async_copy(stage, own_grads.at[n_t - 1 - step], stage_sem.at[0])
        store.start()
        store.wait()

        @pl.when(step == n_t - 2)
        def _():
            take_rows(0)

        @pl.when(step == n_t - 1)
        def _():
            tick(n_t - 2)
            first_norm_back()
            send_rows(1)
            part_hop(0)
            tick(n_t - 1)
            part_hop(1)
            for n in range(n_t, n_jobs - 1):
                tick(n)
            part_hop(2)
            tick(n_jobs - 1)
            last(n_jobs - 1)
            take_rows(1)
            part_hop(3)
            finish()

    dma = pltpu.SemaphoreType.DMA
    chunk = (2 * pd, f2)
    vmem = pltpu.VMEM

    def chunk_block(last):
        return pl.BlockSpec((1, ni, PT, last), lambda k: (n_t - 1 - k, 0, 0, 0))

    anywhere = pl.BlockSpec(memory_space=pl.ANY)
    shape = jax.ShapeDtypeStruct
    n_v = n_p - 1 + n_t
    outs = pl.pallas_call(
        kernel,
        grid=(n_t,),
        in_specs=[
            pl.BlockSpec(memory_space=pltpu.SMEM),
            fixed((ni, PT, D)),
            fixed((ni, PT, D)),
            chunk_block(3 * hc),
            chunk_block(hc),
            chunk_block(hh),
            pl.BlockSpec((1, D, f2), lambda k: (n_t - 1 - k, 0, 0)),
            anywhere,
            anywhere,
            anywhere,
            anywhere,
            anywhere,
            fixed((8, D)),
            fixed((4, D)),
            fixed((n_t, 1, f2)),
        ],
        out_specs=[anywhere] * 3 + [fixed((16, 128))] + [anywhere] * 3,
        out_shape=[
            shape((2, 3, pd, f2), F32),
            shape((cfg.block, D), BF16),
            shape((cfg.block, D), BF16),
            shape((16, 128), F32),
            shape((n_t, *plane, *chunk), BF16),
            shape((imgs, PT, D), F32),
            shape((len(to_z), *chunk), BF16),
        ],
        scratch_shapes=[
            vmem((ni, PT, 3 * hc), BF16),
            vmem((*plane, *chunk), BF16),
            vmem((2, 2, 2 if square else 1, *chunk), BF16),
            vmem((n_jobs, 2, n_got, *chunk), BF16),
            vmem((n_jobs, 2, *(chunk if square else (16, 128))), BF16),
            vmem((2 * (n_t - 1), *chunk), BF16),
            vmem((3, *chunk), F32),
            vmem((ni, PT, D), F32),
            vmem((n_t, hc), F32),
            vmem((n_t, hc), F32),
            vmem((imgs, PT, D), BF16),
            vmem((len(caps), widest, D), BF16),
            vmem((2, len(caps), widest, D), BF16),
            vmem((PT // 2, D), BF16),
            vmem((cfg.block, D), BF16),
            vmem((PT // 2, D), F32),
            vmem((PT // 2, D), F32),
            vmem((n_dev, 16, 128), F32),
            vmem((n_p - 1, 2 * n_t, 16, 128), F32),
            vmem((n_t, 16, 128), F32),
            vmem((n_t, 16, 128), F32),
            dma((2,)),
            dma((2, 2)),
            dma((n_jobs, 2, 1 if square else n_p - 1)),
            dma((n_jobs, 2, 1 if square else n_p - 1)),
            dma((n_jobs, 2)),
            dma((n_jobs, 2)),
            dma((len(to_z),)),
            dma((len(to_z),)),
            dma((2, len(caps))),
            dma((2, len(caps))),
            dma((2,)),
            dma((2,)),
            dma((n_v,)),
            dma((n_v,)),
            dma((3,)),
            dma,
            dma,
        ],
        compiler_params=params(collective_id=1, has_side_effects=True),
        cost_estimate=pl.CostEstimate(
            flops=4 * m * D * f2 * n_t + 10 * m * PT * HD * n_t * hh,
            bytes_accessed=4 * n_t * D * f2 + 20 * m * D,
            transcendentals=m * PT * n_t * hh,
        ),
        name="reduce_and_attend_back",
    )(
        counts,
        grad_hidden,
        attn_in,
        qkv,
        attended,
        lse,
        weights,
        mlp_grads,
        mlp_sums,
        residual,
        x,
        mixed,
        vectors,
        sums,
        fc1_sums,
    )
    return outs[:4]


def mlp_pass(hidden, mlp_in, vectors, cot, fc1, weights, cfg):
    n_p, n_t, m, pd, w, ni, imgs = cfg.n_p, cfg.n_t, cfg.m, cfg.pd, cfg.f2, cfg.ni, cfg.imgs
    early = cfg.early
    square = n_p == 4
    plane = (2, 2) if square else (n_p,)
    piece = (2 * pd, w)

    def kernel(
        hidden_ref, mlp_in, vec_ref, cot_ref, fc1_ref, g_ref,
        sum_ref, grad_ref, plane_ref, res_ref, gh_ref, sums_ref, mixed_ref, late_ref,
        other, other_y, act_all, gpre_all, back, y, gh, w_all, stage, held, got, got_2,
        c_send, c_recv, own_sem, load_sem, keep_sem, z_send, z_recv, p_send, p_recv,
        stage_sem, s_send, s_recv, t_send, t_recv,
    ):
        step = pl.program_id(0)
        p, z = lax.axis_index("p"), lax.axis_index("t")
        pair = {"c": 1 - lax.axis_index("c")}

        def rows(mask):
            return pl.ds(pl.multiple_of((p ^ mask) * 2 * pd, 16), 2 * pd)

        def own_rows(j):
            return g_ref.at[:, early, rows(0), :] if j == 0 else late_ref.at[:, j, rows(0), :]

        def keep():
            return pltpu.make_async_copy(own_rows(0), late_ref.at[:, 0, rows(0), :], keep_sem)

        def z_copy(j):
            target = {"t": lax.rem(z + 1, n_t)}
            return remote(own_rows(j - 1), own_rows(j), (z_send, z_recv), j, target)

        def p_copy(j, mask):
            target = late_ref.at[:, j, rows(0), :]
            return remote(own_rows(j), target, (p_send, p_recv), (j, mask), {"p": p ^ mask})

        def d_copies(j):
            if n_p != 4:
                return []
            ref_1, ref_2 = late_ref.at[0, j, rows(1), :], late_ref.at[1, j, rows(2), :]
            return [
                remote(ref_1, ref_1, (p_send, p_recv), (j, 3), {"p": p ^ 2}),
                remote(ref_2, ref_2, (p_send, p_recv), (j, 0), {"p": p ^ 1}),
            ]

        direct = (1, 2) if n_p == 4 else tuple(range(1, n_p))

        def send_p(j):
            if j > 0:
                z_copy(j).wait_recv()
            if early + j + 1 < n_t:
                z_copy(j + 1).start()
            for mask in direct:
                p_copy(j, mask).start()

        def send_d(j):
            for mask in direct:
                p_copy(j, mask).wait_recv()
            for copy in d_copies(j):
                copy.start()
            if early + j + 1 < n_t:
                send_p(j + 1)

        def complete(j):
            if j == 0:
                keep().wait()
            for copy in d_copies(j):
                copy.wait_recv()

        def load(k):
            source = g_ref.at[:, k] if k < early else late_ref.at[:, k - early]
            return pltpu.make_async_copy(source, w_all.at[k % 2], load_sem.at[k % 2])
        mine, theirs = pl.ds(0, imgs), pl.ds(imgs, imgs)

        def pair_copy(index, source, target):
            return remote(source, target, (c_send, c_recv), index, pair)

        def back_copy():
            return pair_copy(0, back.at[theirs], other)

        def y_copy():
            return pair_copy(1, y.at[theirs], other_y)

        py, px = p >> 1, p & 1

        def first_copies():
            if square:
                return [
                    remote(grad_ref.at[:, px ^ 1, 0, 0], got.at[0], (s_send, s_recv), (0, 0), {"p": p ^ 1}),
                    remote(grad_ref.at[py ^ 1, :, 0, 1], got.at[1], (s_send, s_recv), (1, 0), {"p": p ^ 2}),
                ]
            return [
                remote(grad_ref.at[p ^ q, 0, part], got.at[part, q - 1], (s_send, s_recv), (part, q - 1), {"p": p ^ q})
                for part in range(2)
                for q in range(1, n_p)
            ]

        def second_copies():
            if not square:
                return []
            return [
                remote(got.at[0, py ^ 1], got_2.at[0], (t_send, t_recv), 0, {"p": p ^ 2}),
                remote(got.at[1, px ^ 1], got_2.at[1], (t_send, t_recv), 1, {"p": p ^ 1}),
            ]

        def middle():
            for copy in first_copies():
                copy.wait_recv()
            if square:
                for part, here in enumerate((py, px)):
                    both = held[part, here ^ 1].astype(F32) + got[part, here ^ 1].astype(F32)
                    got[part, here ^ 1] = both.astype(BF16)
                for copy in second_copies():
                    copy.start()

        def last():
            for copy in second_copies():
                copy.wait_recv()
            for part, here in enumerate((py, px)):
                if square:
                    whole = held[part, here].astype(F32) + got[part, here].astype(F32)
                    whole = whole + got_2[part].astype(F32)
                else:
                    whole = held[part, 0].astype(F32)
                    for q in range(n_p - 1):
                        whole = whole + got[part, q].astype(F32)
                plane_ref[part] = whole
            for copy in first_copies() + second_copies():
                copy.wait_send()

        def stage_copy(k):
            ahead = (slice(None),) * len(plane)
            return pltpu.make_async_copy(stage, grad_ref.at[(*ahead, k)], stage_sem)

        @pl.when(step == 0)
        def _():
            pltpu.make_async_copy(hidden_ref, res_ref, own_sem).start()
            keep().start()
            for k in range(min(2, early)):
                load(k).start()
            enter(cfg)
            send_p(0)
        slot = lax.rem(step, 2)
        for k in range(n_t):

            @pl.when(step == k)
            def _(k=k):
                load(k).wait()

        w1, w2 = w_all[slot, 0], w_all[slot, 1]
        total = jnp.zeros((1, w), F32)
        for i in range(ni):
            rows_i = slice(i * PT, (i + 1) * PT)
            pre = dot(mlp_in[i], w1) + fc1_ref[0]
            phi = 0.5 * (1.0 + lax.erf(pre * (1.0 / math.sqrt(2.0))))
            act_all[rows_i, :] = (pre * phi).astype(BF16)
            slope = phi + pre * jnp.exp(-0.5 * pre * pre) * (1.0 / math.sqrt(2.0 * math.pi))
            gpre = dot(cot_ref[i], w2) * slope
            total = total + jnp.sum(gpre, axis=0, keepdims=True)
            gpre_all[rows_i, :] = gpre.astype(BF16)
        sum_ref[0] = total

        def add(target, left, right):
            value = dot_nt(left, right).reshape(ni, PT, D)

            @pl.when(step == 0)
            def _():
                target[...] = value

            @pl.when(step > 0)
            def _():
                target[...] += value

        add(back, gpre_all[...], w1)

        for j in range(1, n_t - early):

            @pl.when(step == early - 1 + j)
            def _(j=j):
                send_d(j)

        @pl.when(step == n_t - 2)
        def _():
            for copy in first_copies():
                copy.start()

        @pl.when(step == n_t - 1)
        def _():
            back_copy().start()

        add(y, act_all[...], w2)

        @pl.when(step == n_t - 1)
        def _():
            y_copy().start()

        @pl.when(step > 0)
        def _():
            stage_copy(0).wait()

        ahead = (slice(None),) * len(plane)
        grad_1 = dot_tn(mlp_in[...].reshape(m, D), gpre_all[...]).astype(BF16)
        stage[(*ahead, 0)] = grad_1.reshape((*plane, *piece))
        grad_2 = dot_tn(cot_ref[...].reshape(m, D), act_all[...]).astype(BF16)
        stage[(*ahead, 1)] = grad_2.reshape((*plane, *piece))
        stage_copy(step).start()

        @pl.when(step == 0)
        def _():
            if square:
                held[0] = stage[:, px, 0]
                held[1] = stage[py, :, 1]
            else:
                held[0, 0] = stage[p, 0]
                held[1, 0] = stage[p, 1]

        @pl.when(step == n_t - 1)
        def _():
            middle()

        @pl.when(step == early - 2)
        def _():
            send_d(0)

        for k in range(2, n_t):

            @pl.when(step == k - 1)
            def _(k=k):
                if k >= early:
                    complete(k - early)
                load(k).start()

        @pl.when(step == n_t - 1)
        def _():
            pltpu.make_async_copy(hidden_ref, res_ref, own_sem).wait()
            back_copy().wait()
            sums = [jnp.zeros((1, D), F32)] * 4
            for i in range(imgs):
                up = back[i] + other[i]
                hidden = res_ref[i]
                other[i] = hidden
                normed, inverse = norm(hidden)
                cot_f = cot_ref[i].astype(F32)
                grad = cot_f + norm_back(up, normed, inverse, vec_ref[1:2, :])
                res_ref[i] = grad
                gh[i] = grad.astype(BF16)
                terms = (up * normed, up, grad, cot_f)
                sums = [s + jnp.sum(t, axis=0, keepdims=True) for s, t in zip(sums, terms)]
            grad_copy = pair_copy(2, gh.at[mine], gh.at[theirs])
            grad_copy.start()
            for r in range(4):
                sums_ref[r : r + 1, :] = sums[r]
            y_copy().wait()
            for i in range(imgs):
                mixed_ref[i] = (other[i] + (y[i] + other_y[i]) + vec_ref[7:8, :]).astype(BF16)
            grad_copy.wait()
            store = pltpu.make_async_copy(gh, gh_ref, own_sem)
            store.start()
            last()
            stage_copy(0).wait()
            for j in range(n_t - early):
                for copy in d_copies(j):
                    copy.wait_send()
                for mask in direct:
                    p_copy(j, mask).wait_send()
                if j > 0:
                    z_copy(j).wait_send()
            store.wait()

    full = fixed((ni, PT, D))
    own = fixed((imgs, PT, D))
    shape, vmem, dma = jax.ShapeDtypeStruct, pltpu.VMEM, pltpu.SemaphoreType.DMA
    return pl.pallas_call(
        kernel,
        grid=(n_t,),
        in_specs=[
            pl.BlockSpec(memory_space=pl.ANY),
            full,
            fixed((8, D)),
            full,
            pl.BlockSpec((1, 1, w), lambda i: (i, 0, 0)),
            pl.BlockSpec(memory_space=pl.ANY),
        ],
        out_specs=[
            pl.BlockSpec((1, 1, w), lambda i: (i, 0, 0)),
            pl.BlockSpec(memory_space=pl.ANY),
            fixed((2, *piece)),
            own,
            pl.BlockSpec(memory_space=pl.ANY),
            fixed((4, D)),
            own,
            pl.BlockSpec(memory_space=pl.ANY),
        ],
        out_shape=[
            shape((n_t, 1, w), F32),
            shape((*plane, n_t, 2, *piece), BF16),
            shape((2, *piece), F32),
            shape((imgs, PT, D), F32),
            shape((ni, PT, D), BF16),
            shape((4, D), F32),
            shape((imgs, PT, D), BF16),
            shape((2, n_t - early, D, w), BF16),
        ],
        scratch_shapes=[
            vmem((imgs, PT, D), F32),
            vmem((imgs, PT, D), F32),
            vmem((m, w), BF16),
            vmem((m, w), BF16),
            vmem((ni, PT, D), F32),
            vmem((ni, PT, D), F32),
            vmem((ni, PT, D), BF16),
            vmem((2, 2, D, w), BF16),
            vmem((*plane, 2, *piece), BF16),
            vmem((2, 2 if square else 1, *piece), BF16),
            vmem((2, 2 if square else n_p - 1, *piece), BF16),
            vmem((2, *(piece if square else (16, 128))), BF16),
            dma((3,)),
            dma((3,)),
            dma,
            dma((2,)),
            dma,
            dma((n_t - early,)),
            dma((n_t - early,)),
            dma((n_t - early, n_p)),
            dma((n_t - early, n_p)),
            dma,
            dma((2, 1 if square else n_p - 1)),
            dma((2, 1 if square else n_p - 1)),
            dma((2,)),
            dma((2,)),
        ],
        compiler_params=params(collective_id=2, has_side_effects=True),
        cost_estimate=pl.CostEstimate(
            flops=12 * m * D * w * n_t,
            bytes_accessed=12 * m * D + 8 * D * w * n_t,
            transcendentals=2 * m * w * n_t,
        ),
        name="mlp_pass",
    )(hidden, mlp_in, vectors, cot, fc1.reshape(n_t, 1, w), weights)[:-1]


def body(cfg, tokens, counts, gains, biases, fc1_bias, w_qkv, w_o, w_1, w_2, cotangent):
    pd, f2, hc = cfg.pd, cfg.f2, cfg.hc
    halves = jnp.stack(
        [
            jnp.concatenate(
                [
                    w_qkv.reshape(pd, 3, 2, hc).transpose(2, 0, 1, 3).reshape(2, pd, 3 * hc),
                    w_o.T.reshape(pd, 2, hc).transpose(1, 0, 2),
                ],
                axis=2,
            ),
            w_1.reshape(pd, 2, f2).transpose(1, 0, 2),
            w_2.T.reshape(pd, 2, f2).transpose(1, 0, 2),
        ],
        axis=1,
    )
    small = jnp.concatenate([gains, biases, fc1_bias.reshape(4, -1)])
    small = jnp.pad(small, ((0, 4), (0, 128 - small.shape[1])))

    x, cot, attn_in, qkv, attended, lse, hidden, mlp_in, vectors, fc1, attn_w, mlp_w = gather_and_attend(
        counts, tokens, cotangent, small, halves, cfg
    )
    fc1_sums, mlp_grads, mlp_sums, residual, grad_hidden, sums, mixed = mlp_pass(
        hidden, mlp_in, vectors, cot, fc1, mlp_w, cfg
    )
    both, mixed, d_tokens, small = reduce_and_attend_back(
        counts, grad_hidden, attn_in, qkv, attended, lse, attn_w, mlp_grads, mlp_sums, residual, x, mixed,
        vectors, sums, fc1_sums, cfg,
    )
    d_qkv = both[:, 0, :, : 3 * hc].reshape(2, pd, 3, hc).transpose(1, 2, 0, 3).reshape(pd, 3, 2 * hc)
    d_o = both[:, 0, :, 3 * hc :].transpose(0, 2, 1).reshape(2 * hc, pd)
    d_1 = both[:, 1].transpose(1, 0, 2).reshape(pd, 2 * f2)
    d_2 = both[:, 2].transpose(0, 2, 1).reshape(2 * f2, pd)
    piece = D // (cfg.n_dp * cfg.n_t)
    small = small[:, :piece]
    return (
        mixed,
        d_tokens,
        d_qkv,
        d_o,
        d_1,
        d_2,
        small[:2],
        small[2:8],
        small[8:12].reshape(-1),
    )


def solution(mesh):
    n_dp, n_t = mesh.shape["dp"], mesh.shape["tensor"]
    split = Mesh(mesh.devices.reshape(n_dp // 2, 2, n_t), ALL)

    def program(tokens, *rest):
        cfg = Cfg(n_dp, n_t, tokens.shape[0])
        return body(cfg, tokens, *rest)

    dp = ("p", "c")
    return jax.shard_map(
        program,
        mesh=split,
        in_specs=(
            P(ALL, None),
            P(dp, None),
            P(None, ALL),
            P(None, ALL),
            P(ALL),
            P(dp, None, "t"),
            P("t", dp),
            P(dp, "t"),
            P("t", dp),
            P(ALL, None),
        ),
        out_specs=(
            P(ALL, None),
            P(ALL, None),
            P(dp, None, "t"),
            P("t", dp),
            P(dp, "t"),
            P("t", dp),
            P(None, ALL),
            P(None, ALL),
            P(ALL),
        ),
        check_vma=False,
    )
```

```python
import math

import jax
import jax.numpy as jnp
from jax import lax
from jax.experimental import pallas as pl
from jax.experimental.pallas import tpu as pltpu
from jax.sharding import Mesh
from jax.sharding import PartitionSpec as P

D = 1280
HD = 80
HEADS = 16
FF = 5120
TOK_IMG = 257
IMG_DEV = 8
TOTAL = IMG_DEV * TOK_IMG
EPS = 1e-06
PT = 272
F32 = jnp.float32
BF16 = jnp.bfloat16
NEG = -1e30
VMEM_LIMIT = 61 * 1024 * 1024


class Cfg:
    def __init__(self, n_dp, n_t, block_rows):
        self.n_dp, self.n_t, self.block = n_dp, n_t, block_rows
        self.n_p = n_dp // 2
        self.imgs = IMG_DEV // n_t
        self.ni = 2 * self.imgs
        self.rows = self.imgs * TOK_IMG
        self.m = self.ni * PT
        self.pd = D // n_dp
        self.hh = HEADS // n_t // 2
        self.hc = self.hh * HD
        self.f2 = FF // n_t // 2
        assert 4 * self.hc == self.f2
        self.early = n_t // 2
        self.caps = self._caps()

    def _caps(self):
        n, b, r = self.n_t, self.block, self.rows
        low = [max(t, TOTAL - (n - t) * b) for t in range(n + 1)]
        high = [min(t * b, TOTAL - (n - t)) for t in range(n + 1)]
        caps = {}
        for t in range(n):
            for dest in range(n):
                size = min(high[t + 1], r * (dest + 1)) - max(low[t], r * dest)
                size = min(size, b, r)
                if size > 0 and dest != t:
                    caps[dest - t] = max(caps.get(dest - t, 0), size)
        return {s: min(-(-c // 16) * 16, b) for s, c in sorted(caps.items())}


def dot(a, b):
    return lax.dot_general(a, b, (((1,), (0,)), ((), ())), preferred_element_type=F32)


def dot_nt(a, b):
    return lax.dot_general(a, b, (((1,), (1,)), ((), ())), preferred_element_type=F32)


def dot_tn(a, b):
    return lax.dot_general(a, b, (((0,), (0,)), ((), ())), preferred_element_type=F32)


def norm(values):
    mean = jnp.mean(values, axis=-1, keepdims=True)
    centred = values - mean
    spread = jnp.mean(centred * centred, axis=-1, keepdims=True)
    inverse = lax.rsqrt(spread + EPS)
    return centred * inverse, inverse


def norm_back(upstream, normed, inverse, gain):
    scaled = upstream * gain
    return inverse * (
        scaled
        - jnp.mean(scaled, axis=-1, keepdims=True)
        - normed * jnp.mean(scaled * normed, axis=-1, keepdims=True)
    )


ALL = ("p", "c", "t")


def params(**more):
    return pltpu.CompilerParams(vmem_limit_bytes=VMEM_LIMIT, **more)


def fixed(shape):
    return pl.BlockSpec(
        shape, lambda i, *s: (0,) * len(shape), pipeline_mode=pl.Buffered(1)
    )


MESH = pl.DeviceIdType.MESH


def enter(cfg):
    p, c, t = (lax.axis_index(axis) for axis in ALL)
    found = [{"c": 1 - c}]
    found += [{"t": lax.rem(t + k, cfg.n_t)} for k in range(1, cfg.n_t)]
    found += [{"p": p ^ m} for m in range(1, cfg.n_p)]
    barrier = pltpu.get_barrier_semaphore()
    for device in found:
        pl.semaphore_signal(barrier, inc=1, device_id=device, device_id_type=MESH)
    pl.semaphore_wait(barrier, len(found))


def remote(source, target, sems, index, device):
    return pltpu.make_async_remote_copy(
        src_ref=source,
        dst_ref=target,
        send_sem=sems[0].at[index],
        recv_sem=sems[1].at[index],
        device_id=device,
        device_id_type=MESH,
    )


class Layout:
    def __init__(self, counts_ref, cfg):
        self.counts, self.cfg = counts_ref, cfg
        self.z = lax.axis_index("t")

    def start(self, block):
        total = 0
        for j in range(self.cfg.n_t):
            total = total + jnp.where(block > j, self.counts[0, j], 0)
        return total

    def end(self, block):
        return self.start(block + 1)

    def has(self, block):
        return (block >= 0) & (block < self.cfg.n_t)

    def window(self, block, dest, size):
        return jnp.clip(self.cfg.rows * dest - self.start(block), 0, self.cfg.block - size)

    def window_back(self, dest, block, size):
        return jnp.clip(self.start(block) - self.cfg.rows * dest, 0, max(0, self.cfg.rows - size))


def one_hot(positions, limit):
    columns = lax.broadcasted_iota(jnp.int32, (positions.shape[0], limit), 1)
    return jnp.where(columns == positions, 1.0, 0.0).astype(BF16)


def row_ids(count):
    return lax.broadcasted_iota(jnp.int32, (count, 1), 0)


def gather_and_attend(counts, tokens, cotangent, small, halves, cfg):
    n_t, n_p, ni, hc, hh, f2, pd, imgs, m = (
        cfg.n_t, cfg.n_p, cfg.ni, cfg.hc, cfg.hh, cfg.f2, cfg.pd, cfg.imgs, cfg.m,
    )
    n_dev = 2 * n_p * n_t
    piece = D // n_dev
    caps = list(cfg.caps.items())
    widest = max(size for _, size in caps)

    def kernel(
        counts_ref, tok_ref, ct_ref, small_ref, half_ref,
        x_out, cot_out, in_out, qkv_out, att_out, lse_out, hidden_out, mlp_out, vec_ref, fc1_ref, g0_ref, g_ref,
        x_ref, cot_ref, in_ref, qkv_ref, att_ref, lse_ref, out_ref, other, mlp_in, w, sent, got, parts, q_bias, v_bias,
        z_send, z_recv, p_send, p_recv, r_send, r_recv, c_send, c_recv, v_send, v_recv, own_sem, out_sem, image_sem,
    ):
        p, core, z = (lax.axis_index(axis) for axis in ALL)
        layout = Layout(counts_ref, cfg)
        pair = {"c": 1 - core}

        def part_rows(plane, member):
            return pl.ds(pl.multiple_of((plane * 2 + member) * pd, 16), pd)

        def place(group, k, mask):
            rows = pl.ds(pl.multiple_of((p ^ mask) * 2 * pd, 16), 2 * pd)
            return w.at[k, rows, :] if group == 0 else g_ref.at[:, k, rows, :]

        def half(group, member):
            return half_ref.at[member, 0] if group == 0 else half_ref.at[member, pl.ds(1, 2)]

        def half_place(group):
            rows = part_rows(p, core)
            return w.at[0, rows, :] if group == 0 else g_ref.at[:, 0, rows, :]

        def keep(group):
            return pltpu.make_async_copy(half(group, core), half_place(group), own_sem.at[group])

        def trade(group):
            return remote(half(group, 1 - core), half_place(group), (c_send, c_recv), group, pair)

        def z_copy(group, k):
            target = {"t": lax.rem(z + 1, n_t)}
            return remote(place(group, k - 1, 0), place(group, k, 0), (z_send, z_recv), (group, k), target)

        def p_copy(group, k, mask):
            ref = place(group, k, 0)
            return remote(ref, ref, (p_send, p_recv), (group, k, mask), {"p": p ^ mask})

        def d_copies(group, k):
            if n_p != 4:
                return []

            def rows(mask):
                return pl.ds(pl.multiple_of((p ^ mask) * 2 * pd, 16), 2 * pd)

            if group == 0:
                via = 1 + k % 2
                ref = w.at[k, rows(via), :]
                return [remote(ref, ref, (p_send, p_recv), (group, k, 3), {"p": p ^ (3 - via)})]
            ref_1, ref_2 = g_ref.at[0, k, rows(1), :], g_ref.at[1, k, rows(2), :]
            return [
                remote(ref_1, ref_1, (p_send, p_recv), (group, k, 3), {"p": p ^ 2}),
                remote(ref_2, ref_2, (p_send, p_recv), (group, k, 0), {"p": p ^ 1}),
            ]

        direct = (1, 2) if n_p == 4 else tuple(range(1, n_p))

        def have_own(group):
            keep(group).wait()
            trade(group).wait()

        def send_p(group, k):
            for mask in direct:
                p_copy(group, k, mask).start()

        def send_z(group, k):
            if k > 1:
                z_copy(group, k - 1).wait_recv()
            z_copy(group, k).start()

        def send_d(group, k):
            for mask in direct:
                p_copy(group, k, mask).wait_recv()
            for copy in d_copies(group, k):
                copy.start()

        def finish(group, chunks):
            for k in chunks:
                for copy in d_copies(group, k):
                    copy.wait_recv()
                    copy.wait_send()
                for mask in direct:
                    p_copy(group, k, mask).wait_send()
            for k in range(1, n_t if group == 0 else cfg.early + 1):
                z_copy(group, k).wait_send()

        def row_copy(which, s):
            shift, size = caps[s]
            rows = pl.ds(0, size)
            return remote(
                sent.at[which, s, rows], got.at[which, s, rows], (r_send, r_recv), (which, s),
                {"t": jnp.clip(z + shift, 0, n_t - 1)},
            )

        def send_rows(which, block_ref):
            for s, (shift, size) in enumerate(caps):

                @pl.when(layout.has(z + shift))
                def _(s=s, shift=shift, size=size):
                    begin = layout.window(z, z + shift, size)
                    picked = dot(one_hot(begin + row_ids(size), cfg.block), block_ref[...])
                    sent[which, s, :size] = picked.astype(BF16)
                    row_copy(which, s).start()

        def take_rows(which, block_ref, images_ref):
            for i in range(imgs):
                row = row_ids(PT)
                position = cfg.rows * z + i * TOK_IMG + row
                valid = row < TOK_IMG
                mine = valid & (position < layout.end(z))
                spots = jnp.where(mine, position - layout.start(z), -1)
                images_ref[i] = dot(one_hot(spots, cfg.block), block_ref[...]).astype(BF16)
            for s, (shift, size) in enumerate(caps):
                source = z - shift

                @pl.when(layout.has(source))
                def _(s=s, size=size, source=source):
                    row_copy(which, s).wait_recv()
                    for i in range(imgs):
                        row = row_ids(PT)
                        position = cfg.rows * z + i * TOK_IMG + row
                        mine = (row < TOK_IMG) & (position < layout.end(source))
                        mine = mine & (position >= layout.start(source))
                        spots = position - layout.start(source) - layout.window(source, z, size)
                        picked = dot(one_hot(jnp.where(mine, spots, -1), size), got[which, s, :size])
                        images_ref[i] += picked.astype(BF16)

                @pl.when(layout.has(z + shift))
                def _(s=s):
                    row_copy(which, s).wait_send()

        def pair_rows(which, images_ref):
            mine, other = pl.ds(0, imgs), pl.ds(imgs, imgs)
            return remote(images_ref.at[mine], images_ref.at[other], (c_send, c_recv), 2 + which, pair)

        device = (2 * p + core) * n_t + z

        def part_copies(stage):
            if stage == 0:
                ref = parts.at[device]
                targets = [(k, {"t": lax.rem(z + k, n_t)}) for k in range(1, n_t)]
            elif stage == 1:
                ref = parts.at[pl.ds((2 * p + core) * n_t, n_t)]
                targets = [(n_t, pair)]
            else:
                ref = parts.at[pl.ds(2 * p * n_t, 2 * n_t)]
                targets = [(n_t + mask, {"p": p ^ mask}) for mask in range(1, n_p)]
            return [remote(ref, ref, (v_send, v_recv), index, target) for index, target in targets]

        def part_stage(stage):
            if stage > 0:
                for copy in part_copies(stage - 1):
                    copy.wait()
            if stage < 3:
                for copy in part_copies(stage):
                    copy.start()

        def spread():
            for d in range(n_dev):
                vec_ref[:, d * piece : (d + 1) * piece] = parts[d, :8, :piece]
            for k in range(n_t):
                block = 2 * lax.rem(z - k + n_t, n_t) + core
                for j in range(hc // piece):
                    cols = slice(j * piece, (j + 1) * piece)
                    owner = block * (hc // piece) + j
                    q_bias[k : k + 1, cols] = parts[owner, 4:5, :piece]
                    v_bias[k : k + 1, cols] = parts[owner, 5:6, :piece]
                for j in range(f2 // (4 * piece)):
                    owner = block * (f2 // (4 * piece)) + j
                    for r in range(4):
                        begin = (4 * j + r) * piece
                        fc1_ref[k : k + 1, begin : begin + piece] = parts[owner, 8 + r : 9 + r, :piece]

        for group in range(2):
            keep(group).start()
        parts[device] = small_ref[...]
        enter(cfg)
        for group in range(2):
            trade(group).start()
        part_stage(0)
        have_own(0)
        send_p(0, 0)
        send_z(0, 1)
        have_own(1)
        send_p(1, 0)
        send_rows(0, tok_ref)
        part_stage(1)
        send_d(0, 0)
        part_stage(2)
        z_last = n_t - 1
        for k in range(1, n_t):
            if k < z_last:
                send_z(0, k + 1)
            else:
                z_copy(0, k).wait_recv()
            if k == z_last - 1:
                send_z(1, 1)
            send_p(0, k)
            if k == 1:
                send_d(1, 0)
                part_stage(3)
                spread()
            else:
                send_d(0, k - 1)
            if k == z_last - 1:
                take_rows(0, tok_ref, x_ref)
                pair_rows(0, x_ref).start()
        send_d(0, z_last)
        steps = []
        for k in range(1, cfg.early + 1):
            if k < cfg.early:
                steps.append(lambda k=k: send_z(1, k + 1))
                steps.append(lambda k=k: send_p(1, k))
            else:
                steps.append(lambda k=k: z_copy(1, k).wait_recv())
            if k > 1:
                steps.append(lambda k=k: send_d(1, k - 1))
        for step in steps[:2]:
            step()
        steps = steps[2:]
        send_rows(1, ct_ref)
        pair_rows(0, x_ref).wait()
        finish(0, range(n_t))
        kept = pltpu.make_async_copy(w, g0_ref, out_sem.at[0])
        kept.start()
        x_copy = pltpu.make_async_copy(x_ref, x_out, out_sem.at[1])
        x_copy.start()
        early = len(steps)

        def image_copies(i):
            return [
                pltpu.make_async_copy(in_ref.at[i], in_out.at[i], image_sem.at[0, i]),
                pltpu.make_async_copy(qkv_ref.at[:, i], qkv_out.at[:, i], image_sem.at[1, i]),
                pltpu.make_async_copy(att_ref.at[:, i], att_out.at[:, i], image_sem.at[2, i]),
                pltpu.make_async_copy(lse_ref.at[:, i], lse_out.at[:, i], image_sem.at[3, i]),
            ]

        keyed = lax.broadcasted_iota(jnp.int32, (PT, PT), 1) < TOK_IMG

        mine, theirs = pl.ds(0, imgs), pl.ds(imgs, imgs)

        def out_copy():
            return remote(out_ref.at[theirs], other, (c_send, c_recv), 4, pair)

        def image(turn, carry):
            i = lax.rem(turn + imgs, ni)
            normed, _ = norm(x_ref[i].astype(F32))
            attn_in = (normed * vec_ref[0:1, :] + vec_ref[2:3, :]).astype(BF16)
            in_ref[i] = attn_in
            for k in range(n_t):
                qkv = dot(attn_in, w[k, :, : 3 * hc])
                query = (qkv[:, :hc] + q_bias[k : k + 1, :]).astype(BF16)
                keys = qkv[:, hc : 2 * hc].astype(BF16)
                values = (qkv[:, 2 * hc :] + v_bias[k : k + 1, :]).astype(BF16)
                qkv_ref[k, i, :, :hc] = query
                qkv_ref[k, i, :, hc : 2 * hc] = keys
                qkv_ref[k, i, :, 2 * hc :] = values
                for h in range(hh):
                    cols = slice(h * HD, (h + 1) * HD)
                    scores = dot_nt(query[:, cols], keys[:, cols]) * (HD**-0.5)
                    scores = jnp.where(keyed, scores, NEG)
                    top = jnp.max(scores, axis=-1, keepdims=True)
                    expo = jnp.exp(scores - top)
                    summed = jnp.sum(expo, axis=-1, keepdims=True)
                    probs = (expo / summed).astype(BF16)
                    att_ref[k, i, :, cols] = dot(probs, values[:, cols]).astype(BF16)
                    lse_ref[k, i, :, h : h + 1] = top + jnp.log(summed)
                part = dot_nt(att_ref[k, i], w[k, :, 3 * hc :])
                if k == 0:
                    out_ref[i] = part
                else:
                    out_ref[i] += part
            for copy in image_copies(i):
                copy.start()

            @pl.when(turn == imgs - 1)
            def _():
                out_copy().start()

            for j in range(early):

                @pl.when(turn == min(j, ni - 1))
                def _(j=j):
                    steps[j]()

            return carry

        lax.fori_loop(0, ni, image, 0)
        out_copy().wait()
        for i in range(imgs):
            hidden = x_ref[i].astype(F32) + (out_ref[i] + other[i]) + vec_ref[6:7, :]
            out_ref[i] = hidden
            normed, _ = norm(hidden)
            mlp_in[i] = (normed * vec_ref[1:2, :] + vec_ref[3:4, :]).astype(BF16)
        in_copy = remote(mlp_in.at[mine], mlp_in.at[theirs], (c_send, c_recv), 5, pair)
        in_copy.start()
        hidden_copy = pltpu.make_async_copy(out_ref.at[mine], hidden_out, out_sem.at[3])
        hidden_copy.start()
        take_rows(1, ct_ref, cot_ref)
        pair_rows(1, cot_ref).start()
        in_copy.wait()
        mlp_copy = pltpu.make_async_copy(mlp_in, mlp_out, out_sem.at[4])
        mlp_copy.start()
        finish(1, range(cfg.early))
        pair_rows(1, cot_ref).wait()
        cot_copy = pltpu.make_async_copy(cot_ref, cot_out, out_sem.at[2])
        cot_copy.start()
        kept.wait()
        x_copy.wait()
        hidden_copy.wait()
        mlp_copy.wait()
        for i in range(ni):
            for copy in image_copies(i):
                copy.wait()
        cot_copy.wait()

    vmem = pl.BlockSpec(memory_space=pltpu.VMEM)
    smem = pl.BlockSpec(memory_space=pltpu.SMEM)
    anywhere = pl.BlockSpec(memory_space=pl.ANY)
    dma = pltpu.SemaphoreType.DMA
    return pl.pallas_call(
        kernel,
        in_specs=[smem, vmem, vmem, vmem, anywhere],
        out_specs=[anywhere] * 8 + [vmem] * 2 + [anywhere] * 2,
        out_shape=[
            jax.ShapeDtypeStruct((ni, PT, D), BF16),
            jax.ShapeDtypeStruct((ni, PT, D), BF16),
            jax.ShapeDtypeStruct((ni, PT, D), BF16),
            jax.ShapeDtypeStruct((n_t, ni, PT, 3 * hc), BF16),
            jax.ShapeDtypeStruct((n_t, ni, PT, hc), BF16),
            jax.ShapeDtypeStruct((n_t, ni, PT, hh), F32),
            jax.ShapeDtypeStruct((imgs, PT, D), F32),
            jax.ShapeDtypeStruct((ni, PT, D), BF16),
            jax.ShapeDtypeStruct((8, D), F32),
            jax.ShapeDtypeStruct((n_t, f2), F32),
            jax.ShapeDtypeStruct((n_t, D, f2), BF16),
            jax.ShapeDtypeStruct((2, n_t, D, f2), BF16),
        ],
        scratch_shapes=[
            pltpu.VMEM((ni, PT, D), BF16),
            pltpu.VMEM((ni, PT, D), BF16),
            pltpu.VMEM((ni, PT, D), BF16),
            pltpu.VMEM((n_t, ni, PT, 3 * hc), BF16),
            pltpu.VMEM((n_t, ni, PT, hc), BF16),
            pltpu.VMEM((n_t, ni, PT, hh), F32),
            pltpu.VMEM((ni, PT, D), F32),
            pltpu.VMEM((imgs, PT, D), F32),
            pltpu.VMEM((ni, PT, D), BF16),
            pltpu.VMEM((n_t, D, f2), BF16),
            pltpu.VMEM((2, len(caps), widest, D), BF16),
            pltpu.VMEM((2, len(caps), widest, D), BF16),
            pltpu.VMEM((n_dev, 16, 128), F32),
            pltpu.VMEM((n_t, hc), F32),
            pltpu.VMEM((n_t, hc), F32),
            dma((2, n_t)),
            dma((2, n_t)),
            dma((2, n_t, n_p)),
            dma((2, n_t, n_p)),
            dma((2, len(caps))),
            dma((2, len(caps))),
            dma((6,)),
            dma((6,)),
            dma((n_t + n_p,)),
            dma((n_t + n_p,)),
            dma((2,)),
            dma((5,)),
            dma((4, ni)),
        ],
        compiler_params=params(collective_id=0, has_side_effects=True),
        cost_estimate=pl.CostEstimate(
            flops=2 * m * D * f2 * n_t,
            bytes_accessed=2 * n_t * D * f2 + 12 * m * D,
            transcendentals=m * PT * n_t * hh,
        ),
        name="gather_and_attend",
    )(counts, tokens, cotangent, small, halves)


def reduce_and_attend_back(
    counts, grad_hidden, attn_in, qkv, attended, lse, weights, mlp_grads, mlp_sums, residual, x, mixed, vectors, sums, fc1_sums, cfg
):
    n_t, n_p, ni, hc, hh, f2, pd, m, imgs = (
        cfg.n_t, cfg.n_p, cfg.ni, cfg.hc, cfg.hh, cfg.f2, cfg.pd, cfg.m, cfg.imgs,
    )
    scale = HD**-0.5
    square = n_p == 4
    plane = (2, 2) if square else (n_p,)
    order = list(range(n_t))[::-1]
    jobs = [((k, k), k) for k in order[:-1]] + [((k, k - 1), None) for k in order[::2]]
    n_jobs = len(jobs)
    n_got = 2 if square else n_p - 1
    n_dev = 2 * n_p * n_t
    width = D // n_dev
    caps = list(cfg.caps.items())
    widest = max(size for _, size in caps)
    to_z = {}
    for n, (chunks, _) in enumerate(jobs):
        for part in range(2):
            if chunks[part] > 0:
                to_z[n, part] = len(to_z)

    def kernel(
        counts_ref, gh_ref, in_ref, qkv_ref, att_ref, lse_ref, w_ref, g_ref, msum_ref, res_ref, x_ref, mix_ref, vec_ref,
        sums_ref, fsum_ref,
        half_0, half_1, half_2, mixed_ref, dtok_ref, small_ref, own_grads, in_other, got_z,
        gqkv, stage, held, got, got_2, got_step, total, out, dq, dv,
        images, sent, rows_got, x_in, block, res_in, other_in, parts, parts_p, parts_c, parts_t,
        stage_sem, held_sem, s_send, s_recv, t_send, t_recv, z_send, z_recv, r_send, r_recv, c_send, c_recv,
        v_send, v_recv, in_sem, out_sem, block_sem,
    ):
        p, core, z = (lax.axis_index(axis) for axis in ALL)
        py, px = p >> 1, p & 1
        pair = {"c": 1 - core}
        step = pl.program_id(0)
        layout = Layout(counts_ref, cfg)

        def pieces(n, part, *index):
            (chunks, k) = jobs[n]
            if k is None:
                return own_grads.at[(chunks[part], *index)]
            return g_ref.at[(*index, k, part)]

        def first_copies(n):
            if square:
                return [
                    remote(pieces(n, 0, slice(None), px ^ 1), got.at[n, 0], (s_send, s_recv), (n, 0, 0), {"p": p ^ 1}),
                    remote(pieces(n, 1, py ^ 1, slice(None)), got.at[n, 1], (s_send, s_recv), (n, 1, 0), {"p": p ^ 2}),
                ]
            return [
                remote(pieces(n, part, p ^ q), got.at[n, part, q - 1], (s_send, s_recv), (n, part, q - 1), {"p": p ^ q})
                for part in range(2)
                for q in range(1, n_p)
            ]

        def second_copies(n):
            if not square:
                return []
            return [
                remote(got.at[n, 0, py ^ 1], got_2.at[n, 0], (t_send, t_recv), (n, 0), {"p": p ^ 2}),
                remote(got.at[n, 1, px ^ 1], got_2.at[n, 1], (t_send, t_recv), (n, 1), {"p": p ^ 1}),
            ]

        def z_copy(n, part):
            k = jobs[n][0][part]
            source = got.at[n, part, (py, px)[part] if square else 0]
            target = {"t": lax.rem(z - k + n_t, n_t)}
            index = to_z[n, part]
            if jobs[n][1] is not None:
                target = {"t": lax.rem(z - 1 + n_t, n_t)}
                return remote(source, got_step.at[index], (z_send, z_recv), index, target)
            return remote(source, got_z.at[index], (z_send, z_recv), index, target)

        def loads(n):
            if square:
                sources = [pieces(n, 0, slice(None), px), pieces(n, 1, py, slice(None))]
            else:
                sources = [pieces(n, 0, p), pieces(n, 1, p)]
            return [
                pltpu.make_async_copy(
                    source, held.at[n % 2, part] if square else held.at[n % 2, part, 0], held_sem.at[n % 2, part]
                )
                for part, source in enumerate(sources)
            ]

        def begin(n):
            for copy in first_copies(n):
                copy.start()

        def fetch(n):
            for copy in loads(n):
                copy.start()

        def middle(n):
            for copy in loads(n):
                copy.wait()
            for copy in first_copies(n):
                copy.wait_recv()
            if square:
                for part, here in enumerate((py, px)):
                    there = here ^ 1
                    both = held[n % 2, part, there].astype(F32) + got[n, part, there].astype(F32)
                    got[n, part, there] = both.astype(BF16)
                for copy in second_copies(n):
                    copy.start()

        def last(n):
            for copy in second_copies(n):
                copy.wait_recv()
            chunks, k = jobs[n]
            for part, here in enumerate((py, px)):
                if square:
                    whole = held[n % 2, part, here].astype(F32) + got[n, part, here].astype(F32)
                    whole = whole + got_2[n, part].astype(F32)
                else:
                    whole = held[n % 2, part, 0].astype(F32)
                    for q in range(n_p - 1):
                        whole = whole + got[n, part, q].astype(F32)
                if k is not None and k < n_t - 1:
                    z_copy(n - 1, part).wait_recv()
                    whole = whole + got_step[to_z[n - 1, part]].astype(F32)
                if chunks[part] == 0:
                    total[0] = whole
                else:
                    got[n, part, here if square else 0] = whole.astype(BF16)
                    z_copy(n, part).start()

        def tick(n):
            middle(n)
            if n > 0:
                last(n - 1)
                if n + 1 < n_jobs:
                    fetch(n + 1)
            if n + 2 < n_jobs:
                begin(n + 2)

        def sums_copy():
            return pltpu.make_async_copy(msum_ref, total.at[pl.ds(1, 2)], stage_sem.at[1])

        def finish():
            for s, (shift, _) in enumerate(caps):

                @pl.when(layout.has(z - shift))
                def _(s=s):
                    row_copy(1, s).wait_send()

            for n in range(n_jobs):
                for copy in first_copies(n) + second_copies(n):
                    copy.wait_send()
                for part in range(2):
                    if (n, part) in to_z:
                        z_copy(n, part).wait_send()
                        if jobs[n][1] is None:
                            z_copy(n, part).wait_recv()
            direct = [(n, part) for n, part in to_z if jobs[n][1] is None]
            reads = [
                pltpu.make_async_copy(got_z.at[to_z[spot]], got.at[(*spot, 0)], z_recv.at[to_z[spot]])
                for spot in direct
            ]
            for read in reads:
                read.start()
            for read in reads:
                read.wait()
            whole = total[0]
            for spot in direct:
                whole = whole + got[(*spot, 0)].astype(F32)
            total[0] = whole
            sums_copy().wait()
            for part in range(2):
                z_copy(n_t - 2, part).wait_recv()
                total[1 + part] += got_step[to_z[n_t - 2, part]].astype(F32)

            def rows(unit, member):
                return total.at[unit, pl.ds(pl.multiple_of(member * pd, 16), pd), :]

            moves = []
            for unit, half_ref in enumerate((half_0, half_1, half_2)):
                moves.append(pltpu.make_async_copy(rows(unit, core), half_ref.at[core], out_sem.at[unit]))
                target = half_ref.at[core]
                moves.append(remote(rows(unit, 1 - core), target, (c_send, c_recv), 1 + unit, pair))
            for move in moves:
                move.start()
            for move in moves:
                move.wait()
            block_store(1).wait()

        def row_copy(which, s):
            shift, size = caps[s]
            return remote(
                sent.at[s, pl.ds(0, size)], rows_got.at[which, s, pl.ds(0, size)], (r_send, r_recv), (which, s),
                {"t": jnp.clip(z - shift, 0, n_t - 1)},
            )

        def of_images(positions, valid):
            rows = None
            for i in range(imgs):
                spots = positions - i * TOK_IMG
                spots = jnp.where(valid & (spots >= 0) & (spots < TOK_IMG), spots, -1)
                picked = dot(one_hot(spots, PT), images[i])
                rows = picked if rows is None else rows + picked
            return rows.astype(BF16)

        def send_rows(which):
            for s, (shift, size) in enumerate(caps):

                @pl.when(layout.has(z - shift))
                def _(s=s, shift=shift, size=size):
                    if which == 1:
                        row_copy(0, s).wait_send()
                    want = layout.window_back(z, z - shift, size) + row_ids(size)
                    sent[s, :size] = of_images(want, want >= 0)
                    row_copy(which, s).start()

        def block_store(which):
            return pltpu.make_async_copy(block, (mixed_ref, dtok_ref)[which], block_sem)

        def take_rows(which):
            if which == 1:
                block_store(0).wait()
            row = row_ids(-(-cfg.block // 16) * 16)
            position = layout.start(z) + row
            valid = position < layout.end(z)
            block[...] = of_images(position - cfg.rows * z, valid)[: cfg.block]
            for s, (shift, size) in enumerate(caps):
                source = z + shift

                @pl.when(layout.has(source))
                def _(s=s, size=size, source=source):
                    row_copy(which, s).wait_recv()
                    local = position - cfg.rows * source
                    mine = valid & (local >= 0) & (local < cfg.rows)
                    spots = jnp.where(mine, local - layout.window_back(source, z, size), -1)
                    block[...] += dot(one_hot(spots, size), rows_got[which, s, :size]).astype(BF16)[: cfg.block]

            block_store(which).start()

        device = (2 * p + core) * n_t + z

        def gather_parts(gain, shift):
            parts[...] = jnp.zeros_like(parts)
            rows = [gain, sums_ref[0:1, :], shift, sums_ref[1:2, :], sums_ref[2:3, :], sums_ref[3:4, :]]
            for d in range(n_dev):
                cols = slice(d * width, (d + 1) * width)
                for r, value in zip((0, 1, 2, 3, 6, 7), rows):
                    parts[d, r : r + 1, :width] = value[:, cols]
            for k in range(n_t):
                chunk = 2 * lax.rem(z - k + n_t, n_t) + core
                for j in range(hc // width):
                    cols = slice(j * width, (j + 1) * width)
                    owner = chunk * (hc // width) + j
                    parts[owner, 4:5, :width] = dq[k : k + 1, cols]
                    parts[owner, 5:6, :width] = dv[k : k + 1, cols]
                for j in range(f2 // (4 * width)):
                    owner = chunk * (f2 // (4 * width)) + j
                    for r in range(4):
                        begin_at = (4 * j + r) * width
                        parts[owner, 8 + r : 9 + r, :width] = fsum_ref[k, :, begin_at : begin_at + width]

        def plane_parts(index):
            return pl.ds(2 * index * n_t, 2 * n_t)

        def core_parts(member):
            return pl.ds((2 * p + member) * n_t, n_t)

        def part_copies(hop):
            if hop == 0:
                return [
                    remote(parts.at[plane_parts(p ^ q)], parts_p.at[q - 1], (v_send, v_recv), q - 1, {"p": p ^ q})
                    for q in range(1, n_p)
                ]
            if hop == 1:
                return [remote(parts.at[core_parts(1 - core)], parts_c, (v_send, v_recv), n_p - 1, pair)]
            copies = []
            for k in range(1, n_t):
                to = lax.rem(z + k, n_t)
                source = parts.at[(2 * p + core) * n_t + to]
                copies.append(remote(source, parts_t.at[k], (v_send, v_recv), n_p - 1 + k, {"t": to}))
            return copies

        def part_hop(hop):
            if hop > 0:
                for copy in part_copies(hop - 1):
                    copy.wait()
            if hop == 1:
                for q in range(n_p - 1):
                    parts[plane_parts(p)] += parts_p[q]
            if hop == 2:
                parts[core_parts(core)] += parts_c[...]
            if hop == 3:
                mine = parts[device]
                for k in range(1, n_t):
                    mine = mine + parts_t[k]
                small_ref[...] = mine
            if hop < 3:
                for copy in part_copies(hop):
                    copy.start()

        def in_copy():
            return remote(out.at[pl.ds(imgs, imgs)], in_other, (c_send, c_recv), 0, pair)

        def first_norm_back():
            in_copy().wait()
            gain, shift = jnp.zeros((1, D), F32), jnp.zeros((1, D), F32)
            half = PT // 2
            for i in range(imgs):
                for begin_at in (0, half):
                    some = pl.ds(begin_at, half)
                    reads = [
                        pltpu.make_async_copy(res_ref.at[i, some], res_in, in_sem.at[0]),
                        pltpu.make_async_copy(in_other.at[i, some], other_in, in_sem.at[1]),
                        pltpu.make_async_copy(x_ref.at[i, some], x_in, in_sem.at[2]),
                    ]
                    for read in reads:
                        read.start()
                    for read in reads:
                        read.wait()
                    up = out[i, begin_at : begin_at + half] + other_in[...]
                    normed, inverse = norm(x_in[...].astype(F32))
                    grad = res_in[...] + norm_back(up, normed, inverse, vec_ref[0:1, :])
                    images[i, begin_at : begin_at + half] = grad.astype(BF16)
                    gain = gain + jnp.sum(up * normed, axis=0, keepdims=True)
                    shift = shift + jnp.sum(up, axis=0, keepdims=True)
            gather_parts(gain, shift)

        @pl.when(step == 0)
        def _():
            sums_copy().start()
            fetch(0)
            fetch(1)
            read = pltpu.make_async_copy(mix_ref, images, in_sem.at[0])
            read.start()
            enter(cfg)
            begin(0)
            begin(1)
            read.wait()
            send_rows(0)

        keyed = lax.broadcasted_iota(jnp.int32, (PT, PT), 1) < TOK_IMG

        def image(i, carry):
            total_q, total_v = carry
            grad_att = dot(gh_ref[i], w_ref[0, :, 3 * hc :]).astype(BF16)
            sums_q, sums_v = [], []
            for h in range(hh):
                cols = slice(h * HD, (h + 1) * HD)
                key_cols = slice(hc + h * HD, hc + (h + 1) * HD)
                value_cols = slice(2 * hc + h * HD, 2 * hc + (h + 1) * HD)
                query = qkv_ref[0, i, :, cols]
                keys = qkv_ref[0, i, :, key_cols]
                values = qkv_ref[0, i, :, value_cols]
                grad = grad_att[:, cols]
                scores = dot_nt(query, keys) * scale - lse_ref[0, i, :, h : h + 1]
                probs = jnp.exp(jnp.where(keyed, scores, NEG))
                delta = jnp.sum(
                    grad.astype(F32) * att_ref[0, i, :, cols].astype(F32), axis=-1, keepdims=True
                )
                grad_v = dot_tn(probs.astype(BF16), grad)
                grad_s = (probs * (dot_nt(grad, values) - delta) * scale).astype(BF16)
                grad_q = dot(grad_s, keys)
                grad_k = dot_tn(grad_s, query)
                sums_q.append(jnp.sum(grad_q, axis=0, keepdims=True))
                sums_v.append(jnp.sum(grad_v, axis=0, keepdims=True))
                gqkv[i, :, cols] = grad_q.astype(BF16)
                gqkv[i, :, key_cols] = grad_k.astype(BF16)
                gqkv[i, :, value_cols] = grad_v.astype(BF16)
            total_q = total_q + jnp.concatenate(sums_q, axis=1)
            total_v = total_v + jnp.concatenate(sums_v, axis=1)
            part = dot_nt(gqkv[i], w_ref[0, :, : 3 * hc])

            @pl.when(step == 0)
            def _():
                out[i] = part

            @pl.when(step > 0)
            def _():
                out[i] += part

            for n in range(n_t - 2):

                @pl.when((step == n + 1) & (i == min(2 * n + 1, ni - 1)))
                def _(n=n):
                    tick(n)

            return total_q, total_v

        nothing = jnp.zeros((1, hc), F32)
        total_q, total_v = lax.fori_loop(0, ni, image, (nothing, nothing))
        dq[pl.ds(n_t - 1 - step, 1), :] = total_q
        dv[pl.ds(n_t - 1 - step, 1), :] = total_v

        @pl.when(step == n_t - 1)
        def _():
            in_copy().start()

        for side in range(2):
            cols = slice(side * D // 2, (side + 1) * D // 2)
            ahead = (side,) if square else (slice(side * n_p // 2, (side + 1) * n_p // 2),)
            ahead = ahead + (slice(None),) * len(plane)
            for lhs, rhs, lanes in (
                (in_ref, gqkv[...].reshape(m, 3 * hc), slice(0, 3 * hc)),
                (gh_ref, att_ref[0].reshape(m, hc), slice(3 * hc, f2)),
            ):
                value = dot_tn(lhs[:, :, cols].reshape(m, D // 2), rhs).astype(BF16)
                stage[(*ahead, lanes)] = value.reshape(
                    (n_p // 2, 2 * pd, lanes.stop - lanes.start)
                )
        store = pltpu.make_async_copy(stage, own_grads.at[n_t - 1 - step], stage_sem.at[0])
        store.start()
        store.wait()

        @pl.when(step == n_t - 2)
        def _():
            take_rows(0)

        @pl.when(step == n_t - 1)
        def _():
            tick(n_t - 2)
            first_norm_back()
            send_rows(1)
            part_hop(0)
            tick(n_t - 1)
            part_hop(1)
            for n in range(n_t, n_jobs - 1):
                tick(n)
            part_hop(2)
            tick(n_jobs - 1)
            last(n_jobs - 1)
            take_rows(1)
            part_hop(3)
            finish()

    dma = pltpu.SemaphoreType.DMA
    chunk = (2 * pd, f2)
    vmem = pltpu.VMEM

    def chunk_block(last):
        return pl.BlockSpec((1, ni, PT, last), lambda k: (n_t - 1 - k, 0, 0, 0))

    anywhere = pl.BlockSpec(memory_space=pl.ANY)
    shape = jax.ShapeDtypeStruct
    n_v = n_p - 1 + n_t
    outs = pl.pallas_call(
        kernel,
        grid=(n_t,),
        in_specs=[
            pl.BlockSpec(memory_space=pltpu.SMEM),
            fixed((ni, PT, D)),
            fixed((ni, PT, D)),
            chunk_block(3 * hc),
            chunk_block(hc),
            chunk_block(hh),
            pl.BlockSpec((1, D, f2), lambda k: (n_t - 1 - k, 0, 0)),
            anywhere,
            anywhere,
            anywhere,
            anywhere,
            anywhere,
            fixed((8, D)),
            fixed((4, D)),
            fixed((n_t, 1, f2)),
        ],
        out_specs=[anywhere] * 5 + [fixed((16, 128))] + [anywhere] * 3,
        out_shape=[
            shape((2, pd, f2), F32),
            shape((2, pd, f2), F32),
            shape((2, pd, f2), F32),
            shape((cfg.block, D), BF16),
            shape((cfg.block, D), BF16),
            shape((16, 128), F32),
            shape((n_t, *plane, *chunk), BF16),
            shape((imgs, PT, D), F32),
            shape((len(to_z), *chunk), BF16),
        ],
        scratch_shapes=[
            vmem((ni, PT, 3 * hc), BF16),
            vmem((*plane, *chunk), BF16),
            vmem((2, 2, 2 if square else 1, *chunk), BF16),
            vmem((n_jobs, 2, n_got, *chunk), BF16),
            vmem((n_jobs, 2, *(chunk if square else (16, 128))), BF16),
            vmem((2 * (n_t - 1), *chunk), BF16),
            vmem((3, *chunk), F32),
            vmem((ni, PT, D), F32),
            vmem((n_t, hc), F32),
            vmem((n_t, hc), F32),
            vmem((imgs, PT, D), BF16),
            vmem((len(caps), widest, D), BF16),
            vmem((2, len(caps), widest, D), BF16),
            vmem((PT // 2, D), BF16),
            vmem((cfg.block, D), BF16),
            vmem((PT // 2, D), F32),
            vmem((PT // 2, D), F32),
            vmem((n_dev, 16, 128), F32),
            vmem((n_p - 1, 2 * n_t, 16, 128), F32),
            vmem((n_t, 16, 128), F32),
            vmem((n_t, 16, 128), F32),
            dma((2,)),
            dma((2, 2)),
            dma((n_jobs, 2, 1 if square else n_p - 1)),
            dma((n_jobs, 2, 1 if square else n_p - 1)),
            dma((n_jobs, 2)),
            dma((n_jobs, 2)),
            dma((len(to_z),)),
            dma((len(to_z),)),
            dma((2, len(caps))),
            dma((2, len(caps))),
            dma((4,)),
            dma((4,)),
            dma((n_v,)),
            dma((n_v,)),
            dma((3,)),
            dma((3,)),
            dma,
        ],
        compiler_params=params(collective_id=1, has_side_effects=True),
        cost_estimate=pl.CostEstimate(
            flops=4 * m * D * f2 * n_t + 10 * m * PT * HD * n_t * hh,
            bytes_accessed=4 * n_t * D * f2 + 20 * m * D,
            transcendentals=m * PT * n_t * hh,
        ),
        name="reduce_and_attend_back",
    )(
        counts,
        grad_hidden,
        attn_in,
        qkv,
        attended,
        lse,
        weights,
        mlp_grads,
        mlp_sums,
        residual,
        x,
        mixed,
        vectors,
        sums,
        fc1_sums,
    )
    return outs[:6]


def mlp_pass(hidden, mlp_in, vectors, cot, fc1, weights, cfg):
    n_p, n_t, m, pd, w, ni, imgs = cfg.n_p, cfg.n_t, cfg.m, cfg.pd, cfg.f2, cfg.ni, cfg.imgs
    early = cfg.early
    square = n_p == 4
    plane = (2, 2) if square else (n_p,)
    piece = (2 * pd, w)

    def kernel(
        hidden_ref, mlp_in, vec_ref, cot_ref, fc1_ref, g_ref,
        sum_ref, grad_ref, plane_ref, res_ref, gh_ref, sums_ref, mixed_ref, late_ref,
        other, other_y, act_all, gpre_all, back, y, gh, w_all, stage, held, got, got_2,
        c_send, c_recv, own_sem, load_sem, keep_sem, z_send, z_recv, p_send, p_recv,
        stage_sem, s_send, s_recv, t_send, t_recv,
    ):
        step = pl.program_id(0)
        p, z = lax.axis_index("p"), lax.axis_index("t")
        pair = {"c": 1 - lax.axis_index("c")}

        def rows(mask):
            return pl.ds(pl.multiple_of((p ^ mask) * 2 * pd, 16), 2 * pd)

        def own_rows(j):
            return g_ref.at[:, early, rows(0), :] if j == 0 else late_ref.at[:, j, rows(0), :]

        def keep():
            return pltpu.make_async_copy(own_rows(0), late_ref.at[:, 0, rows(0), :], keep_sem)

        def z_copy(j):
            target = {"t": lax.rem(z + 1, n_t)}
            return remote(own_rows(j - 1), own_rows(j), (z_send, z_recv), j, target)

        def p_copy(j, mask):
            target = late_ref.at[:, j, rows(0), :]
            return remote(own_rows(j), target, (p_send, p_recv), (j, mask), {"p": p ^ mask})

        def d_copies(j):
            if n_p != 4:
                return []
            ref_1, ref_2 = late_ref.at[0, j, rows(1), :], late_ref.at[1, j, rows(2), :]
            return [
                remote(ref_1, ref_1, (p_send, p_recv), (j, 3), {"p": p ^ 2}),
                remote(ref_2, ref_2, (p_send, p_recv), (j, 0), {"p": p ^ 1}),
            ]

        direct = (1, 2) if n_p == 4 else tuple(range(1, n_p))

        def send_p(j):
            if j > 0:
                z_copy(j).wait_recv()
            if early + j + 1 < n_t:
                z_copy(j + 1).start()
            for mask in direct:
                p_copy(j, mask).start()

        def send_d(j):
            for mask in direct:
                p_copy(j, mask).wait_recv()
            for copy in d_copies(j):
                copy.start()
            if early + j + 1 < n_t:
                send_p(j + 1)

        def complete(j):
            if j == 0:
                keep().wait()
            for copy in d_copies(j):
                copy.wait_recv()

        def load(k):
            source = g_ref.at[:, k] if k < early else late_ref.at[:, k - early]
            return pltpu.make_async_copy(source, w_all.at[k % 2], load_sem.at[k % 2])
        mine, theirs = pl.ds(0, imgs), pl.ds(imgs, imgs)

        def pair_copy(index, source, target):
            return remote(source, target, (c_send, c_recv), index, pair)

        def back_copy():
            return pair_copy(0, back.at[theirs], other)

        def y_copy():
            return pair_copy(1, y.at[theirs], other_y)

        py, px = p >> 1, p & 1

        def first_copies():
            if square:
                return [
                    remote(grad_ref.at[:, px ^ 1, 0, 0], got.at[0], (s_send, s_recv), (0, 0), {"p": p ^ 1}),
                    remote(grad_ref.at[py ^ 1, :, 0, 1], got.at[1], (s_send, s_recv), (1, 0), {"p": p ^ 2}),
                ]
            return [
                remote(grad_ref.at[p ^ q, 0, part], got.at[part, q - 1], (s_send, s_recv), (part, q - 1), {"p": p ^ q})
                for part in range(2)
                for q in range(1, n_p)
            ]

        def second_copies():
            if not square:
                return []
            return [
                remote(got.at[0, py ^ 1], got_2.at[0], (t_send, t_recv), 0, {"p": p ^ 2}),
                remote(got.at[1, px ^ 1], got_2.at[1], (t_send, t_recv), 1, {"p": p ^ 1}),
            ]

        def middle():
            for copy in first_copies():
                copy.wait_recv()
            if square:
                for part, here in enumerate((py, px)):
                    both = held[part, here ^ 1].astype(F32) + got[part, here ^ 1].astype(F32)
                    got[part, here ^ 1] = both.astype(BF16)
                for copy in second_copies():
                    copy.start()

        def last():
            for copy in second_copies():
                copy.wait_recv()
            for part, here in enumerate((py, px)):
                if square:
                    whole = held[part, here].astype(F32) + got[part, here].astype(F32)
                    whole = whole + got_2[part].astype(F32)
                else:
                    whole = held[part, 0].astype(F32)
                    for q in range(n_p - 1):
                        whole = whole + got[part, q].astype(F32)
                plane_ref[part] = whole
            for copy in first_copies() + second_copies():
                copy.wait_send()

        def stage_copy(k):
            ahead = (slice(None),) * len(plane)
            return pltpu.make_async_copy(stage, grad_ref.at[(*ahead, k)], stage_sem)

        @pl.when(step == 0)
        def _():
            pltpu.make_async_copy(hidden_ref, res_ref, own_sem).start()
            keep().start()
            for k in range(min(2, early)):
                load(k).start()
            enter(cfg)
            send_p(0)
        slot = lax.rem(step, 2)
        for k in range(n_t):

            @pl.when(step == k)
            def _(k=k):
                load(k).wait()

        w1, w2 = w_all[slot, 0], w_all[slot, 1]
        total = jnp.zeros((1, w), F32)
        for i in range(ni):
            rows_i = slice(i * PT, (i + 1) * PT)
            pre = dot(mlp_in[i], w1) + fc1_ref[0]
            phi = 0.5 * (1.0 + lax.erf(pre * (1.0 / math.sqrt(2.0))))
            act_all[rows_i, :] = (pre * phi).astype(BF16)
            slope = phi + pre * jnp.exp(-0.5 * pre * pre) * (1.0 / math.sqrt(2.0 * math.pi))
            gpre = dot(cot_ref[i], w2) * slope
            total = total + jnp.sum(gpre, axis=0, keepdims=True)
            gpre_all[rows_i, :] = gpre.astype(BF16)
        sum_ref[0] = total

        def add(target, left, right):
            value = dot_nt(left, right).reshape(ni, PT, D)

            @pl.when(step == 0)
            def _():
                target[...] = value

            @pl.when(step > 0)
            def _():
                target[...] += value

        add(back, gpre_all[...], w1)

        for j in range(1, n_t - early):

            @pl.when(step == early - 1 + j)
            def _(j=j):
                send_d(j)

        @pl.when(step == n_t - 2)
        def _():
            for copy in first_copies():
                copy.start()

        @pl.when(step == n_t - 1)
        def _():
            back_copy().start()

        add(y, act_all[...], w2)

        @pl.when(step == n_t - 1)
        def _():
            y_copy().start()

        @pl.when(step > 0)
        def _():
            stage_copy(0).wait()

        ahead = (slice(None),) * len(plane)
        grad_1 = dot_tn(mlp_in[...].reshape(m, D), gpre_all[...]).astype(BF16)
        stage[(*ahead, 0)] = grad_1.reshape((*plane, *piece))
        grad_2 = dot_tn(cot_ref[...].reshape(m, D), act_all[...]).astype(BF16)
        stage[(*ahead, 1)] = grad_2.reshape((*plane, *piece))
        stage_copy(step).start()

        @pl.when(step == 0)
        def _():
            if square:
                held[0] = stage[:, px, 0]
                held[1] = stage[py, :, 1]
            else:
                held[0, 0] = stage[p, 0]
                held[1, 0] = stage[p, 1]

        @pl.when(step == n_t - 1)
        def _():
            middle()

        @pl.when(step == early - 2)
        def _():
            send_d(0)

        for k in range(2, n_t):

            @pl.when(step == k - 1)
            def _(k=k):
                if k >= early:
                    complete(k - early)
                load(k).start()

        @pl.when(step == n_t - 1)
        def _():
            pltpu.make_async_copy(hidden_ref, res_ref, own_sem).wait()
            back_copy().wait()
            sums = [jnp.zeros((1, D), F32)] * 4
            for i in range(imgs):
                up = back[i] + other[i]
                hidden = res_ref[i]
                other[i] = hidden
                normed, inverse = norm(hidden)
                cot_f = cot_ref[i].astype(F32)
                grad = cot_f + norm_back(up, normed, inverse, vec_ref[1:2, :])
                res_ref[i] = grad
                gh[i] = grad.astype(BF16)
                terms = (up * normed, up, grad, cot_f)
                sums = [s + jnp.sum(t, axis=0, keepdims=True) for s, t in zip(sums, terms)]
            grad_copy = pair_copy(2, gh.at[mine], gh.at[theirs])
            grad_copy.start()
            for r in range(4):
                sums_ref[r : r + 1, :] = sums[r]
            y_copy().wait()
            for i in range(imgs):
                mixed_ref[i] = (other[i] + (y[i] + other_y[i]) + vec_ref[7:8, :]).astype(BF16)
            grad_copy.wait()
            store = pltpu.make_async_copy(gh, gh_ref, own_sem)
            store.start()
            last()
            stage_copy(0).wait()
            for j in range(n_t - early):
                for copy in d_copies(j):
                    copy.wait_send()
                for mask in direct:
                    p_copy(j, mask).wait_send()
                if j > 0:
                    z_copy(j).wait_send()
            store.wait()

    full = fixed((ni, PT, D))
    own = fixed((imgs, PT, D))
    shape, vmem, dma = jax.ShapeDtypeStruct, pltpu.VMEM, pltpu.SemaphoreType.DMA
    return pl.pallas_call(
        kernel,
        grid=(n_t,),
        in_specs=[
            pl.BlockSpec(memory_space=pl.ANY),
            full,
            fixed((8, D)),
            full,
            pl.BlockSpec((1, 1, w), lambda i: (i, 0, 0)),
            pl.BlockSpec(memory_space=pl.ANY),
        ],
        out_specs=[
            pl.BlockSpec((1, 1, w), lambda i: (i, 0, 0)),
            pl.BlockSpec(memory_space=pl.ANY),
            fixed((2, *piece)),
            own,
            pl.BlockSpec(memory_space=pl.ANY),
            fixed((4, D)),
            own,
            pl.BlockSpec(memory_space=pl.ANY),
        ],
        out_shape=[
            shape((n_t, 1, w), F32),
            shape((*plane, n_t, 2, *piece), BF16),
            shape((2, *piece), F32),
            shape((imgs, PT, D), F32),
            shape((ni, PT, D), BF16),
            shape((4, D), F32),
            shape((imgs, PT, D), BF16),
            shape((2, n_t - early, D, w), BF16),
        ],
        scratch_shapes=[
            vmem((imgs, PT, D), F32),
            vmem((imgs, PT, D), F32),
            vmem((m, w), BF16),
            vmem((m, w), BF16),
            vmem((ni, PT, D), F32),
            vmem((ni, PT, D), F32),
            vmem((ni, PT, D), BF16),
            vmem((2, 2, D, w), BF16),
            vmem((*plane, 2, *piece), BF16),
            vmem((2, 2 if square else 1, *piece), BF16),
            vmem((2, 2 if square else n_p - 1, *piece), BF16),
            vmem((2, *(piece if square else (16, 128))), BF16),
            dma((3,)),
            dma((3,)),
            dma,
            dma((2,)),
            dma,
            dma((n_t - early,)),
            dma((n_t - early,)),
            dma((n_t - early, n_p)),
            dma((n_t - early, n_p)),
            dma,
            dma((2, 1 if square else n_p - 1)),
            dma((2, 1 if square else n_p - 1)),
            dma((2,)),
            dma((2,)),
        ],
        compiler_params=params(collective_id=2, has_side_effects=True),
        cost_estimate=pl.CostEstimate(
            flops=12 * m * D * w * n_t,
            bytes_accessed=12 * m * D + 8 * D * w * n_t,
            transcendentals=2 * m * w * n_t,
        ),
        name="mlp_pass",
    )(hidden, mlp_in, vectors, cot, fc1.reshape(n_t, 1, w), weights)[:-1]


def body(cfg, tokens, counts, gains, biases, fc1_bias, w_qkv, w_o, w_1, w_2, cotangent):
    pd, f2, hc = cfg.pd, cfg.f2, cfg.hc
    halves = jnp.stack(
        [
            jnp.concatenate(
                [
                    w_qkv.reshape(pd, 3, 2, hc).transpose(2, 0, 1, 3).reshape(2, pd, 3 * hc),
                    w_o.T.reshape(pd, 2, hc).transpose(1, 0, 2),
                ],
                axis=2,
            ),
            w_1.reshape(pd, 2, f2).transpose(1, 0, 2),
            w_2.T.reshape(pd, 2, f2).transpose(1, 0, 2),
        ],
        axis=1,
    )
    small = jnp.concatenate([gains, biases, fc1_bias.reshape(4, -1)])
    small = jnp.pad(small, ((0, 4), (0, 128 - small.shape[1])))

    x, cot, attn_in, qkv, attended, lse, hidden, mlp_in, vectors, fc1, attn_w, mlp_w = gather_and_attend(
        counts, tokens, cotangent, small, halves, cfg
    )
    fc1_sums, mlp_grads, mlp_sums, residual, grad_hidden, sums, mixed = mlp_pass(
        hidden, mlp_in, vectors, cot, fc1, mlp_w, cfg
    )
    attn, first, second, mixed, d_tokens, small = reduce_and_attend_back(
        counts, grad_hidden, attn_in, qkv, attended, lse, attn_w, mlp_grads, mlp_sums, residual, x, mixed,
        vectors, sums, fc1_sums, cfg,
    )
    d_qkv = attn[:, :, : 3 * hc].reshape(2, pd, 3, hc).transpose(1, 2, 0, 3).reshape(pd, 3, 2 * hc)
    d_o = attn[:, :, 3 * hc :].transpose(0, 2, 1).reshape(2 * hc, pd)
    d_1 = first.transpose(1, 0, 2).reshape(pd, 2 * f2)
    d_2 = second.transpose(0, 2, 1).reshape(2 * f2, pd)
    piece = D // (cfg.n_dp * cfg.n_t)
    small = small[:, :piece]
    return (
        mixed,
        d_tokens,
        d_qkv,
        d_o,
        d_1,
        d_2,
        small[:2],
        small[2:8],
        small[8:12].reshape(-1),
    )


def solution(mesh):
    n_dp, n_t = mesh.shape["dp"], mesh.shape["tensor"]
    split = Mesh(mesh.devices.reshape(n_dp // 2, 2, n_t), ALL)

    def program(tokens, *rest):
        cfg = Cfg(n_dp, n_t, tokens.shape[0])
        return body(cfg, tokens, *rest)

    dp = ("p", "c")
    return jax.shard_map(
        program,
        mesh=split,
        in_specs=(
            P(ALL, None),
            P(dp, None),
            P(None, ALL),
            P(None, ALL),
            P(ALL),
            P(dp, None, "t"),
            P("t", dp),
            P(dp, "t"),
            P("t", dp),
            P(ALL, None),
        ),
        out_specs=(
            P(ALL, None),
            P(ALL, None),
            P(dp, None, "t"),
            P("t", dp),
            P(dp, "t"),
            P("t", dp),
            P(None, ALL),
            P(None, ALL),
            P(ALL),
        ),
        check_vma=False,
    )
```
